32 devices in a mesh: seq: 16 (over z, y, x), head: 2 (over core).
Axes of the slice: x: 2, y: 2, z: 4, core: 2. Of those that a mesh axis runs over, the one named last changes fastest.
Arguments:
- attn_q: bfloat16 [2048, 512], P('seq', 'head'), may hold values from -6 to 6
- attn_k: bfloat16 [2048, 512], P('seq', 'head'), may hold values from -6 to 6
- attn_v: bfloat16 [2048, 512], P('seq', 'head'), may hold values from -6 to 6
- attn_out: bfloat16 [2048, 512], P('seq', 'head'), may hold values from -0.29882812 to 0.29882812
- attn_dout: bfloat16 [2048, 512], P('seq', 'head'), may hold values from -96 to 96
- attn_lse: float32 [4, 2048], P('head', 'seq'), may hold values from 7 to 8
- w_kv: bfloat16 [512, 2, 512], P('seq', None, 'head'), may hold values from -0.25 to 0.25
- gdn_q: bfloat16 [2048, 512], P('seq', 'head'), may hold values from -6 to 6
- gdn_k: bfloat16 [2048, 512], P('seq', 'head'), may hold values from -6 to 6
- gdn_v: bfloat16 [2048, 512], P('seq', 'head'), may hold values from -6 to 6
- gdn_dout: bfloat16 [2048, 512], P('seq', 'head'), may hold values from -6 to 6
- gdn_log_decay: float32 [4, 2048], P('head', 'seq'), may hold values from -0.56 to 0
- gdn_beta: float32 [4, 2048], P('head', 'seq'), may hold values from 0 to 0.9
- gdn_states: float32 [32, 4, 128, 128], P('seq', 'head'), may hold values from -24 to 24
Outputs:
- attn_dq: bfloat16 [2048, 512], P('seq', 'head')
- attn_dx: bfloat16 [512, 2048], P('head', 'seq')
- gdn_dq: bfloat16 [2048, 512], P('seq', 'head')
- gdn_dk: bfloat16 [2048, 512], P('seq', 'head')
- gdn_dv: bfloat16 [2048, 512], P('seq', 'head')
- gdn_dlog_decay: float32 [4, 2048], P('head', 'seq')
- gdn_dbeta: float32 [4, 2048], P('head', 'seq')
The draws below stay inside these ranges and needn't reach their ends.
All inputs are finite; a program needn't handle non-finite values.
Results may differ from the reference program's by a relative error of at most 0.0078.
Values may be sent and summed in bfloat16 or wider, within the bound.
A program may use at most 64 MiB of HBM per device.

```python
import math
import jax
import jax.numpy as jnp
from jax import lax

TOK_DEV = 128
HEAD_DIM = 128
BLOCK = 64
WINDOW = 1024
HEADS = 4
WIDTH = 512
TOKENS = 2048
BLOCKS = 32


def head_speed(key):
    share = 0.5
    return jax.random.uniform(jax.random.fold_in(key, 11), (HEADS,)) < share


def draw_gdn_log_decay(key, part):
    lasting = head_speed(key)
    branch = jax.random.fold_in(key, 23)
    key_jitter, key_places, key_losses = jax.random.split(branch, 3)
    speeds = jnp.where(lasting, 0.5 / TOKENS, 1.0 / 48.0)
    jitter = jnp.exp(jax.random.uniform(key_jitter, (HEADS, TOKENS), minval=math.log(0.5), maxval=math.log(2.0)))
    places = jax.random.randint(key_places, (3,), 0, TOKENS)
    positions = jnp.arange(TOKENS)
    struck = jnp.any(positions[:, None] == places[None, :], axis=1)
    losses = jax.random.uniform(key_losses, (HEADS, TOKENS), minval=math.log(0.6), maxval=math.log(0.8))
    return -speeds[:, None] * jitter + jnp.where(struck[None, :], losses, 0.0)


def draw_gdn_beta(key, part):
    lasting = head_speed(key)
    branch = jax.random.fold_in(key, 37)
    key_slow, key_fast = jax.random.split(branch, 2)
    slow_values = jax.random.uniform(key_slow, (HEADS, TOKENS), minval=0.1, maxval=0.3) * (HEAD_DIM / TOKENS)
    fast_values = jax.random.uniform(key_fast, (HEADS, TOKENS), minval=0.3, maxval=0.9)
    return jnp.where(lasting[:, None], slow_values, fast_values)


def block_scale(stream_key, shape, pieces, low, top_value):
    loudness = 1.0
    for position, blocks in pieces:
        steps = jax.random.uniform(jax.random.fold_in(jax.random.fold_in(stream_key, 6), position), (blocks,), jnp.float32, low / len(pieces), top_value / len(pieces))
        loudness = loudness * jnp.repeat(jnp.exp(steps), shape[position] // blocks).reshape((-1,) + (1,) * (len(shape) - 1 - position))
    return loudness


def bell_draw(key, extent, spread, reach, cuts=(), kind=jnp.bfloat16):
    drawn = spread * jax.random.normal(key, extent, jnp.float32)
    if cuts:
        drawn = drawn * block_scale(key, extent, cuts, -0.22, 0.18)
    return jnp.clip(drawn, -reach, reach).astype(kind)


def setup_inputs(seed: int = 0) -> dict:
    streams_of = jax.random.split(jax.random.key(seed), 15)
    return {
        "attn_q": bell_draw(streams_of[0], (TOKENS, WIDTH), 1.0, 6.0, ((0, 16), (1, 2))),
        "attn_k": bell_draw(streams_of[1], (TOKENS, WIDTH), 1.0, 6.0, ((0, 16), (1, 2))),
        "attn_v": bell_draw(streams_of[2], (TOKENS, WIDTH), 1.0, 6.0, ((0, 16), (1, 2))),
        "attn_out": bell_draw(streams_of[3], (TOKENS, WIDTH), 0.05, 0.29882812, ((0, 16), (1, 2))),
        "attn_dout": bell_draw(streams_of[4], (TOKENS, WIDTH), 16.0, 96.0, ((0, 16), (1, 2))),
        "attn_lse": jnp.clip(7.0 + 1.0 * jax.random.uniform(streams_of[5], (HEADS, TOKENS), jnp.float32) ** block_scale(streams_of[5], (HEADS, TOKENS), ((0, 2), (1, 16)), -0.2, 0.2), 7.0, 8.0),
        "w_kv": bell_draw(streams_of[6], (WIDTH, 2, WIDTH), WIDTH ** -0.5, 0.25, ((0, 16), (2, 2))),
        "gdn_q": bell_draw(streams_of[7], (TOKENS, WIDTH), 1.0, 6.0, ((0, 16), (1, 2))),
        "gdn_k": bell_draw(streams_of[8], (TOKENS, WIDTH), 1.0, 6.0, ((0, 16), (1, 2))),
        "gdn_v": bell_draw(streams_of[9], (TOKENS, WIDTH), 1.0, 6.0, ((0, 16), (1, 2))),
        "gdn_dout": bell_draw(streams_of[10], (TOKENS, WIDTH), 1.0, 6.0, ((0, 16), (1, 2))),
        "gdn_log_decay": draw_gdn_log_decay(jax.random.fold_in(streams_of[14], 71), 0),
        "gdn_beta": draw_gdn_beta(jax.random.fold_in(streams_of[14], 71), 0),
        "gdn_states": bell_draw(streams_of[13], (BLOCKS, HEADS, HEAD_DIM, HEAD_DIM), 4.0, 24.0, ((0, 16), (1, 2)), jnp.float32),
    }


HIGH = lax.Precision.HIGHEST

def matmul(left_side, right_side):
    return jnp.dot(left_side, right_side, precision=HIGH)

def unit_rows(matrix):
    return matrix * lax.rsqrt(lax.optimization_barrier(jnp.sum(matrix * matrix, axis=-1, keepdims=True)) + 1e-06)

def inverse_unit(lower_part):
    length = lower_part.shape[0]
    identity = jnp.eye(length, dtype=jnp.float32)
    powered = lower_part
    result = identity - lower_part
    for _ in range(length.bit_length() - 2):
        powered = matmul(powered, powered)
        result = matmul(result, identity + powered)
    return result

def block_parts(queries, keys_in, decays, strengths):
    length, depth = queries.shape
    unit_q = unit_rows(queries) * depth ** (-0.5)
    unit_k = unit_rows(keys_in)
    summed = jnp.cumsum(decays)
    row_ids = lax.broadcasted_iota(jnp.int32, (length, length), 0)
    col_ids = lax.broadcasted_iota(jnp.int32, (length, length), 1)
    causal = row_ids >= col_ids
    fading = jnp.where(causal, jnp.exp(jnp.where(causal, summed[:, None] - summed[None, :], 0.0)), 0.0)
    strict = jnp.where(row_ids > col_ids, fading, 0.0)
    lower_part = strengths[:, None] * strict * matmul(unit_k, unit_k.T)
    solved = inverse_unit(lower_part)
    growth = jnp.exp(summed)
    widened = matmul(solved, (strengths * growth)[:, None] * unit_k)
    attention = fading * matmul(unit_q, unit_k.T)
    tailing = jnp.exp(summed[-1] - summed)[:, None] * unit_k
    return (unit_q, solved, growth, widened, attention, tailing)

def block_forward(queries, keys_in, values, decays, strengths, initial):
    unit_q, solved, growth, widened, attention, tailing = block_parts(queries, keys_in, decays, strengths)
    fresh = matmul(solved, strengths[:, None] * values) - matmul(widened, initial)
    output = growth[:, None] * matmul(unit_q, initial) + matmul(attention, fresh)
    final = growth[-1] * initial + matmul(tailing.T, fresh)
    return (output, final)

def block_adjoint(queries, keys_in, decays, strengths, out_grad):
    unit_q, solved, growth, widened, attention, tailing = block_parts(queries, keys_in, decays, strengths)
    depth = queries.shape[1]
    carry_map = growth[-1] * jnp.eye(depth, dtype=jnp.float32) - matmul(widened.T, tailing)
    local_term = matmul((growth[:, None] * unit_q).T, out_grad) - matmul(widened.T, matmul(attention.T, out_grad))
    return (carry_map, local_term)

def block_grads(queries, keys_in, values, decays, strengths, initial, out_grad, later_adjoint):
    _, pullback = jax.vjp(block_forward, queries, keys_in, values, decays, strengths, initial)
    grad_q, grad_k, grad_v, grad_decay, grad_beta, _ = pullback((out_grad, later_adjoint))
    return (grad_q, grad_k, grad_v, grad_decay, grad_beta)

def gdn_head(inputs):
    head_q, head_k, head_v, head_grad, head_decay, head_beta, saved = inputs
    block_count = head_q.shape[0] // BLOCK

    def blocks(matrix):
        return matrix.reshape(block_count, BLOCK, -1)
    queries, keys_in, values, out_grad = (blocks(head_q), blocks(head_k), blocks(head_v), blocks(head_grad))
    decays = head_decay.reshape(block_count, BLOCK)
    strengths = head_beta.reshape(block_count, BLOCK)
    carry_map, local_term = jax.vmap(block_adjoint)(queries, keys_in, decays, strengths, out_grad)

    def backward(carry, couple):
        return (matmul(couple[0], carry) + couple[1], carry)
    nothing = jnp.zeros(saved.shape[1:], jnp.float32)
    _, later_adjoint = lax.scan(backward, nothing, (carry_map, local_term), reverse=True)
    grad_q, grad_k, grad_v, grad_decay, grad_beta = jax.vmap(block_grads)(queries, keys_in, values, decays, strengths, saved, out_grad, later_adjoint)
    depth = head_q.shape[1]
    return (grad_q.reshape(-1, depth), grad_k.reshape(-1, depth), grad_v.reshape(-1, depth), grad_decay.reshape(-1), grad_beta.reshape(-1))

def attention_terms(queries, keys_in, values, out_grad, log_totals, dot_terms, query_pos, key_pos):
    scaling = queries.shape[1] ** (-0.5)
    query_wide = queries.astype(jnp.float32)
    key_wide = keys_in.astype(jnp.float32)
    grad_wide = out_grad.astype(jnp.float32)
    logits = matmul(query_wide, key_wide.T) * scaling
    distance = query_pos[:, None] - key_pos[None, :]
    visible = (distance >= 0) & (distance < WINDOW) & (key_pos[None, :] >= 0)
    chances = jnp.where(visible, jnp.exp(jnp.where(visible, logits - log_totals[:, None], 0.0)), 0.0)
    grad_prob = matmul(grad_wide, values.astype(jnp.float32).T)
    grad_logit = lax.optimization_barrier((chances * (grad_prob - dot_terms[:, None])).astype(jnp.bfloat16)).astype(jnp.float32)
    weights = lax.optimization_barrier(chances.astype(jnp.bfloat16)).astype(jnp.float32)
    grad_q = matmul(grad_logit, key_wide) * scaling
    grad_k = matmul(grad_logit.T, query_wide) * scaling
    grad_v = matmul(weights.T, grad_wide)
    return (grad_q, grad_k, grad_v)

def attention_head(inputs):
    head_q, head_k, head_v, head_out, head_grad, head_log = inputs
    depth = head_q.shape[1]
    dot_terms = lax.optimization_barrier(jnp.sum(head_grad.astype(jnp.float32) * head_out.astype(jnp.float32), axis=1))
    padding = jnp.zeros((WINDOW, depth), jnp.bfloat16)
    padded_k = jnp.concatenate([padding, head_k], axis=0)
    padded_v = jnp.concatenate([padding, head_v], axis=0)

    def one_block(index):
        row_start = (index * TOK_DEV).astype(jnp.int32)
        queries = lax.dynamic_slice_in_dim(head_q, row_start, TOK_DEV, 0)
        out_grad = lax.dynamic_slice_in_dim(head_grad, row_start, TOK_DEV, 0)
        log_totals = lax.dynamic_slice_in_dim(head_log, row_start, TOK_DEV, 0)
        row_terms = lax.dynamic_slice_in_dim(dot_terms, row_start, TOK_DEV, 0)
        keys_in = lax.dynamic_slice_in_dim(padded_k, row_start, WINDOW + TOK_DEV, 0)
        values = lax.dynamic_slice_in_dim(padded_v, row_start, WINDOW + TOK_DEV, 0)
        query_pos = row_start + jnp.arange(TOK_DEV, dtype=jnp.int32)
        key_pos = row_start - WINDOW + jnp.arange(WINDOW + TOK_DEV, dtype=jnp.int32)
        return attention_terms(queries, keys_in, values, out_grad, log_totals, row_terms, query_pos, key_pos)
    grad_q, grad_k, grad_v = lax.map(one_block, jnp.arange(head_q.shape[0] // TOK_DEV, dtype=jnp.int32))
    reach_count = WINDOW // TOK_DEV

    def gather_back(contrib):
        shaped = contrib.reshape(-1, reach_count + 1, TOK_DEV, depth)
        block_count = shaped.shape[0]
        summed = jnp.zeros((block_count + reach_count, TOK_DEV, depth), jnp.float32)
        for index in range(reach_count + 1):
            summed = summed.at[index:index + block_count].add(shaped[:, index])
        return summed[reach_count:].reshape(-1, depth)
    return (grad_q.reshape(-1, depth), gather_back(grad_k), gather_back(grad_v))

def reference(attn_q, attn_k, attn_v, attn_out, attn_dout, attn_lse, w_kv, gdn_q, gdn_k, gdn_v, gdn_dout, gdn_log_decay, gdn_beta, gdn_states):

    def heads_first(matrix):
        return matrix.reshape(matrix.shape[0], HEADS, -1).transpose(1, 0, 2)

    def tokens_first(stacked):
        return stacked.transpose(1, 0, 2).reshape(stacked.shape[1], -1)
    attn_parts = lax.map(attention_head, (heads_first(attn_q), heads_first(attn_k), heads_first(attn_v), heads_first(attn_out), heads_first(attn_dout), attn_lse))
    attn_dq = tokens_first(attn_parts[0]).astype(jnp.bfloat16)
    key_grad = lax.optimization_barrier(tokens_first(attn_parts[1]).astype(jnp.bfloat16)).astype(jnp.float32)
    value_grad = lax.optimization_barrier(tokens_first(attn_parts[2]).astype(jnp.bfloat16)).astype(jnp.float32)
    weights_wide = w_kv.astype(jnp.float32)
    attn_dx = (matmul(weights_wide[:, 0, :], key_grad.T) + matmul(weights_wide[:, 1, :], value_grad.T)).astype(jnp.bfloat16)

    def heads_wide(matrix):
        return heads_first(matrix.astype(jnp.float32))
    gdn_parts = lax.map(gdn_head, (heads_wide(gdn_q), heads_wide(gdn_k), heads_wide(gdn_v), heads_wide(gdn_dout), gdn_log_decay, gdn_beta, gdn_states.transpose(1, 0, 2, 3)))
    gdn_dq = tokens_first(gdn_parts[0]).astype(jnp.bfloat16)
    gdn_dk = tokens_first(gdn_parts[1]).astype(jnp.bfloat16)
    gdn_dv = tokens_first(gdn_parts[2]).astype(jnp.bfloat16)
    return (attn_dq, attn_dx, gdn_dq, gdn_dk, gdn_dv, gdn_parts[3], gdn_parts[4])
```

```python
import functools
import jax
import jax.numpy as jnp
from jax import lax
from jax.experimental import pallas as pl
from jax.experimental.pallas import tpu as pltpu
from jax.sharding import PartitionSpec as P

BLOCK = 64
WINDOW = 1024
EPS = 1e-06
MESH = pl.DeviceIdType.MESH
F32 = jnp.float32
BF16 = jnp.bfloat16

NN = (((1,), (0,)), ((), ()))
NT = (((1,), (1,)), ((), ()))
TN = (((0,), (0,)), ((), ()))


def dot(left, right, dims=NN):
    return lax.dot_general(left, right, dims, preferred_element_type=F32)


def split(matrix):
    high = matrix.astype(BF16)
    return high, (matrix - high.astype(F32)).astype(BF16)


def mm(left, right, dims=NN):
    left_high, left_low = split(left)
    right_high, right_low = split(right)
    return dot(left_high, right_high, dims) + (
        dot(left_high, right_low, dims) + dot(left_low, right_high, dims)
    )


def mm_once(left, right, dims=NN):
    return dot(left.astype(BF16), right.astype(BF16), dims)


def mm_full(left, right, dims=NN):
    return lax.dot_general(
        left, right, dims, precision=lax.Precision.HIGHEST, preferred_element_type=F32
    )


def row_sum(matrix):
    return jnp.sum(matrix, axis=1, keepdims=True)


def column_sum(matrix):
    return jnp.sum(matrix, axis=0, keepdims=True)


def stack_heads(matrix, heads):
    depth = matrix.shape[1] // heads
    return jnp.concatenate([matrix[:, h * depth : (h + 1) * depth] for h in range(heads)], axis=0)


def kernel(
    n,
    head_n,
    q_ref, k_ref, v_ref, out_ref, dout_ref, lse_ref, w_ref,
    gq_ref, gk_ref, gv_ref, gdo_ref, decay_ref, beta_ref, states_ref,
    dq_out, dx_out, gdq_out, gdk_out, gdv_out, gdecay_out, gbeta_out,
    kv_buf, qd_buf, stat_buf, stat_own, w_flat, w_all, ab_send_buf, ab_buf,
    map_hi, map_lo, map_add, carry_in, carry_out, adj_out, adj_in,
    grad_out, grad_in, dx_send, dx_recv, dq_acc, dk_acc, dv_acc, map_buf,
    a_send, a_recv, z_send, z_recv, p_send, p_recv,
    w_send, w_recv, w_pass, ab_send, ab_recv, c_send, c_recv, j_send, j_recv,
    t_send, t_recv, x_send, x_recv,
):
    me = lax.axis_index("seq")
    my_head = lax.axis_index("head")
    rows, columns = q_ref.shape
    heads = lse_ref.shape[0]
    depth = columns // heads
    blocks = rows // BLOCK
    total = heads * rows
    size = 2 * heads
    groups = n // size
    steps = WINDOW // (size * rows)
    reach = 2 * steps
    rank = lax.rem(me, size)
    group = lax.div(me, size)
    first = group * size
    core = lax.rem(my_head, 2)
    pair = my_head - core
    partner = pair + 1 - core
    half = lax.div(rank, heads)
    place = lax.rem(rank, heads)
    place_rows = pl.ds(pl.multiple_of(place * rows, rows), rows)
    composer = half == core
    scaling = depth ** (-0.5)

    barrier = pltpu.get_barrier_semaphore()

    def greet(device):
        pl.semaphore_signal(barrier, inc=1, device_id=device, device_id_type=MESH)

    for j in range(1, size):
        peer = first + lax.rem(rank + j, size)
        greet({"seq": peer, "head": my_head})
        greet({"seq": peer, "head": partner})
    for m in range(1, groups):
        greet({"seq": lax.rem(me + m * size, n), "head": my_head})
    for j in range(1, head_n):
        greet({"seq": me, "head": lax.rem(my_head + j, head_n)})
    greeted = 2 * (size - 1) + groups - 1 + head_n - 1

    ones = jnp.ones((8, depth), F32)
    top = lax.broadcasted_iota(jnp.int32, (8, rows), 0) == 0
    for h in range(heads):
        cols = slice(h * depth, (h + 1) * depth)
        product = dout_ref[:, cols].astype(F32) * out_ref[:, cols].astype(F32)
        stat_own[h] = jnp.where(top, lse_ref[h : h + 1, :], mm_full(ones, product, NT))
    w_flat[:, :columns] = w_ref[:, 0, :]
    w_flat[:, columns:] = w_ref[:, 1, :]
    pl.semaphore_wait(barrier, greeted)

    def move(source, target, sent, received, seq, head):
        return pltpu.make_async_remote_copy(
            src_ref=source,
            dst_ref=target,
            send_sem=sent,
            recv_sem=received,
            device_id={"seq": seq, "head": head},
            device_id_type=MESH,
        )

    own_kv = 1 - core
    own_qd = core

    def spread_refs(h, kind):
        cols = slice(h * depth, (h + 1) * depth)
        if kind == 4:
            return stat_own.at[h], stat_buf.at[half, place]
        source = (k_ref, v_ref, q_ref, dout_ref)[kind].at[:, cols]
        if kind < 2:
            return source, kv_buf.at[1 - half, kind, place_rows, :]
        return source, qd_buf.at[half, kind - 2, place_rows, :]

    def spread(h, kind):
        source, target = spread_refs(h, kind)
        return move(
            source, target, a_send.at[h, kind], a_recv.at[place, kind],
            first + heads * core + h, pair + half,
        )

    def spread_here(h, kind):
        source, target = spread_refs(h, kind)
        return pltpu.make_async_copy(source, target, a_recv.at[place, kind])

    def spread_in(block, kind):
        part_rows = slice(block * rows, (block + 1) * rows)
        if kind == 4:
            target = stat_buf.at[own_qd, block]
        elif kind < 2:
            target = kv_buf.at[own_kv, kind, part_rows, :]
        else:
            target = qd_buf.at[own_qd, kind - 2, part_rows, :]
        return move(
            target, target, a_send.at[0, kind], a_recv.at[block, kind], me, partner
        )

    def start_spread(kinds):
        for kind in kinds:
            for h in range(heads):
                @pl.when(heads * core + h == rank)
                def _():
                    spread_here(h, kind).start()

                @pl.when(heads * core + h != rank)
                def _():
                    spread(h, kind).start()

    def take_spread(kinds):
        for kind in kinds:
            for block in range(heads):
                spread_in(block, kind).wait_recv()

    def chunk(kind, index):
        if kind == 4:
            return stat_buf.at[index]
        if kind < 2:
            return kv_buf.at[index, kind]
        return qd_buf.at[index, kind - 2]

    def slot(kind, m, lane):
        return 2 * m + 1 - lane if kind < 2 else 2 * m + lane

    def hop(kind, m):
        return move(
            chunk(kind, slot(kind, m - 1, core)), chunk(kind, slot(kind, m, core)),
            z_send.at[m - 1, kind], z_recv.at[m - 1, kind],
            lax.rem(me + (size if kind < 2 else n - size), n), my_head,
        )

    def hop_goes(kind, m):
        if kind < 2:
            return (group >= m - 1) & (group + 1 < groups)
        return (group + m - 1 < groups) & (group >= 1)

    def there(kind, m):
        return group >= m if kind < 2 else group + m < groups

    def share(kind, m):
        refs = chunk(kind, slot(kind, m, core))
        return move(refs, refs, p_send.at[m, kind], p_recv.at[m, kind], me, partner)

    def share_in(kind, m):
        refs = chunk(kind, slot(kind, m, 1 - core))
        return move(refs, refs, p_send.at[m, kind], p_recv.at[m, kind], me, partner)

    def share_goes(kind, m):
        near, far = (0, 1) if kind < 2 else (1, 0)
        needed = there(kind, m)
        if m == 0:
            needed = needed & (core == near)
        if m == steps:
            needed = needed & (core == far)
        return needed

    def share_comes(kind, m):
        near, far = (1, 0) if kind < 2 else (0, 1)
        needed = there(kind, m)
        if m == 0:
            needed = needed & (core == near)
        if m == steps:
            needed = needed & (core == far)
        return needed

    KEYS = (0, 1)
    QUERIES = (2, 3, 4)

    def act_if(condition, copy, act):
        @pl.when(condition)
        def _():
            getattr(copy, act)()

    def send_on(kinds, m):
        for kind in kinds:
            if m < steps:
                act_if(hop_goes(kind, m + 1), hop(kind, m + 1), "start")
        for kind in kinds:
            act_if(share_goes(kind, m), share(kind, m), "start")

    def arrive(kinds, m):
        for kind in kinds:
            act_if(there(kind, m), hop(kind, m), "wait_recv")
            if m < steps:
                act_if(hop_goes(kind, m + 1), hop(kind, m + 1), "start")
            act_if(share_goes(kind, m), share(kind, m), "start")

    w_rows = w_ref.shape[0]

    def w_copy(m):
        return move(
            w_flat, w_all.at[me], w_send.at[m - 1], w_recv.at[0, m],
            lax.rem(me + m * size, n), my_head,
        )

    def w_passes(i):
        peer = first + lax.rem(rank + i, size)
        return [
            move(
                w_flat if m == 0 else w_all.at[lax.rem(me + n - m * size, n)],
                w_all.at[lax.rem(me + n - m * size, n)],
                w_pass.at[i, m], w_recv.at[i, m], peer, my_head,
            )
            for m in range(groups)
        ]

    def each(copies, act):
        for copy in copies:
            getattr(copy, act)()

    def ab_copy(h):
        return move(
            ab_send_buf.at[h], ab_buf.at[rank], ab_send.at[h], ab_recv.at[rank],
            first + heads * core + h, my_head,
        )

    def ab_in(j):
        source = lax.rem(rank + j, size)
        return move(
            ab_buf.at[source], ab_buf.at[source], ab_send.at[0], ab_recv.at[source], me, partner
        )

    def carry_copy():
        return move(carry_out, carry_in, c_send, c_recv, lax.rem(me + n - size, n), my_head)

    def adj_copy(j):
        target = lax.rem(rank + j, size)
        return move(
            adj_out.at[target], adj_in.at[place], j_send.at[j - 1], j_recv.at[place],
            first + target, my_head,
        )

    def adj_arrival(h):
        return move(adj_in.at[h], adj_in.at[h], j_send.at[0], j_recv.at[h], me, partner)

    def back_rank(block):
        return core * heads + block

    def back_copy(block, item):
        return move(
            grad_out.at[item, block], grad_in.at[place, item],
            t_send.at[block, item], t_recv.at[place, item],
            first + back_rank(block), pair + half,
        )

    def back_here(block, item):
        return pltpu.make_async_copy(
            grad_out.at[item, block], grad_in.at[place, item], t_recv.at[place, item]
        )

    def back_in(h, item):
        return move(
            grad_in.at[h, item], grad_in.at[h, item],
            t_send.at[0, item], t_recv.at[h, item], me, partner,
        )

    def start_back(items):
        for item in items:
            for block in range(heads):
                act_if(back_rank(block) == rank, back_here(block, item), "start")
                act_if(back_rank(block) != rank, back_copy(block, item), "start")

    start_spread(KEYS + QUERIES)
    for m in range(1, groups):
        w_copy(m).start()

    row_ids = lax.broadcasted_iota(jnp.int32, (total, total), 0)
    col_ids = lax.broadcasted_iota(jnp.int32, (total, total), 1)
    shift = BLOCK.bit_length() - 1
    same = lax.shift_right_logical(row_ids, shift) == lax.shift_right_logical(col_ids, shift)
    eye = row_ids == col_ids
    causal = same & (row_ids >= col_ids)
    strict = same & (row_ids > col_ids)

    def to_column(row):
        return row_sum(jnp.where(eye, row, 0.0))

    def to_row(column):
        return column_sum(jnp.where(eye, column, 0.0))

    def flat_row(ref):
        return jnp.concatenate([ref[h : h + 1, :] for h in range(heads)], axis=1)

    decay_row = flat_row(decay_ref)
    decay_col = to_column(decay_row)
    beta = to_column(flat_row(beta_ref))
    summed = row_sum(jnp.where(causal, decay_row, 0.0))
    summed_row = column_sum(jnp.where(same & (row_ids <= col_ids), decay_col, 0.0))
    whole = row_sum(jnp.where(same, decay_row, 0.0))
    growth = jnp.exp(summed)
    tail = jnp.exp(row_sum(jnp.where(same & (row_ids < col_ids), decay_row, 0.0)))
    end_growth = jnp.exp(whole)
    raw_q = stack_heads(gq_ref[...], heads).astype(F32)
    raw_k = stack_heads(gk_ref[...], heads).astype(F32)
    values = stack_heads(gv_ref[...], heads).astype(F32)
    out_grad = stack_heads(gdo_ref[...], heads).astype(F32)
    inv_q = lax.rsqrt(row_sum(raw_q * raw_q) + EPS)
    inv_k = lax.rsqrt(row_sum(raw_k * raw_k) + EPS)
    unit_q = raw_q * inv_q * scaling
    unit_k = raw_k * inv_k
    fading = jnp.where(causal, jnp.exp(jnp.where(causal, summed - summed_row, 0.0)), 0.0)
    products = mm(jnp.concatenate([unit_k, unit_q], axis=0), unit_k, NT)
    key_products = products[:total]
    query_products = products[total:]
    strict_fading = jnp.where(strict, fading, 0.0)
    faded_keys = strict_fading * key_products
    lower = beta * faded_keys
    solved = jnp.where(eye, 1.0, 0.0) - lower
    powered = mm(lower, lower)
    for step in range(BLOCK.bit_length() - 2):
        if step < BLOCK.bit_length() - 3:
            both = mm(jnp.concatenate([solved, powered], axis=0), powered)
            solved = solved + both[:total]
            powered = both[total:]
        else:
            solved = solved + mm(solved, powered)
    attention = fading * query_products
    widened = mm(solved, (beta * growth) * unit_k)
    pulled = mm(attention, out_grad, TN)
    tailing = tail * unit_k
    grown_q = growth * unit_q

    def part(matrix, h, b):
        start = h * rows + b * BLOCK
        return matrix[start : start + BLOCK]

    depth_eye = jnp.where(
        lax.broadcasted_iota(jnp.int32, (depth, depth), 0)
        == lax.broadcasted_iota(jnp.int32, (depth, depth), 1),
        1.0,
        0.0,
    )
    for h in range(heads):
        across = None
        for b in reversed(range(blocks)):
            wide = part(widened, h, b)
            right = jnp.concatenate([part(tailing, h, b), part(pulled, h, b)], axis=1)
            product = mm(wide, right, TN)
            carry_map = part(end_growth, h, b)[0:1, :] * depth_eye - product[:, :depth]
            local = mm(part(grown_q, h, b), part(out_grad, h, b), TN) - product[:, depth:]
            map_buf[h, b, :, :depth] = carry_map
            map_buf[h, b, :, depth:] = local
            if across is None:
                across, offset = carry_map, local
            else:
                joined = mm(carry_map, jnp.concatenate([across, offset], axis=1))
                across, offset = joined[:, :depth], joined[:, depth:] + local
        change = jnp.concatenate([across - depth_eye, offset], axis=1).astype(BF16)
        ab_send_buf[h] = change

        @pl.when(heads * core + h == rank)
        def _():
            ab_buf[rank] = change

        act_if(heads * core + h != rank, ab_copy(h), "start")

    take_spread(KEYS)
    send_on(KEYS, 0)
    take_spread(QUERIES)
    send_on(QUERIES, 0)

    key_ids = row_ids
    query_ids = col_ids

    def stat_row(index, which):
        return jnp.concatenate(
            [stat_buf[index, block, which : which + 1, :] for block in range(heads)], axis=1
        )

    def terms(logits, grad_prob, lse, dots, mask):
        shifted = logits * scaling - lse
        if mask is None:
            chances = jnp.exp(shifted)
        else:
            chances = jnp.where(mask, jnp.exp(jnp.where(mask, shifted, 0.0)), 0.0)
        return (chances * (grad_prob - dots)).astype(BF16), chances.astype(BF16)

    own_lse = stat_row(own_qd, 0)
    own_dots = stat_row(own_qd, 1)
    keys = kv_buf[own_kv, 0]
    queries = qd_buf[own_qd, 0]
    grads = qd_buf[own_qd, 1]
    grad_logit, weights = terms(
        dot(keys, queries, NT), dot(kv_buf[own_kv, 1], grads, NT),
        own_lse, own_dots, query_ids >= key_ids,
    )
    dq_acc[...] = dot(grad_logit, keys, TN)
    dk_acc[...] = dot(grad_logit, queries)
    dv_acc[...] = dot(weights, grads)
    lse_column = to_column(own_lse)
    dots_column = to_column(own_dots)

    def attend_keys(d):
        @pl.when(2 * group + core >= d)
        def _():
            keys = kv_buf[d + 1 - core, 0]
            grad_logit, _ = terms(
                dot(qd_buf[own_qd, 0], keys, NT),
                dot(qd_buf[own_qd, 1], kv_buf[d + 1 - core, 1], NT),
                lse_column, dots_column, row_ids < col_ids if d == reach else None,
            )
            dq_acc[...] += dot(grad_logit, keys)

    def attend_queries(d):
        @pl.when(2 * group + core + d < 2 * groups)
        def _():
            queries = qd_buf[d + core, 0]
            grads = qd_buf[d + core, 1]
            grad_logit, weights = terms(
                dot(kv_buf[own_kv, 0], queries, NT), dot(kv_buf[own_kv, 1], grads, NT),
                stat_row(d + core, 0), stat_row(d + core, 1),
                query_ids < key_ids if d == reach else None,
            )
            dk_acc[...] += dot(grad_logit, queries)
            dv_acc[...] += dot(weights, grads)

    def attend_shared(d):
        for lane in range(2):
            m = (d + 1 - lane) // 2
            for kind in KEYS:
                act_if(share_comes(kind, m) & (core == lane), share_in(kind, m), "wait_recv")
        attend_keys(d)
        for lane in range(2):
            m = (d + lane) // 2
            for kind in QUERIES:
                act_if(share_comes(kind, m) & (core == lane), share_in(kind, m), "wait_recv")
        attend_queries(d)

    pairs = [(h, b) for h in range(heads) for b in range(blocks)]

    def by_parts(make):
        return jnp.concatenate([make(h, b) for h, b in pairs], axis=0)

    reads = [
        mm(jnp.concatenate([part(unit_k, h, b), part(unit_q, h, b)], axis=0), states_ref[b, h])
        for h, b in pairs
    ]
    key_reads = jnp.concatenate([item[:BLOCK] for item in reads], axis=0)
    query_reads = jnp.concatenate([item[BLOCK:] for item in reads], axis=0)
    remainder = values - growth * key_reads
    fresh = mm(solved, beta * remainder)
    faded_grad = fading * mm(out_grad, fresh, NT)
    out_back = by_parts(lambda h, b: mm_once(part(out_grad, h, b), states_ref[b, h], NT))
    unit_q_grad = growth * out_back + mm_once(faded_grad, unit_k)
    faded_back = mm_once(faded_grad, unit_q, TN)

    for m in range(1, groups):
        w_copy(m).wait_recv()
    for i in range(1, size):
        each(w_passes(i), "start")

    @pl.when(composer)
    def _():
        joined = None
        for j in range(1, size):
            ab_in(j).wait_recv()
        for r in reversed(range(size)):
            change = ab_buf[r, :, :depth]
            local = ab_buf[r, :, depth:].astype(F32)
            if joined is None:
                joined = jnp.concatenate([change.astype(F32) + depth_eye, local], axis=1)
            else:
                high, low = split(joined)
                joined = joined + (dot(change, high) + dot(change, low))
                joined = jnp.concatenate([joined[:, :depth], joined[:, depth:] + local], axis=1)
            map_hi[r], map_lo[r] = split(joined[:, :depth])
            map_add[r] = joined[:, depth:]

    def carry_step(condition):
        @pl.when(composer & condition)
        def _():
            @pl.when(group == groups - 1)
            def _():
                carry_in[...] = jnp.zeros_like(carry_in)

            act_if(group < groups - 1, carry_copy(), "wait_recv")
            state = carry_in[...]

            def start_of(r):
                return (dot(map_hi[r], state) + dot(map_lo[r], state) + map_add[r]).astype(BF16)

            carry_out[...] = start_of(0)
            act_if(group > 0, carry_copy(), "start")
            for r in range(size - 1):
                adj_out[r] = start_of(r + 1)
            adj_out[size - 1] = state
            for j in range(1, size):
                adj_copy(j).start()
            adj_in[place] = adj_out[rank]

    last = groups - 1 - group
    carry_step(last == 0)
    arrive(KEYS, 1)
    arrive(QUERIES, 1)
    attend_keys(2)
    attend_queries(2)
    carry_step(last == 1)
    attend_shared(1)
    for m in range(2, steps + 1):
        arrive(KEYS, m)
        arrive(QUERIES, m)
    carry_step(last == 2)
    for d in range(3, reach + 1):
        if d % 2:
            attend_shared(d)
        else:
            attend_keys(d)
            attend_queries(d)

    def blocks_of(matrix):
        return matrix.astype(BF16).reshape(heads, rows, depth)

    grad_out[1] = blocks_of(dk_acc[...] * scaling)
    grad_out[2] = blocks_of(dv_acc[...])
    grad_out[0] = blocks_of(dq_acc[...] * scaling)
    start_back((1, 2, 0))
    carry_step(last >= 3)

    for h in range(heads):
        act_if(heads * core + h != rank, adj_arrival(h), "wait_recv")
    later = {}
    for h in range(heads):
        adjoint = adj_in[h].astype(F32)
        for b in reversed(range(blocks)):
            later[h, b] = adjoint
            if b > 0:
                adjoint = mm(map_buf[h, b, :, :depth], adjoint) + map_buf[h, b, :, depth:]
    fresh_grad = pulled + by_parts(lambda h, b: mm(part(tailing, h, b), later[h, b]))
    solved_grad = mm(solved, fresh_grad, TN)
    lower_grad = -mm(solved_grad, fresh, NT)
    key_products_grad = beta * strict_fading * lower_grad
    value_grad = beta * solved_grad
    value_back = by_parts(lambda h, b: mm_once(part(value_grad, h, b), states_ref[b, h], NT))
    fresh_back = tail * by_parts(lambda h, b: mm(part(fresh, h, b), later[h, b], NT))
    unit_k_grad = (
        fresh_back
        - growth * value_back
        + faded_back
        + mm_once(key_products_grad, unit_k)
        + mm_once(key_products_grad, unit_k, TN)
    )
    q_grad = scaling * inv_q * (unit_q_grad - raw_q * (inv_q * inv_q * row_sum(unit_q_grad * raw_q)))
    k_grad = inv_k * (unit_k_grad - raw_k * (inv_k * inv_k * row_sum(unit_k_grad * raw_k)))
    for h in range(heads):
        cols = slice(h * depth, (h + 1) * depth)
        own = slice(h * rows, (h + 1) * rows)
        gdq_out[:, cols] = q_grad[own].astype(BF16)
        gdk_out[:, cols] = k_grad[own].astype(BF16)
        gdv_out[:, cols] = value_grad[own].astype(BF16)
    beta_grad = row_sum(solved_grad * remainder) + row_sum(lower_grad * faded_keys)
    exponent = faded_grad * query_products + key_products_grad * key_products
    tail_grad = row_sum(unit_k * fresh_back)
    growth_grad = row_sum(out_grad * query_reads) - row_sum(value_grad * key_reads)
    summed_grad = (
        row_sum(exponent) - to_column(column_sum(exponent)) - tail_grad + growth * growth_grad
    )
    end_grad = end_growth * by_parts(
        lambda h, b: jnp.broadcast_to(
            column_sum(row_sum(later[h, b] * states_ref[b, h])), (BLOCK, 1)
        )
    )
    decay_grad = (
        column_sum(jnp.where(causal, summed_grad, 0.0))
        + column_sum(jnp.where(same, tail_grad, 0.0))
        + to_row(end_grad)
    )
    beta_row = to_row(beta_grad)
    for h in range(heads):
        own = slice(h * rows, (h + 1) * rows)
        gdecay_out[h : h + 1, :] = decay_grad[:, own]
        gbeta_out[h : h + 1, :] = beta_row[:, own]

    for item in (1, 2, 0):
        for h in range(heads):
            back_in(h, item).wait_recv()
    for h in range(heads):
        dq_out[:, h * depth : (h + 1) * depth] = grad_in[h, 0]
    both_grads = jnp.concatenate(
        [grad_in[h, item] for item in (1, 2) for h in range(heads)], axis=1
    )
    w_all[me] = w_flat[...]
    for i in range(1, size):
        each(w_passes(i), "wait_recv")
    out_rows = dx_out.shape[0]
    pieces_each = out_rows // w_rows

    def dx_rows(owner):
        piece = w_all[pl.ds(owner * pieces_each, pieces_each)].reshape(out_rows, 2 * columns)
        return dot(piece, both_grads, NT)

    def dx_copy(j):
        return move(
            dx_send.at[j - 1], dx_recv.at[j - 1], x_send.at[j - 1], x_recv.at[j - 1],
            me, lax.rem(my_head + j, head_n),
        )

    for j in range(1, head_n):
        dx_send[j - 1] = dx_rows(lax.rem(my_head + j, head_n))
        dx_copy(j).start()
    result = dx_rows(my_head)
    for j in range(1, head_n):
        dx_copy(j).wait_recv()
        result = result + dx_recv[j - 1]
    dx_out[...] = result.astype(BF16)

    for kind in KEYS + QUERIES:
        for h in range(heads):
            act_if(heads * core + h != rank, spread(h, kind), "wait_send")
        for m in range(steps + 1):
            if m:
                act_if(hop_goes(kind, m), hop(kind, m), "wait_send")
            act_if(share_goes(kind, m), share(kind, m), "wait_send")
    for m in range(1, groups):
        w_copy(m).wait_send()
    for i in range(1, size):
        each(w_passes(i), "wait_send")
    for h in range(heads):
        act_if(heads * core + h != rank, ab_copy(h), "wait_send")
    act_if(composer & (group > 0), carry_copy(), "wait_send")
    for j in range(1, size):
        act_if(composer, adj_copy(j), "wait_send")
    for item in range(3):
        for block in range(heads):
            act_if(back_rank(block) != rank, back_copy(block, item), "wait_send")
    for j in range(1, head_n):
        dx_copy(j).wait_send()


def hand_over(*refs):
    half = len(refs) // 2
    for source, target in zip(refs[:half], refs[half:]):
        target[...] = source[...]


def per_device(n, head_n, *args):
    attn_q, attn_lse, w_kv, states = args[0], args[5], args[6], args[13]
    rows, columns = attn_q.shape
    heads = attn_lse.shape[0]
    depth = columns // heads
    size = 2 * heads
    steps = WINDOW // (size * rows)
    blocks = states.shape[0]
    groups = n // size
    assert head_n % 2 == 0 and n % size == 0 and WINDOW == steps * size * rows
    w_rows = w_kv.shape[0]
    out_rows = n * w_rows // head_n
    dma = pltpu.SemaphoreType.DMA
    vmem = pl.BlockSpec(memory_space=pltpu.VMEM)
    others = max(head_n - 1, 1)
    slots = 2 * (steps + 1)
    span = heads * rows
    results = pl.pallas_call(
        functools.partial(kernel, n, head_n),
        out_shape=(
            jax.ShapeDtypeStruct((rows, columns), BF16),
            jax.ShapeDtypeStruct((out_rows, rows), BF16),
            jax.ShapeDtypeStruct((rows, columns), BF16),
            jax.ShapeDtypeStruct((rows, columns), BF16),
            jax.ShapeDtypeStruct((rows, columns), BF16),
            jax.ShapeDtypeStruct((heads, rows), F32),
            jax.ShapeDtypeStruct((heads, rows), F32),
        ),
        in_specs=[vmem] * len(args),
        out_specs=(vmem,) * 7,
        scratch_shapes=[
            pltpu.VMEM((slots, 2, span, depth), BF16),
            pltpu.VMEM((slots, 2, span, depth), BF16),
            pltpu.VMEM((slots, heads, 8, rows), F32),
            pltpu.VMEM((heads, 8, rows), F32),
            pltpu.VMEM((w_rows, 2 * columns), BF16),
            pltpu.VMEM((n, w_rows, 2 * columns), BF16),
            pltpu.VMEM((heads, depth, 2 * depth), BF16),
            pltpu.VMEM((size, depth, 2 * depth), BF16),
            pltpu.VMEM((size, depth, depth), BF16),
            pltpu.VMEM((size, depth, depth), BF16),
            pltpu.VMEM((size, depth, depth), F32),
            pltpu.VMEM((depth, depth), BF16),
            pltpu.VMEM((depth, depth), BF16),
            pltpu.VMEM((size, depth, depth), BF16),
            pltpu.VMEM((heads, depth, depth), BF16),
            pltpu.VMEM((3, heads, rows, depth), BF16),
            pltpu.VMEM((heads, 3, rows, depth), BF16),
            pltpu.VMEM((others, out_rows, rows), F32),
            pltpu.VMEM((others, out_rows, rows), F32),
            pltpu.VMEM((span, depth), F32),
            pltpu.VMEM((span, depth), F32),
            pltpu.VMEM((span, depth), F32),
            pltpu.VMEM((heads, blocks, depth, 2 * depth), F32),
            dma((heads, 5)), dma((heads, 5)),
            dma((steps, 5)), dma((steps, 5)),
            dma((steps + 1, 5)), dma((steps + 1, 5)),
            dma((groups,)), dma((size, groups)), dma((size, groups)),
            dma((heads,)), dma((size,)),
            dma, dma,
            dma((size,)), dma((heads,)),
            dma((heads, 3)), dma((heads, 3)),
            dma((others,)), dma((others,)),
        ],
        compiler_params=pltpu.CompilerParams(
            collective_id=0, has_side_effects=True, vmem_limit_bytes=60000000
        ),
        name="layer_backward",
    )(*args)
    return pl.pallas_call(
        hand_over,
        out_shape=[jax.ShapeDtypeStruct(item.shape, item.dtype) for item in results],
        in_specs=[vmem] * len(results),
        out_specs=[vmem] * len(results),
        name="hand_over",
    )(*results)


def solution(mesh):
    rows = P("seq", "head")
    gates = P("head", "seq")
    return jax.shard_map(
        functools.partial(per_device, mesh.shape["seq"], mesh.shape["head"]),
        mesh=mesh,
        in_specs=(
            rows, rows, rows, rows, rows, gates, P("seq", None, "head"),
            rows, rows, rows, rows, gates, gates, P("seq", "head", None, None),
        ),
        out_specs=(rows, gates, rows, rows, rows, gates, gates),
        check_vma=False,
    )
```

```python
import functools
import jax
import jax.numpy as jnp
from jax import lax
from jax.experimental import pallas as pl
from jax.experimental.pallas import tpu as pltpu
from jax.sharding import PartitionSpec as P

BLOCK = 64
WINDOW = 1024
EPS = 1e-06
MESH = pl.DeviceIdType.MESH
F32 = jnp.float32
BF16 = jnp.bfloat16

NN = (((1,), (0,)), ((), ()))
NT = (((1,), (1,)), ((), ()))
TN = (((0,), (0,)), ((), ()))


def dot(left, right, dims=NN):
    return lax.dot_general(left, right, dims, preferred_element_type=F32)


def split(matrix):
    high = matrix.astype(BF16)
    return high, (matrix - high.astype(F32)).astype(BF16)


def mm(left, right, dims=NN):
    left_high, left_low = split(left)
    right_high, right_low = split(right)
    return dot(left_high, right_high, dims) + (
        dot(left_high, right_low, dims) + dot(left_low, right_high, dims)
    )


def mm_once(left, right, dims=NN):
    return dot(left.astype(BF16), right.astype(BF16), dims)


def mm_full(left, right, dims=NN):
    return lax.dot_general(
        left, right, dims, precision=lax.Precision.HIGHEST, preferred_element_type=F32
    )


def row_sum(matrix):
    return jnp.sum(matrix, axis=1, keepdims=True)


def column_sum(matrix):
    return jnp.sum(matrix, axis=0, keepdims=True)


def stack_heads(matrix, heads):
    depth = matrix.shape[1] // heads
    return jnp.concatenate([matrix[:, h * depth : (h + 1) * depth] for h in range(heads)], axis=0)


def kernel(
    n,
    head_n,
    q_hbm, k_hbm, v_hbm, out_hbm, dout_hbm, lse_hbm, w_hbm,
    gq_hbm, gk_hbm, gv_hbm, gdo_hbm, decay_hbm, beta_hbm, states_hbm,
    dq_out, dx_out, gdq_out, gdk_out, gdv_out, gdecay_out, gbeta_out,
    out_ref, dout_ref, lse_ref, w_ref,
    gq_ref, gk_ref, gv_ref, gdo_ref, decay_ref, beta_ref, states_ref,
    kv_buf, qd_buf, stat_buf, stat_own, w_all, ab_send_buf, ab_buf,
    map_hi, map_lo, map_add, whole_out, whole_in, carry_in, carry_out, adj_out, adj_in,
    grad_out, grad_in, dx_send, dx_recv, dq_acc, dk_acc, dv_acc, map_buf,
    sems, a_recv, z_send, z_recv, p_send, p_recv,
    w_send, w_recv, w_pass, w_taken, ab_send, ab_recv, o_send, o_recv, c_send, c_recv, j_recv,
    t_recv, x_recv,
):
    me = lax.axis_index("seq")
    my_head = lax.axis_index("head")
    rows, columns = q_hbm.shape
    heads = lse_ref.shape[0]
    depth = columns // heads
    blocks = rows // BLOCK
    total = heads * rows
    size = 2 * heads
    groups = n // size
    steps = WINDOW // (size * rows)
    reach = 2 * steps
    rank = lax.rem(me, size)
    group = lax.div(me, size)
    first = group * size
    core = lax.rem(my_head, 2)
    pair = my_head - core
    partner = pair + 1 - core
    half = lax.div(rank, heads)
    place = lax.rem(rank, heads)
    place_rows = pl.ds(pl.multiple_of(place * rows, rows), rows)
    composer = half == core
    scaling = depth ** (-0.5)

    barrier = pltpu.get_barrier_semaphore()

    def greet(device):
        pl.semaphore_signal(barrier, inc=1, device_id=device, device_id_type=MESH)

    for j in range(1, size):
        peer = first + lax.rem(rank + j, size)
        greet({"seq": peer, "head": my_head})
        greet({"seq": peer, "head": partner})
    for m in range(1, groups):
        greet({"seq": lax.rem(me + m * size, n), "head": my_head})
    for j in range(1, head_n):
        greet({"seq": me, "head": lax.rem(my_head + j, head_n)})
    greeted = 2 * (size - 1) + groups - 1 + head_n - 1

    def load(source, target, index):
        copy = pltpu.make_async_copy(source, target, sems.at[index])
        copy.start()
        return copy

    gdn_loads = [
        load(source, target, index)
        for index, (source, target) in enumerate([
            (decay_hbm, decay_ref), (beta_hbm, beta_ref), (gk_hbm, gk_ref), (gq_hbm, gq_ref),
            (gv_hbm, gv_ref), (gdo_hbm, gdo_ref),
        ])
    ]
    attention_loads = [
        load(source, target, len(gdn_loads) + index)
        for index, (source, target) in enumerate([
            (lse_hbm, lse_ref), (dout_hbm, dout_ref), (out_hbm, out_ref), (w_hbm, w_ref),
        ])
    ]
    states_load = load(states_hbm, states_ref, 10)
    for copy in gdn_loads:
        copy.wait()

    def move(source, target, sent, received, seq, head):
        return pltpu.make_async_remote_copy(
            src_ref=source,
            dst_ref=target,
            send_sem=sent,
            recv_sem=received,
            device_id={"seq": seq, "head": head},
            device_id_type=MESH,
        )

    own_kv = 1 - core
    own_qd = core

    def spread_refs(h, kind):
        cols = slice(h * depth, (h + 1) * depth)
        if kind == 4:
            return stat_own.at[h], stat_buf.at[half, place]
        source = (k_hbm, v_hbm, q_hbm, dout_hbm)[kind].at[:, cols]
        if kind < 2:
            return source, kv_buf.at[1 - half, kind, place_rows, :]
        return source, qd_buf.at[half, kind - 2, place_rows, :]

    def spread(h, kind):
        source, target = spread_refs(h, kind)
        return move(
            source, target, sems.at[5 * h + kind], a_recv.at[place, kind],
            first + heads * core + h, pair + half,
        )

    def spread_here(h, kind):
        source, target = spread_refs(h, kind)
        return pltpu.make_async_copy(source, target, a_recv.at[place, kind])

    def spread_in(block, kind):
        part_rows = slice(block * rows, (block + 1) * rows)
        if kind == 4:
            target = stat_buf.at[own_qd, block]
        elif kind < 2:
            target = kv_buf.at[own_kv, kind, part_rows, :]
        else:
            target = qd_buf.at[own_qd, kind - 2, part_rows, :]
        return move(
            target, target, sems.at[kind], a_recv.at[block, kind], me, partner
        )

    def start_spread(kinds):
        for kind in kinds:
            for h in range(heads):
                @pl.when(heads * core + h == rank)
                def _():
                    spread_here(h, kind).start()

                @pl.when(heads * core + h != rank)
                def _():
                    spread(h, kind).start()

    def take_spread(kinds):
        for kind in kinds:
            for block in range(heads):
                spread_in(block, kind).wait_recv()

    def chunk(kind, index):
        if kind == 4:
            return stat_buf.at[index]
        if kind < 2:
            return kv_buf.at[index, kind]
        return qd_buf.at[index, kind - 2]

    def slot(kind, m, lane):
        return 2 * m + 1 - lane if kind < 2 else 2 * m + lane

    def hop(kind, m):
        return move(
            chunk(kind, slot(kind, m - 1, core)), chunk(kind, slot(kind, m, core)),
            z_send.at[kind], z_recv.at[m - 1, kind],
            lax.rem(me + (size if kind < 2 else n - size), n), my_head,
        )

    def hop_goes(kind, m):
        if kind < 2:
            return (group >= m - 1) & (group + 1 < groups)
        return (group + m - 1 < groups) & (group >= 1)

    def there(kind, m):
        return group >= m if kind < 2 else group + m < groups

    def share_refs(kind, m, lane):
        index = slot(kind, m, lane)
        return kv_buf.at[index] if kind == 0 else qd_buf.at[index] if kind == 2 else stat_buf.at[index]

    def share(kind, m):
        refs = share_refs(kind, m, core)
        return move(refs, refs, p_send.at[kind // 2], p_recv.at[m, kind // 2], me, partner)

    def share_in(kind, m):
        refs = share_refs(kind, m, 1 - core)
        return move(refs, refs, p_send.at[kind // 2], p_recv.at[m, kind // 2], me, partner)

    def share_goes(kind, m):
        near, far = (0, 1) if kind < 2 else (1, 0)
        needed = there(kind, m)
        if m == 0:
            needed = needed & (core == near)
        if m == steps:
            needed = needed & (core == far)
        return needed

    def share_comes(kind, m):
        near, far = (1, 0) if kind < 2 else (0, 1)
        needed = there(kind, m)
        if m == 0:
            needed = needed & (core == near)
        if m == steps:
            needed = needed & (core == far)
        return needed

    KEYS = (0, 1)
    QUERIES = (2, 3, 4)

    def act_if(condition, copy, act):
        @pl.when(condition)
        def _():
            getattr(copy, act)()

    def pass_on(kind, m):
        act_if(hop_goes(kind, m + 1), hop(kind, m + 1), "start")

    def share_all(kinds, m):
        for kind in kinds:
            if kind % 2 == 0:
                if m:
                    act_if(share_goes(kind, m - 1), share(kind, m - 1), "wait_send")
                act_if(share_goes(kind, m), share(kind, m), "start")

    def arrive(kinds, m, condition=True):
        for kind in kinds:
            act_if(there(kind, m) & condition(kind), hop(kind, m), "wait_recv")
            if m < steps:
                act_if(hop_goes(kind, m) & condition(kind), hop(kind, m), "wait_send")
                act_if(hop_goes(kind, m + 1) & condition(kind), hop(kind, m + 1), "start")

    w_rows = w_ref.shape[0]

    def w_copy(m):
        return move(
            w_all.at[group, rank], w_all.at[group, rank], w_send.at[m - 1], w_recv.at[m - 1],
            lax.rem(me + m * size, n), my_head,
        )

    def w_in(m):
        source = lax.rem(group + groups - m, groups)
        return move(
            w_all.at[source, rank], w_all.at[source, rank], w_send.at[m - 1], w_recv.at[m - 1],
            me, partner,
        )

    def w_spread(j):
        return move(
            w_all.at[:, rank], w_all.at[:, rank], w_pass.at[j - 1], w_taken.at[j - 1],
            first + lax.rem(rank + j, size), my_head,
        )

    def w_spread_in(j):
        source = lax.rem(rank + size - j, size)
        return move(
            w_all.at[:, source], w_all.at[:, source], w_pass.at[j - 1], w_taken.at[j - 1],
            me, partner,
        )

    def ab_copy(h):
        return move(
            ab_send_buf.at[h], ab_buf.at[rank], ab_send.at[h], ab_recv.at[rank],
            first + heads * core + h, my_head,
        )

    def ab_in(j):
        source = lax.rem(rank + j, size)
        return move(
            ab_buf.at[source], ab_buf.at[source], ab_send.at[0], ab_recv.at[source], me, partner
        )

    def whole_copy():
        return move(whole_out, whole_in, o_send, o_recv, lax.rem(me + n - size, n), my_head)

    def carry_copy():
        return move(
            carry_out, carry_in, c_send, c_recv, lax.rem(me + 2 * n - 2 * size, n), my_head
        )

    def adj_copy(j):
        target = lax.rem(rank + j, size)
        return move(
            adj_out.at[target], adj_in.at[place], sems.at[j - 1], j_recv.at[place],
            first + target, my_head,
        )

    def adj_arrival(h):
        return move(adj_in.at[h], adj_in.at[h], sems.at[0], j_recv.at[h], me, partner)

    def back_rank(block):
        return core * heads + block

    def part_of(item):
        return slice(0, 1) if item == 0 else slice(1, 3)

    def back_copy(block, item):
        return move(
            grad_out.at[part_of(item), block], grad_in.at[place, part_of(item)],
            sems.at[size + 2 * block + item], t_recv.at[place, item],
            first + back_rank(block), pair + half,
        )

    def back_here(block, item):
        return pltpu.make_async_copy(
            grad_out.at[part_of(item), block], grad_in.at[place, part_of(item)],
            t_recv.at[place, item],
        )

    def back_in(h, item):
        refs = grad_in.at[h, part_of(item)]
        return move(refs, refs, sems.at[size], t_recv.at[h, item], me, partner)

    row_ids = lax.broadcasted_iota(jnp.int32, (total, total), 0)
    col_ids = lax.broadcasted_iota(jnp.int32, (total, total), 1)
    shift = BLOCK.bit_length() - 1
    same = lax.shift_right_logical(row_ids, shift) == lax.shift_right_logical(col_ids, shift)
    eye = row_ids == col_ids
    causal = same & (row_ids >= col_ids)
    strict = same & (row_ids > col_ids)

    def to_column(row):
        return row_sum(jnp.where(eye, row, 0.0))

    def to_row(column):
        return column_sum(jnp.where(eye, column, 0.0))

    def flat_row(ref):
        return jnp.concatenate([ref[h : h + 1, :] for h in range(heads)], axis=1)

    decay_row = flat_row(decay_ref)
    decay_col = to_column(decay_row)
    beta = to_column(flat_row(beta_ref))
    summed = row_sum(jnp.where(causal, decay_row, 0.0))
    summed_row = column_sum(jnp.where(same & (row_ids <= col_ids), decay_col, 0.0))
    whole = row_sum(jnp.where(same, decay_row, 0.0))
    growth = jnp.exp(summed)
    tail = jnp.exp(row_sum(jnp.where(same & (row_ids < col_ids), decay_row, 0.0)))
    end_growth = jnp.exp(whole)
    raw_q = stack_heads(gq_ref[...], heads).astype(F32)
    raw_k = stack_heads(gk_ref[...], heads).astype(F32)
    values = stack_heads(gv_ref[...], heads).astype(F32)
    out_grad = stack_heads(gdo_ref[...], heads).astype(F32)
    inv_q = lax.rsqrt(row_sum(raw_q * raw_q) + EPS)
    inv_k = lax.rsqrt(row_sum(raw_k * raw_k) + EPS)
    unit_q = raw_q * inv_q * scaling
    unit_k = raw_k * inv_k
    fading = jnp.where(causal, jnp.exp(jnp.where(causal, summed - summed_row, 0.0)), 0.0)
    products = mm(jnp.concatenate([unit_k, unit_q], axis=0), unit_k, NT)
    key_products = products[:total]
    query_products = products[total:]
    strict_fading = jnp.where(strict, fading, 0.0)
    faded_keys = strict_fading * key_products
    lower = beta * faded_keys
    solved = jnp.where(eye, 1.0, 0.0) - lower
    powered = mm(lower, lower)

    states_load.wait()
    for copy in attention_loads:
        copy.wait()
    pl.semaphore_wait(barrier, greeted)
    start_spread((0, 2, 1, 3))
    ones = jnp.ones((8, depth), F32)
    top = lax.broadcasted_iota(jnp.int32, (8, rows), 0) == 0
    for h in range(heads):
        cols = slice(h * depth, (h + 1) * depth)
        product = dout_ref[:, cols].astype(F32) * out_ref[:, cols].astype(F32)
        stat_own[h] = jnp.where(top, lse_ref[h : h + 1, :], mm_full(ones, product, NT))
    start_spread((4,))
    w_all[group, rank, :, :columns] = w_ref[:, 0, :]
    w_all[group, rank, :, columns:] = w_ref[:, 1, :]
    for m in range(1, groups):
        w_copy(m).start()

    for step in range(BLOCK.bit_length() - 2):
        if step < BLOCK.bit_length() - 3:
            both = mm(jnp.concatenate([solved, powered], axis=0), powered)
            solved = solved + both[:total]
            powered = both[total:]
        else:
            solved = solved + mm(solved, powered)
    attention = fading * query_products
    widened = mm(solved, (beta * growth) * unit_k)
    pulled = mm(attention, out_grad, TN)
    tailing = tail * unit_k
    grown_q = growth * unit_q

    def part(matrix, h, b):
        start = h * rows + b * BLOCK
        return matrix[start : start + BLOCK]

    depth_eye = jnp.where(
        lax.broadcasted_iota(jnp.int32, (depth, depth), 0)
        == lax.broadcasted_iota(jnp.int32, (depth, depth), 1),
        1.0,
        0.0,
    )
    for h in range(heads):
        across = None
        for b in reversed(range(blocks)):
            wide = part(widened, h, b)
            right = jnp.concatenate([part(tailing, h, b), part(pulled, h, b)], axis=1)
            product = mm(wide, right, TN)
            carry_map = part(end_growth, h, b)[0:1, :] * depth_eye - product[:, :depth]
            local = mm(part(grown_q, h, b), part(out_grad, h, b), TN) - product[:, depth:]
            map_buf[h, b, :, :depth] = carry_map
            map_buf[h, b, :, depth:] = local
            if across is None:
                across, offset = carry_map, local
            else:
                joined = mm(carry_map, jnp.concatenate([across, offset], axis=1))
                across, offset = joined[:, :depth], joined[:, depth:] + local
        change = jnp.concatenate([across - depth_eye, offset], axis=1).astype(BF16)
        ab_send_buf[h] = change

        @pl.when(heads * core + h == rank)
        def _():
            ab_buf[rank] = change

        act_if(heads * core + h != rank, ab_copy(h), "start")

    for kinds in ((0, 2), (1, 3, 4)):
        take_spread(kinds)
        for kind in kinds:
            pass_on(kind, 0)
    share_all(KEYS + QUERIES, 0)
    for kind in KEYS + QUERIES:
        for h in range(heads):
            act_if(heads * core + h != rank, spread(h, kind), "wait_send")

    key_ids = row_ids
    query_ids = col_ids

    def stat_row(index, which):
        return jnp.concatenate(
            [stat_buf[index, block, which : which + 1, :] for block in range(heads)], axis=1
        )

    def terms(logits, grad_prob, lse, dots, mask):
        shifted = logits * scaling - lse
        if mask is None:
            chances = jnp.exp(shifted)
        else:
            chances = jnp.where(mask, jnp.exp(jnp.where(mask, shifted, 0.0)), 0.0)
        return (chances * (grad_prob - dots)).astype(BF16), chances.astype(BF16)

    own_lse = stat_row(own_qd, 0)
    own_dots = stat_row(own_qd, 1)
    keys = kv_buf[own_kv, 0]
    queries = qd_buf[own_qd, 0]
    grads = qd_buf[own_qd, 1]
    grad_logit, weights = terms(
        dot(keys, queries, NT), dot(kv_buf[own_kv, 1], grads, NT),
        own_lse, own_dots, query_ids >= key_ids,
    )
    dq_acc[...] = dot(grad_logit, keys, TN)
    dk_acc[...] = dot(grad_logit, queries)
    dv_acc[...] = dot(weights, grads)
    lse_column = to_column(own_lse)
    dots_column = to_column(own_dots)

    def attend_keys(d):
        @pl.when(2 * group + core >= d)
        def _():
            keys = kv_buf[d + 1 - core, 0]
            grad_logit, _ = terms(
                dot(qd_buf[own_qd, 0], keys, NT),
                dot(qd_buf[own_qd, 1], kv_buf[d + 1 - core, 1], NT),
                lse_column, dots_column, row_ids < col_ids if d == reach else None,
            )
            dq_acc[...] += dot(grad_logit, keys)

    def attend_queries(d):
        @pl.when(2 * group + core + d < 2 * groups)
        def _():
            queries = qd_buf[d + core, 0]
            grads = qd_buf[d + core, 1]
            grad_logit, weights = terms(
                dot(kv_buf[own_kv, 0], queries, NT), dot(kv_buf[own_kv, 1], grads, NT),
                stat_row(d + core, 0), stat_row(d + core, 1),
                query_ids < key_ids if d == reach else None,
            )
            dk_acc[...] += dot(grad_logit, queries)
            dv_acc[...] += dot(weights, grads)

    def take_shared_keys(d):
        for lane in range(2):
            m = (d + 1 - lane) // 2
            act_if(share_comes(0, m) & (core == lane), share_in(0, m), "wait_recv")

    def take_shared_queries(d):
        for lane in range(2):
            m = (d + lane) // 2
            for kind in (2, 4):
                act_if(share_comes(kind, m) & (core == lane), share_in(kind, m), "wait_recv")

    def attend_shared(d):
        take_shared_keys(d)
        attend_keys(d)
        take_shared_queries(d)
        attend_queries(d)

    pairs = [(h, b) for h in range(heads) for b in range(blocks)]

    def by_parts(make):
        return jnp.concatenate([make(h, b) for h, b in pairs], axis=0)

    reads = [
        mm(jnp.concatenate([part(unit_k, h, b), part(unit_q, h, b)], axis=0), states_ref[b, h])
        for h, b in pairs
    ]
    key_reads = jnp.concatenate([item[:BLOCK] for item in reads], axis=0)
    query_reads = jnp.concatenate([item[BLOCK:] for item in reads], axis=0)
    remainder = values - growth * key_reads
    fresh = mm(solved, beta * remainder)
    faded_grad = fading * mm(out_grad, fresh, NT)
    out_back = by_parts(lambda h, b: mm_once(part(out_grad, h, b), states_ref[b, h], NT))
    unit_q_grad = growth * out_back + mm_once(faded_grad, unit_k)
    faded_back = mm_once(faded_grad, unit_q, TN)

    relays = {kind: hop_goes(kind, 2) for kind in KEYS + QUERIES} if steps > 1 else {}
    if steps > 1:
        arrive((0, 2), 1, lambda kind: relays[kind])

    @pl.when(composer)
    def _():
        joined = None
        for j in range(1, size):
            ab_in(j).wait_recv()
        for r in reversed(range(size)):
            change = ab_buf[r, :, :depth]
            local = ab_buf[r, :, depth:].astype(F32)
            if joined is None:
                joined = jnp.concatenate([change.astype(F32) + depth_eye, local], axis=1)
            else:
                high, low = split(joined)
                joined = joined + (dot(change, high) + dot(change, low))
                joined = jnp.concatenate([joined[:, :depth], joined[:, depth:] + local], axis=1)
            map_hi[r], map_lo[r] = split(joined[:, :depth])
            map_add[r] = joined[:, depth:]

        @pl.when(group > 0)
        def _():
            whole_out[:, :depth] = (joined[:, :depth] - depth_eye).astype(BF16)
            whole_out[:, depth:] = joined[:, depth:].astype(BF16)
            whole_copy().start()

    def carry_step(condition):
        @pl.when(composer & condition)
        def _():
            state_buf = adj_out.at[size - 1]

            @pl.when(group == groups - 1)
            def _():
                state_buf[...] = jnp.zeros_like(carry_in)

            @pl.when(group < groups - 1)
            def _():
                whole_copy().wait_recv()

            @pl.when(group == groups - 2)
            def _():
                state_buf[...] = whole_in[:, depth:]

            @pl.when(group < groups - 2)
            def _():
                carry_copy().wait_recv()
                carried = carry_in[...]
                state_buf[...] = (
                    carried.astype(F32)
                    + (dot(whole_in[:, :depth], carried) + whole_in[:, depth:].astype(F32))
                ).astype(BF16)

            state = state_buf[...]

            def start_of(r):
                return (dot(map_hi[r], state) + dot(map_lo[r], state) + map_add[r]).astype(BF16)

            @pl.when(group > 1)
            def _():
                carry_out[...] = start_of(0)
                carry_copy().start()

            for r in range(size - 1):
                adj_out[r] = start_of(r + 1)
            for j in range(1, size):
                adj_copy(j).start()
            adj_in[place] = adj_out[rank]

    last = groups - 1 - group
    carry_step(last == 0)
    for m in range(1, groups):
        w_in(m).wait_recv()
    for j in range(1, size):
        w_spread(j).start()
    if steps > 1:
        arrive((0, 2), 1, lambda kind: jnp.logical_not(relays[kind]))
    else:
        arrive((0, 2), 1, lambda kind: True)
    arrive((1, 3, 4), 1, lambda kind: True)
    share_all(KEYS + QUERIES, 1)
    attend_keys(2)
    attend_queries(2)
    carry_step(last == 1)
    attend_shared(1)
    carry_step(last == 2)
    for m in range(2, steps + 1):
        arrive((0, 2, 1, 3, 4), m, lambda kind: True)
        share_all(KEYS + QUERIES, m)
    for d in range(3, reach + 1):
        if d % 2:
            take_shared_keys(d)
        attend_keys(d)

    def blocks_of(matrix):
        return matrix.astype(BF16).reshape(heads, rows, depth)

    def send_back(item):
        for block in range(heads):
            act_if(back_rank(block) == rank, back_here(block, item), "start")
            act_if(back_rank(block) != rank, back_copy(block, item), "start")

    grad_out[0] = blocks_of(dq_acc[...] * scaling)
    send_back(0)
    for d in range(3, reach + 1):
        if d % 2:
            take_shared_queries(d)
        attend_queries(d)
    grad_out[1] = blocks_of(dk_acc[...] * scaling)
    grad_out[2] = blocks_of(dv_acc[...])
    send_back(1)
    carry_step(last >= 3)

    for item in range(2):
        for h in range(heads):
            back_in(h, item).wait_recv()
    for h in range(heads):
        dq_out[:, h * depth : (h + 1) * depth] = grad_in[h, 0]
    both_grads = jnp.concatenate(
        [grad_in[h, item] for item in (1, 2) for h in range(heads)], axis=1
    )
    for j in range(1, size):
        w_spread_in(j).wait_recv()
    out_rows = dx_out.shape[0]
    pieces_each = out_rows // (size * w_rows)

    def dx_rows(owner):
        piece = w_all[pl.ds(owner * pieces_each, pieces_each)].reshape(out_rows, 2 * columns)
        return dot(piece, both_grads, NT)

    def dx_copy(j):
        return move(
            dx_send.at[j - 1], dx_recv.at[j - 1], sems.at[size + 2 * heads + j - 1], x_recv.at[j - 1],
            me, lax.rem(my_head + j, head_n),
        )

    for j in range(1, head_n):
        dx_send[j - 1] = dx_rows(lax.rem(my_head + j, head_n))
        dx_copy(j).start()
    result = dx_rows(my_head)
    for h in range(heads):
        act_if(heads * core + h != rank, adj_arrival(h), "wait_recv")
    later = {}
    for h in range(heads):
        adjoint = adj_in[h].astype(F32)
        for b in reversed(range(blocks)):
            later[h, b] = adjoint
            if b > 0:
                adjoint = mm(map_buf[h, b, :, :depth], adjoint) + map_buf[h, b, :, depth:]
    fresh_grad = pulled + by_parts(lambda h, b: mm(part(tailing, h, b), later[h, b]))
    solved_grad = mm(solved, fresh_grad, TN)
    lower_grad = -mm(solved_grad, fresh, NT)
    key_products_grad = beta * strict_fading * lower_grad
    value_grad = beta * solved_grad
    value_back = by_parts(lambda h, b: mm_once(part(value_grad, h, b), states_ref[b, h], NT))
    fresh_back = tail * by_parts(lambda h, b: mm(part(fresh, h, b), later[h, b], NT))
    unit_k_grad = (
        fresh_back
        - growth * value_back
        + faded_back
        + mm_once(key_products_grad, unit_k)
        + mm_once(key_products_grad, unit_k, TN)
    )
    q_grad = scaling * inv_q * (unit_q_grad - raw_q * (inv_q * inv_q * row_sum(unit_q_grad * raw_q)))
    k_grad = inv_k * (unit_k_grad - raw_k * (inv_k * inv_k * row_sum(unit_k_grad * raw_k)))
    for h in range(heads):
        cols = slice(h * depth, (h + 1) * depth)
        own = slice(h * rows, (h + 1) * rows)
        gdq_out[:, cols] = q_grad[own].astype(BF16)
        gdk_out[:, cols] = k_grad[own].astype(BF16)
        gdv_out[:, cols] = value_grad[own].astype(BF16)
    beta_grad = row_sum(solved_grad * remainder) + row_sum(lower_grad * faded_keys)
    exponent = faded_grad * query_products + key_products_grad * key_products
    tail_grad = row_sum(unit_k * fresh_back)
    growth_grad = row_sum(out_grad * query_reads) - row_sum(value_grad * key_reads)
    summed_grad = (
        row_sum(exponent) - to_column(column_sum(exponent)) - tail_grad + growth * growth_grad
    )
    end_grad = end_growth * by_parts(
        lambda h, b: jnp.broadcast_to(
            column_sum(row_sum(later[h, b] * states_ref[b, h])), (BLOCK, 1)
        )
    )
    decay_grad = (
        column_sum(jnp.where(causal, summed_grad, 0.0))
        + column_sum(jnp.where(same, tail_grad, 0.0))
        + to_row(end_grad)
    )
    beta_row = to_row(beta_grad)
    for h in range(heads):
        own = slice(h * rows, (h + 1) * rows)
        gdecay_out[h : h + 1, :] = decay_grad[:, own]
        gbeta_out[h : h + 1, :] = beta_row[:, own]

    for j in range(1, head_n):
        dx_copy(j).wait_recv()
        result = result + dx_recv[j - 1]
    dx_out[...] = result.astype(BF16)

    for kind in KEYS + QUERIES:
        act_if(hop_goes(kind, steps), hop(kind, steps), "wait_send")
        if kind % 2 == 0:
            act_if(share_goes(kind, steps), share(kind, steps), "wait_send")
    for m in range(1, groups):
        w_copy(m).wait_send()
    for j in range(1, size):
        w_spread(j).wait_send()
    for h in range(heads):
        act_if(heads * core + h != rank, ab_copy(h), "wait_send")
    act_if(composer & (group > 0), whole_copy(), "wait_send")
    act_if(composer & (group > 1), carry_copy(), "wait_send")
    for j in range(1, size):
        act_if(composer, adj_copy(j), "wait_send")
    for block in range(heads):
        for item in range(2):
            act_if(back_rank(block) != rank, back_copy(block, item), "wait_send")
    for j in range(1, head_n):
        dx_copy(j).wait_send()


def hand_over(*refs):
    half = (len(refs) - 1) // 2
    sems = refs[-1]
    copies = [
        pltpu.make_async_copy(refs[i], refs[half + i], sems.at[i]) for i in range(half)
    ]
    for copy in copies:
        copy.start()
    for copy in copies:
        copy.wait()


def per_device(n, head_n, *args):
    attn_q, attn_lse, w_kv, states = args[0], args[5], args[6], args[13]
    rows, columns = attn_q.shape
    heads = attn_lse.shape[0]
    depth = columns // heads
    size = 2 * heads
    steps = WINDOW // (size * rows)
    blocks = states.shape[0]
    groups = n // size
    assert head_n % 2 == 0 and n % size == 0 and WINDOW == steps * size * rows
    w_rows = w_kv.shape[0]
    out_rows = n * w_rows // head_n
    dma = pltpu.SemaphoreType.DMA
    vmem = pl.BlockSpec(memory_space=pltpu.VMEM)
    others = max(head_n - 1, 1)
    slots = 2 * (steps + 1)
    span = heads * rows
    results = pl.pallas_call(
        functools.partial(kernel, n, head_n),
        out_shape=(
            pltpu.VMEM((rows, columns), BF16),
            pltpu.VMEM((out_rows, rows), BF16),
            pltpu.VMEM((rows, columns), BF16),
            pltpu.VMEM((rows, columns), BF16),
            pltpu.VMEM((rows, columns), BF16),
            pltpu.VMEM((heads, rows), F32),
            pltpu.VMEM((heads, rows), F32),
        ),
        in_specs=[pl.BlockSpec(memory_space=pl.ANY)] * len(args),
        out_specs=(vmem,) * 7,
        scratch_shapes=[pltpu.VMEM(item.shape, item.dtype) for item in args[3:]] + [
            pltpu.VMEM((slots, 2, span, depth), BF16),
            pltpu.VMEM((slots, 2, span, depth), BF16),
            pltpu.VMEM((slots, heads, 8, rows), F32),
            pltpu.VMEM((heads, 8, rows), F32),
            pltpu.VMEM((groups, size, w_rows, 2 * columns), BF16),
            pltpu.VMEM((heads, depth, 2 * depth), BF16),
            pltpu.VMEM((size, depth, 2 * depth), BF16),
            pltpu.VMEM((size, depth, depth), BF16),
            pltpu.VMEM((size, depth, depth), BF16),
            pltpu.VMEM((size, depth, depth), F32),
            pltpu.VMEM((depth, 2 * depth), BF16),
            pltpu.VMEM((depth, 2 * depth), BF16),
            pltpu.VMEM((depth, depth), BF16),
            pltpu.VMEM((depth, depth), BF16),
            pltpu.VMEM((size, depth, depth), BF16),
            pltpu.VMEM((heads, depth, depth), BF16),
            pltpu.VMEM((3, heads, rows, depth), BF16),
            pltpu.VMEM((heads, 3, rows, depth), BF16),
            pltpu.VMEM((others, out_rows, rows), F32),
            pltpu.VMEM((others, out_rows, rows), F32),
            pltpu.VMEM((span, depth), F32),
            pltpu.VMEM((span, depth), F32),
            pltpu.VMEM((span, depth), F32),
            pltpu.VMEM((heads, blocks, depth, 2 * depth), F32),
            dma((max(5 * heads + 1, size + 2 * heads + others, 11),)), dma((heads, 5)),
            dma((5,)), dma((steps, 5)),
            dma((3,)), dma((steps + 1, 3)),
            dma((groups,)), dma((groups,)), dma((size,)), dma((size,)),
            dma((heads,)), dma((size,)),
            dma, dma, dma, dma,
            dma((heads,)),
            dma((heads, 2)),
            dma((others,)),
        ],
        compiler_params=pltpu.CompilerParams(
            collective_id=0, has_side_effects=True, vmem_limit_bytes=60000000
        ),
        name="layer_backward",
    )(*args)
    results = [pltpu.with_memory_space_constraint(item, pltpu.VMEM) for item in results]
    return pl.pallas_call(
        hand_over,
        out_shape=[jax.ShapeDtypeStruct(item.shape, item.dtype) for item in results],
        in_specs=[vmem] * len(results),
        out_specs=[pl.BlockSpec(memory_space=pl.ANY)] * len(results),
        scratch_shapes=[dma((len(results),))],
        name="hand_over",
    )(*results)


def solution(mesh):
    rows = P("seq", "head")
    gates = P("head", "seq")
    return jax.shard_map(
        functools.partial(per_device, mesh.shape["seq"], mesh.shape["head"]),
        mesh=mesh,
        in_specs=(
            rows, rows, rows, rows, rows, gates, P("seq", None, "head"),
            rows, rows, rows, rows, gates, gates, P("seq", "head", None, None),
        ),
        out_specs=(rows, gates, rows, rows, rows, gates, gates),
        check_vma=False,
    )
```

```python
import functools
import jax
import jax.numpy as jnp
from jax import lax
from jax.experimental import pallas as pl
from jax.experimental.pallas import tpu as pltpu
from jax.sharding import PartitionSpec as P

BLOCK = 64
WINDOW = 1024
EPS = 1e-06
MESH = pl.DeviceIdType.MESH
F32 = jnp.float32
BF16 = jnp.bfloat16

NN = (((1,), (0,)), ((), ()))
NT = (((1,), (1,)), ((), ()))
TN = (((0,), (0,)), ((), ()))


def dot(left, right, dims=NN):
    return lax.dot_general(left, right, dims, preferred_element_type=F32)


def split(matrix):
    high = matrix.astype(BF16)
    return high, (matrix - high.astype(F32)).astype(BF16)


def mm(left, right, dims=NN):
    left_high, left_low = split(left)
    right_high, right_low = split(right)
    return dot(left_high, right_high, dims) + (
        dot(left_high, right_low, dims) + dot(left_low, right_high, dims)
    )


def mm_once(left, right, dims=NN):
    return dot(left.astype(BF16), right.astype(BF16), dims)


def mm_full(left, right, dims=NN):
    return lax.dot_general(
        left, right, dims, precision=lax.Precision.HIGHEST, preferred_element_type=F32
    )


def row_sum(matrix):
    return jnp.sum(matrix, axis=1, keepdims=True)


def column_sum(matrix):
    return jnp.sum(matrix, axis=0, keepdims=True)


def stack_heads(matrix, heads):
    depth = matrix.shape[1] // heads
    return jnp.concatenate([matrix[:, h * depth : (h + 1) * depth] for h in range(heads)], axis=0)


def kernel(
    n,
    head_n,
    q_hbm, k_hbm, v_hbm, out_hbm, dout_hbm, lse_hbm, w_hbm,
    gq_hbm, gk_hbm, gv_hbm, gdo_hbm, decay_hbm, beta_hbm, states_hbm,
    dq_out, dx_out, gdq_out, gdk_out, gdv_out, gdecay_out, gbeta_out,
    out_ref, dout_ref, lse_ref, w_ref,
    gq_ref, gk_ref, gv_ref, gdo_ref, decay_ref, beta_ref, states_ref,
    kv_buf, qd_buf, stat_buf, stat_own, w_all, ab_send_buf, ab_buf,
    map_hi, map_lo, map_add, whole_out, whole_in, carry_in, carry_out, adj_out, adj_in,
    grad_out, grad_in, dx_send, dx_recv, dq_acc, dk_acc, dv_acc, map_buf,
    sems, a_recv, z_send, z_recv, p_send, p_recv,
    w_send, w_recv, w_pass, w_taken, ab_send, ab_recv, o_send, o_recv, c_send, c_recv, j_recv,
    t_recv, x_recv,
):
    me = lax.axis_index("seq")
    my_head = lax.axis_index("head")
    rows, columns = q_hbm.shape
    heads = lse_ref.shape[0]
    depth = columns // heads
    blocks = rows // BLOCK
    total = heads * rows
    size = 2 * heads
    groups = n // size
    steps = WINDOW // (size * rows)
    reach = 2 * steps
    rank = lax.rem(me, size)
    group = lax.div(me, size)
    first = group * size
    core = lax.rem(my_head, 2)
    pair = my_head - core
    partner = pair + 1 - core
    half = lax.div(rank, heads)
    place = lax.rem(rank, heads)
    place_rows = pl.ds(pl.multiple_of(place * rows, rows), rows)
    composer = half == core
    scaling = depth ** (-0.5)

    barrier = pltpu.get_barrier_semaphore()

    def greet(device):
        pl.semaphore_signal(barrier, inc=1, device_id=device, device_id_type=MESH)

    for j in range(1, size):
        peer = first + lax.rem(rank + j, size)
        greet({"seq": peer, "head": my_head})
        greet({"seq": peer, "head": partner})
    for m in range(1, groups):
        greet({"seq": lax.rem(me + m * size, n), "head": my_head})
    for j in range(1, head_n):
        greet({"seq": me, "head": lax.rem(my_head + j, head_n)})
    greeted = 2 * (size - 1) + groups - 1 + head_n - 1

    spare = [ab_send.at[h] for h in range(heads)] + [p_send.at[i] for i in range(3)]
    spare += [z_send.at[i] for i in range(5)] + [o_send]

    def load(source, target, index):
        copy = pltpu.make_async_copy(source, target, spare[index])
        copy.start()
        return copy

    gdn_loads = [
        load(source, target, index)
        for index, (source, target) in enumerate([
            (decay_hbm, decay_ref), (beta_hbm, beta_ref), (gk_hbm, gk_ref), (gq_hbm, gq_ref),
            (gv_hbm, gv_ref), (gdo_hbm, gdo_ref),
        ])
    ]
    attention_loads = [
        load(source, target, len(gdn_loads) + index)
        for index, (source, target) in enumerate([
            (lse_hbm, lse_ref), (dout_hbm, dout_ref), (out_hbm, out_ref), (w_hbm, w_ref),
        ])
    ]
    states_load = load(states_hbm, states_ref, len(spare) - 1)

    def move(source, target, sent, received, seq, head):
        return pltpu.make_async_remote_copy(
            src_ref=source,
            dst_ref=target,
            send_sem=sent,
            recv_sem=received,
            device_id={"seq": seq, "head": head},
            device_id_type=MESH,
        )

    own_kv = 1 - core
    own_qd = core

    def spread_refs(h, kind):
        cols = slice(h * depth, (h + 1) * depth)
        if kind == 4:
            return stat_own.at[h], stat_buf.at[half, place]
        source = (k_hbm, v_hbm, q_hbm, dout_hbm)[kind].at[:, cols]
        if kind < 2:
            return source, kv_buf.at[1 - half, kind, place_rows, :]
        return source, qd_buf.at[half, kind - 2, place_rows, :]

    def spread(h, kind):
        source, target = spread_refs(h, kind)
        return move(
            source, target, sems.at[5 * h + kind], a_recv.at[kind],
            first + heads * core + h, pair + half,
        )

    def spread_here(h, kind):
        source, target = spread_refs(h, kind)
        return pltpu.make_async_copy(source, target, a_recv.at[kind])

    def spread_in(kind):
        target = chunk(kind, slot(kind, 0, core))
        return move(target, target, sems.at[kind], a_recv.at[kind], me, partner)

    def start_spread(kinds):
        for kind in kinds:
            for h in range(heads):
                @pl.when(heads * core + h == rank)
                def _():
                    spread_here(h, kind).start()

                @pl.when(heads * core + h != rank)
                def _():
                    spread(h, kind).start()

    def take_spread(kinds):
        for kind in kinds:
            spread_in(kind).wait_recv()

    def chunk(kind, index):
        if kind == 4:
            return stat_buf.at[index]
        if kind < 2:
            return kv_buf.at[index, kind]
        return qd_buf.at[index, kind - 2]

    def slot(kind, m, lane):
        return 2 * m + 1 - lane if kind < 2 else 2 * m + lane

    def hop(kind, m):
        return move(
            chunk(kind, slot(kind, m - 1, core)), chunk(kind, slot(kind, m, core)),
            z_send.at[kind], z_recv.at[m - 1, kind],
            lax.rem(me + (size if kind < 2 else n - size), n), my_head,
        )

    def hop_goes(kind, m):
        if kind < 2:
            return (group >= m - 1) & (group + 1 < groups)
        return (group + m - 1 < groups) & (group >= 1)

    def there(kind, m):
        return group >= m if kind < 2 else group + m < groups

    def share_refs(kind, m, lane):
        index = slot(kind, m, lane)
        return kv_buf.at[index] if kind == 0 else qd_buf.at[index] if kind == 2 else stat_buf.at[index]

    def share(kind, m):
        refs = share_refs(kind, m, core)
        return move(refs, refs, p_send.at[kind // 2], p_recv.at[m, kind // 2], me, partner)

    def share_in(kind, m):
        refs = share_refs(kind, m, 1 - core)
        return move(refs, refs, p_send.at[kind // 2], p_recv.at[m, kind // 2], me, partner)

    def share_goes(kind, m):
        near, far = (0, 1) if kind < 2 else (1, 0)
        needed = there(kind, m)
        if m == 0:
            needed = needed & (core == near)
        if m == steps:
            needed = needed & (core == far)
        return needed

    def share_comes(kind, m):
        near, far = (1, 0) if kind < 2 else (0, 1)
        needed = there(kind, m)
        if m == 0:
            needed = needed & (core == near)
        if m == steps:
            needed = needed & (core == far)
        return needed

    KEYS = (0, 1)
    QUERIES = (2, 3, 4)

    def act_if(condition, copy, act):
        @pl.when(condition)
        def _():
            getattr(copy, act)()

    def pass_on(kind, m):
        act_if(hop_goes(kind, m + 1), hop(kind, m + 1), "start")

    def share_all(kinds, m):
        for kind in kinds:
            if kind % 2 == 0:
                if m:
                    act_if(share_goes(kind, m - 1), share(kind, m - 1), "wait_send")
                act_if(share_goes(kind, m), share(kind, m), "start")

    def arrive(kinds, m, condition=True):
        for kind in kinds:
            act_if(there(kind, m) & condition(kind), hop(kind, m), "wait_recv")
            if m < steps:
                act_if(hop_goes(kind, m) & condition(kind), hop(kind, m), "wait_send")
                act_if(hop_goes(kind, m + 1) & condition(kind), hop(kind, m + 1), "start")

    w_rows = w_ref.shape[0]

    def w_copy(m):
        return move(
            w_all.at[group, rank], w_all.at[group, rank], w_send.at[m - 1], w_recv,
            lax.rem(me + m * size, n), my_head,
        )

    def w_in():
        refs = w_all.at[0 : groups - 1, rank]
        return move(refs, refs, w_send.at[0], w_recv, me, partner)

    def w_spread(j):
        return move(
            w_all.at[:, rank], w_all.at[:, rank], w_pass.at[j - 1], w_taken,
            first + lax.rem(rank + j, size), my_head,
        )

    def w_spread_in():
        refs = w_all.at[:, 0 : size - 1]
        return move(refs, refs, w_pass.at[0], w_taken, me, partner)

    def ab_copy(h):
        return move(
            ab_send_buf.at[h], ab_buf.at[rank], ab_send.at[h], ab_recv,
            first + heads * core + h, my_head,
        )

    def ab_in():
        refs = ab_buf.at[0 : size - 1]
        return move(refs, refs, ab_send.at[0], ab_recv, me, partner)

    def whole_copy():
        return move(whole_out, whole_in, o_send, o_recv, lax.rem(me + n - size, n), my_head)

    def carry_copy():
        return move(
            carry_out, carry_in, c_send, c_recv, lax.rem(me + 2 * n - 2 * size, n), my_head
        )

    def adj_copy(j):
        target = lax.rem(rank + j, size)
        return move(
            adj_out.at[target], adj_in.at[place], sems.at[j - 1], j_recv.at[place],
            first + target, my_head,
        )

    def adj_arrival(h):
        return move(adj_in.at[h], adj_in.at[h], sems.at[0], j_recv.at[h], me, partner)

    def back_rank(block):
        return core * heads + block

    def part_of(item):
        return slice(0, 1) if item == 0 else slice(1, 3)

    def back_copy(block, item):
        return move(
            grad_out.at[part_of(item), block], grad_in.at[place, part_of(item)],
            sems.at[size + 2 * block + item], t_recv.at[item],
            first + back_rank(block), pair + half,
        )

    def back_here(block, item):
        return pltpu.make_async_copy(
            grad_out.at[part_of(item), block], grad_in.at[place, part_of(item)],
            t_recv.at[item],
        )

    def back_in(item):
        refs = grad_in.at[:, part_of(item)]
        return move(refs, refs, sems.at[size], t_recv.at[item], me, partner)

    def open_links():
        pl.semaphore_wait(barrier, greeted)
        start_spread((0, 2, 1, 3))

    pl.when(half == 1)(open_links)
    for copy in gdn_loads:
        copy.wait()

    row_ids = lax.broadcasted_iota(jnp.int32, (rows, rows), 0)
    col_ids = lax.broadcasted_iota(jnp.int32, (rows, rows), 1)
    shift = BLOCK.bit_length() - 1
    same = lax.shift_right_logical(row_ids, shift) == lax.shift_right_logical(col_ids, shift)
    eye = row_ids == col_ids
    causal = same & (row_ids >= col_ids)
    strict = same & (row_ids > col_ids)

    def to_column(row):
        return row_sum(jnp.where(eye, row, 0.0))

    def to_row(column):
        return column_sum(jnp.where(eye, column, 0.0))

    def per_head(function, *lists):
        return [function(*items) for items in zip(*lists)]

    def cut(ref):
        return [ref[:, h * depth : (h + 1) * depth].astype(F32) for h in range(heads)]

    decay_row = [decay_ref[h : h + 1, :] for h in range(heads)]
    decay_col = per_head(to_column, decay_row)
    beta = [to_column(beta_ref[h : h + 1, :]) for h in range(heads)]
    summed = [row_sum(jnp.where(causal, row, 0.0)) for row in decay_row]
    summed_row = [column_sum(jnp.where(same & (row_ids <= col_ids), col, 0.0)) for col in decay_col]
    raw_q = cut(gq_ref)
    raw_k = cut(gk_ref)
    inv_q = [lax.rsqrt(row_sum(raw * raw) + EPS) for raw in raw_q]
    inv_k = [lax.rsqrt(row_sum(raw * raw) + EPS) for raw in raw_k]
    unit_q = [raw * inv * scaling for raw, inv in zip(raw_q, inv_q)]
    unit_k = [raw * inv for raw, inv in zip(raw_k, inv_k)]
    fading = per_head(
        lambda col, row: jnp.where(causal, jnp.exp(jnp.where(causal, col - row, 0.0)), 0.0),
        summed, summed_row,
    )
    products = [
        mm(jnp.concatenate([k, q], axis=0), k, NT) for k, q in zip(unit_k, unit_q)
    ]
    key_products = [item[:rows] for item in products]
    query_products = [item[rows:] for item in products]
    strict_fading = [jnp.where(strict, item, 0.0) for item in fading]
    faded_keys = per_head(lambda a, b: a * b, strict_fading, key_products)
    lower = per_head(lambda a, b: a * b, beta, faded_keys)

    def pack(matrix):
        packed = matrix[:BLOCK]
        for b in range(1, blocks):
            packed = packed + matrix[b * BLOCK : (b + 1) * BLOCK]
        return packed

    def unpack(packed):
        return jnp.where(same, jnp.concatenate([packed] * blocks, axis=0), 0.0)

    packed = per_head(pack, lower)
    unit = pack(jnp.where(eye, 1.0, 0.0))
    solved = [unit - item for item in packed]
    powered = per_head(mm, packed, lower)

    pl.when(half == 0)(open_links)
    for copy in attention_loads:
        copy.wait()
    ones = jnp.ones((8, depth), F32)
    top = lax.broadcasted_iota(jnp.int32, (8, rows), 0) == 0
    for h in range(heads):
        cols = slice(h * depth, (h + 1) * depth)
        product = dout_ref[:, cols].astype(F32) * out_ref[:, cols].astype(F32)
        stat_own[h] = jnp.where(top, lse_ref[h : h + 1, :], mm_full(ones, product, NT))
    start_spread((4,))
    w_all[group, rank, :, :columns] = w_ref[:, 0, :]
    w_all[group, rank, :, columns:] = w_ref[:, 1, :]
    for m in range(1, groups):
        w_copy(m).start()

    for step in range(BLOCK.bit_length() - 2):
        wide = per_head(unpack, powered)
        if step < BLOCK.bit_length() - 3:
            both = [
                mm(jnp.concatenate([a, b], axis=0), c) for a, b, c in zip(solved, powered, wide)
            ]
            solved = [a + b[:BLOCK] for a, b in zip(solved, both)]
            powered = [b[BLOCK:] for b in both]
        else:
            solved = [a + mm(a, c) for a, c in zip(solved, wide)]
    solved = per_head(unpack, solved)

    whole = [row_sum(jnp.where(same, row, 0.0)) for row in decay_row]
    growth = per_head(jnp.exp, summed)
    tail = [
        jnp.exp(row_sum(jnp.where(same & (row_ids < col_ids), row, 0.0))) for row in decay_row
    ]
    end_growth = per_head(jnp.exp, whole)
    out_grad = cut(gdo_ref)
    attention = per_head(lambda a, b: a * b, fading, query_products)
    widened = [mm(s, (b * g) * k) for s, b, g, k in zip(solved, beta, growth, unit_k)]
    pulled = per_head(lambda a, o: mm(a, o, TN), attention, out_grad)
    tailing = per_head(lambda a, b: a * b, tail, unit_k)
    grown_q = per_head(lambda a, b: a * b, growth, unit_q)

    def part(matrix, h, b):
        return matrix[h][b * BLOCK : (b + 1) * BLOCK]

    depth_eye = jnp.where(
        lax.broadcasted_iota(jnp.int32, (depth, depth), 0)
        == lax.broadcasted_iota(jnp.int32, (depth, depth), 1),
        1.0,
        0.0,
    )
    ends = []
    for h in range(heads):
        across = None
        for b in reversed(range(blocks)):
            wide = part(widened, h, b)
            right = jnp.concatenate([part(tailing, h, b), part(pulled, h, b)], axis=1)
            product = mm(wide, right, TN)
            carry_map = part(end_growth, h, b)[0:1, :] * depth_eye - product[:, :depth]
            local = mm(part(grown_q, h, b), part(out_grad, h, b), TN) - product[:, depth:]
            map_buf[h, b, :, :depth] = carry_map
            map_buf[h, b, :, depth:] = local
            if across is None:
                across, offset = carry_map, local
            else:
                joined = mm(carry_map, jnp.concatenate([across, offset], axis=1))
                across, offset = joined[:, :depth], joined[:, depth:] + local
        ends.append((across, offset))
    for h in range(heads):
        across, offset = ends[h]
        change = jnp.concatenate([across - depth_eye, offset], axis=1).astype(BF16)
        ab_send_buf[h] = change

        @pl.when(heads * core + h == rank)
        def _():
            ab_buf[rank] = change

        act_if(heads * core + h != rank, ab_copy(h), "start")

    def by_parts(make):
        return [
            jnp.concatenate([make(h, b) for b in range(blocks)], axis=0) for h in range(heads)
        ]

    values = cut(gv_ref)
    states_load.wait()
    reads = [
        [
            mm(jnp.concatenate([part(unit_k, h, b), part(unit_q, h, b)], axis=0), states_ref[b, h])
            for b in range(blocks)
        ]
        for h in range(heads)
    ]
    key_reads = [jnp.concatenate([item[:BLOCK] for item in row], axis=0) for row in reads]
    query_reads = [jnp.concatenate([item[BLOCK:] for item in row], axis=0) for row in reads]
    remainder = [v - g * r for v, g, r in zip(values, growth, key_reads)]
    fresh = [mm(s, b * r) for s, b, r in zip(solved, beta, remainder)]
    faded_grad = [f * mm(o, r, NT) for f, o, r in zip(fading, out_grad, fresh)]
    out_back = by_parts(lambda h, b: mm_once(part(out_grad, h, b), states_ref[b, h], NT))
    unit_q_grad = [
        g * o + mm_once(f, k) for g, o, f, k in zip(growth, out_back, faded_grad, unit_k)
    ]
    faded_back = [mm_once(f, q, TN) for f, q in zip(faded_grad, unit_q)]

    for kinds in ((0, 2), (1, 3, 4)):
        take_spread(kinds)
        for kind in kinds:
            pass_on(kind, 0)
    share_all(KEYS + QUERIES, 0)
    for kind in KEYS + QUERIES:
        for h in range(heads):
            act_if(heads * core + h != rank, spread(h, kind), "wait_send")

    key_ids = lax.broadcasted_iota(jnp.int32, (total, total), 0)
    query_ids = lax.broadcasted_iota(jnp.int32, (total, total), 1)

    def stat_row(index, which):
        return jnp.concatenate(
            [stat_buf[index, block, which : which + 1, :] for block in range(heads)], axis=1
        )

    def terms(logits, grad_prob, lse, dots, mask):
        shifted = logits * scaling - lse
        if mask is None:
            chances = jnp.exp(shifted)
        else:
            chances = jnp.where(mask, jnp.exp(jnp.where(mask, shifted, 0.0)), 0.0)
        return (chances * (grad_prob - dots)).astype(BF16), chances.astype(BF16)

    own_lse = stat_row(own_qd, 0)
    own_dots = stat_row(own_qd, 1)
    keys = kv_buf[own_kv, 0]
    queries = qd_buf[own_qd, 0]
    grads = qd_buf[own_qd, 1]
    grad_logit, weights = terms(
        dot(keys, queries, NT), dot(kv_buf[own_kv, 1], grads, NT),
        own_lse, own_dots, query_ids >= key_ids,
    )
    dq_acc[...] = dot(grad_logit, keys, TN)
    dk_acc[...] = dot(grad_logit, queries)
    dv_acc[...] = dot(weights, grads)

    def stat_column(which):
        return jnp.concatenate(
            [
                to_column(stat_buf[own_qd, block, which : which + 1, :])
                for block in range(heads)
            ],
            axis=0,
        )

    lse_column = stat_column(0)
    dots_column = stat_column(1)

    def attend_keys(d):
        @pl.when(2 * group + core >= d)
        def _():
            keys = kv_buf[d + 1 - core, 0]
            grad_logit, _ = terms(
                dot(qd_buf[own_qd, 0], keys, NT),
                dot(qd_buf[own_qd, 1], kv_buf[d + 1 - core, 1], NT),
                lse_column, dots_column, key_ids < query_ids if d == reach else None,
            )
            dq_acc[...] += dot(grad_logit, keys)

    def attend_queries(d):
        @pl.when(2 * group + core + d < 2 * groups)
        def _():
            queries = qd_buf[d + core, 0]
            grads = qd_buf[d + core, 1]
            grad_logit, weights = terms(
                dot(kv_buf[own_kv, 0], queries, NT), dot(kv_buf[own_kv, 1], grads, NT),
                stat_row(d + core, 0), stat_row(d + core, 1),
                query_ids < key_ids if d == reach else None,
            )
            dk_acc[...] += dot(grad_logit, queries)
            dv_acc[...] += dot(weights, grads)

    def take_shared_keys(d):
        for lane in range(2):
            m = (d + 1 - lane) // 2
            act_if(share_comes(0, m) & (core == lane), share_in(0, m), "wait_recv")

    def take_shared_queries(d):
        for lane in range(2):
            m = (d + lane) // 2
            for kind in (2, 4):
                act_if(share_comes(kind, m) & (core == lane), share_in(kind, m), "wait_recv")

    def attend_shared(d):
        take_shared_keys(d)
        attend_keys(d)
        take_shared_queries(d)
        attend_queries(d)

    relays = {kind: hop_goes(kind, 2) for kind in KEYS + QUERIES} if steps > 1 else {}
    if steps > 1:
        arrive((0, 2), 1, lambda kind: relays[kind])

    @pl.when(composer)
    def _():
        joined = None
        ab_in().wait_recv()
        for r in reversed(range(size)):
            change = ab_buf[r, :, :depth]
            local = ab_buf[r, :, depth:].astype(F32)
            if joined is None:
                joined = jnp.concatenate([change.astype(F32) + depth_eye, local], axis=1)
            else:
                high, low = split(joined)
                joined = joined + (dot(change, high) + dot(change, low))
                joined = jnp.concatenate([joined[:, :depth], joined[:, depth:] + local], axis=1)
            map_hi[r], map_lo[r] = split(joined[:, :depth])
            map_add[r] = joined[:, depth:]

        @pl.when(group > 0)
        def _():
            whole_out[:, :depth] = (joined[:, :depth] - depth_eye).astype(BF16)
            whole_out[:, depth:] = joined[:, depth:].astype(BF16)
            whole_copy().start()

    def carry_step(condition):
        @pl.when(composer & condition)
        def _():
            state_buf = adj_out.at[size - 1]

            @pl.when(group == groups - 1)
            def _():
                state_buf[...] = jnp.zeros_like(carry_in)

            @pl.when(group < groups - 1)
            def _():
                whole_copy().wait_recv()

            @pl.when(group == groups - 2)
            def _():
                state_buf[...] = whole_in[:, depth:]

            @pl.when(group < groups - 2)
            def _():
                carry_copy().wait_recv()
                carried = carry_in[...]
                state_buf[...] = (
                    carried.astype(F32)
                    + (dot(whole_in[:, :depth], carried) + whole_in[:, depth:].astype(F32))
                ).astype(BF16)

            state = state_buf[...]

            def start_of(r):
                return (dot(map_hi[r], state) + dot(map_lo[r], state) + map_add[r]).astype(BF16)

            @pl.when(group > 1)
            def _():
                carry_out[...] = start_of(0)
                carry_copy().start()

            for r in range(size - 1):
                adj_out[r] = start_of(r + 1)
            for j in range(1, size):
                adj_copy(j).start()
            adj_in[place] = adj_out[rank]

    last = groups - 1 - group
    carry_step(last == 0)
    if groups > 1:
        w_in().wait_recv()
    for j in range(1, size):
        w_spread(j).start()
    if steps > 1:
        arrive((0, 2), 1, lambda kind: jnp.logical_not(relays[kind]))
    else:
        arrive((0, 2), 1, lambda kind: True)
    arrive((1, 3, 4), 1, lambda kind: True)
    share_all(KEYS + QUERIES, 1)
    attend_keys(2)
    attend_queries(2)
    carry_step(last == 1)
    attend_shared(1)
    carry_step(last == 2)

    def blocks_of(matrix):
        return matrix.astype(BF16).reshape(heads, rows, depth)

    def send_back(item):
        for block in range(heads):
            act_if(back_rank(block) == rank, back_here(block, item), "start")
            act_if(back_rank(block) != rank, back_copy(block, item), "start")

    def send_queries():
        grad_out[0] = blocks_of(dq_acc[...] * scaling)
        send_back(0)

    pl.when(group == 0)(send_queries)
    for m in range(2, steps + 1):
        arrive((0, 2, 1, 3, 4), m, lambda kind: True)
        share_all(KEYS + QUERIES, m)
    for d in range(3, reach + 1):
        if d % 2:
            take_shared_keys(d)
        attend_keys(d)

    pl.when(group > 0)(send_queries)
    for d in range(3, reach + 1):
        if d % 2:
            take_shared_queries(d)
        attend_queries(d)
    grad_out[1] = blocks_of(dk_acc[...] * scaling)
    grad_out[2] = blocks_of(dv_acc[...])
    send_back(1)
    carry_step(last >= 3)

    for item in range(2):
        back_in(item).wait_recv()
    for h in range(heads):
        dq_out[:, h * depth : (h + 1) * depth] = grad_in[h, 0]
    both_grads = jnp.concatenate(
        [grad_in[h, item] for item in (1, 2) for h in range(heads)], axis=1
    )
    w_spread_in().wait_recv()
    out_rows = dx_out.shape[0]
    pieces_each = out_rows // (size * w_rows)

    def dx_rows(owner):
        piece = w_all[pl.ds(owner * pieces_each, pieces_each)].reshape(out_rows, 2 * columns)
        return dot(piece, both_grads, NT)

    def dx_copy(j):
        return move(
            dx_send.at[j - 1], dx_recv.at[j - 1], sems.at[size + 2 * heads + j - 1], x_recv.at[j - 1],
            me, lax.rem(my_head + j, head_n),
        )

    for j in range(1, head_n):
        dx_send[j - 1] = dx_rows(lax.rem(my_head + j, head_n))
        dx_copy(j).start()
    result = dx_rows(my_head)
    for h in range(heads):
        act_if(heads * core + h != rank, adj_arrival(h), "wait_recv")
    later = {}
    for h in range(heads):
        adjoint = adj_in[h].astype(F32)
        for b in reversed(range(blocks)):
            later[h, b] = adjoint
            if b > 0:
                adjoint = mm(map_buf[h, b, :, :depth], adjoint) + map_buf[h, b, :, depth:]
    moved = by_parts(lambda h, b: mm(part(tailing, h, b), later[h, b]))
    fresh_grad = per_head(lambda a, b: a + b, pulled, moved)
    solved_grad = [mm(s, f, TN) for s, f in zip(solved, fresh_grad)]
    lower_grad = [-mm(s, f, NT) for s, f in zip(solved_grad, fresh)]
    key_products_grad = [b * f * g for b, f, g in zip(beta, strict_fading, lower_grad)]
    value_grad = per_head(lambda a, b: a * b, beta, solved_grad)
    value_back = by_parts(lambda h, b: mm_once(part(value_grad, h, b), states_ref[b, h], NT))
    fresh_moved = by_parts(lambda h, b: mm(part(fresh, h, b), later[h, b], NT))
    fresh_back = per_head(lambda a, b: a * b, tail, fresh_moved)
    for h in range(heads):
        cols = slice(h * depth, (h + 1) * depth)
        unit_k_grad = (
            fresh_back[h]
            - growth[h] * value_back[h]
            + faded_back[h]
            + mm_once(key_products_grad[h], unit_k[h])
            + mm_once(key_products_grad[h], unit_k[h], TN)
        )
        q_share = inv_q[h] * inv_q[h] * row_sum(unit_q_grad[h] * raw_q[h])
        k_share = inv_k[h] * inv_k[h] * row_sum(unit_k_grad * raw_k[h])
        gdq_out[:, cols] = (scaling * inv_q[h] * (unit_q_grad[h] - raw_q[h] * q_share)).astype(BF16)
        gdk_out[:, cols] = (inv_k[h] * (unit_k_grad - raw_k[h] * k_share)).astype(BF16)
        gdv_out[:, cols] = value_grad[h].astype(BF16)
        beta_grad = row_sum(solved_grad[h] * remainder[h]) + row_sum(lower_grad[h] * faded_keys[h])
        exponent = faded_grad[h] * query_products[h] + key_products_grad[h] * key_products[h]
        tail_grad = row_sum(unit_k[h] * fresh_back[h])
        growth_grad = row_sum(out_grad[h] * query_reads[h]) - row_sum(value_grad[h] * key_reads[h])
        summed_grad = (
            row_sum(exponent) - to_column(column_sum(exponent)) - tail_grad + growth[h] * growth_grad
        )
        end_grad = end_growth[h] * jnp.concatenate(
            [
                jnp.broadcast_to(column_sum(row_sum(later[h, b] * states_ref[b, h])), (BLOCK, 1))
                for b in range(blocks)
            ],
            axis=0,
        )
        gdecay_out[h : h + 1, :] = (
            column_sum(jnp.where(causal, summed_grad, 0.0))
            + column_sum(jnp.where(same, tail_grad, 0.0))
            + to_row(end_grad)
        )
        gbeta_out[h : h + 1, :] = to_row(beta_grad)

    for j in range(1, head_n):
        dx_copy(j).wait_recv()
        result = result + dx_recv[j - 1]
    dx_out[...] = result.astype(BF16)

    for kind in KEYS + QUERIES:
        act_if(hop_goes(kind, steps), hop(kind, steps), "wait_send")
        if kind % 2 == 0:
            act_if(share_goes(kind, steps), share(kind, steps), "wait_send")
    for m in range(1, groups):
        w_copy(m).wait_send()
    for j in range(1, size):
        w_spread(j).wait_send()
    for h in range(heads):
        act_if(heads * core + h != rank, ab_copy(h), "wait_send")
    act_if(composer & (group > 0), whole_copy(), "wait_send")
    act_if(composer & (group > 1), carry_copy(), "wait_send")
    for j in range(1, size):
        act_if(composer, adj_copy(j), "wait_send")
    for block in range(heads):
        for item in range(2):
            act_if(back_rank(block) != rank, back_copy(block, item), "wait_send")
    for j in range(1, head_n):
        dx_copy(j).wait_send()


def hand_over(*refs):
    half = (len(refs) - 1) // 2
    sems = refs[-1]
    copies = [
        pltpu.make_async_copy(refs[i], refs[half + i], sems.at[i]) for i in range(half)
    ]
    for copy in copies:
        copy.start()
    for copy in copies:
        copy.wait()


def per_device(n, head_n, *args):
    attn_q, attn_lse, w_kv, states = args[0], args[5], args[6], args[13]
    rows, columns = attn_q.shape
    heads = attn_lse.shape[0]
    depth = columns // heads
    size = 2 * heads
    steps = WINDOW // (size * rows)
    blocks = states.shape[0]
    groups = n // size
    assert head_n % 2 == 0 and n % size == 0 and WINDOW == steps * size * rows
    w_rows = w_kv.shape[0]
    out_rows = n * w_rows // head_n
    dma = pltpu.SemaphoreType.DMA
    vmem = pl.BlockSpec(memory_space=pltpu.VMEM)
    others = max(head_n - 1, 1)
    slots = 2 * (steps + 1)
    span = heads * rows
    results = pl.pallas_call(
        functools.partial(kernel, n, head_n),
        out_shape=(
            pltpu.VMEM((rows, columns), BF16),
            pltpu.VMEM((out_rows, rows), BF16),
            pltpu.VMEM((rows, columns), BF16),
            pltpu.VMEM((rows, columns), BF16),
            pltpu.VMEM((rows, columns), BF16),
            pltpu.VMEM((heads, rows), F32),
            pltpu.VMEM((heads, rows), F32),
        ),
        in_specs=[pl.BlockSpec(memory_space=pl.ANY)] * len(args),
        out_specs=(vmem,) * 7,
        scratch_shapes=[pltpu.VMEM(item.shape, item.dtype) for item in args[3:]] + [
            pltpu.VMEM((slots, 2, span, depth), BF16),
            pltpu.VMEM((slots, 2, span, depth), BF16),
            pltpu.VMEM((slots, heads, 8, rows), F32),
            pltpu.VMEM((heads, 8, rows), F32),
            pltpu.VMEM((groups, size, w_rows, 2 * columns), BF16),
            pltpu.VMEM((heads, depth, 2 * depth), BF16),
            pltpu.VMEM((size, depth, 2 * depth), BF16),
            pltpu.VMEM((size, depth, depth), BF16),
            pltpu.VMEM((size, depth, depth), BF16),
            pltpu.VMEM((size, depth, depth), F32),
            pltpu.VMEM((depth, 2 * depth), BF16),
            pltpu.VMEM((depth, 2 * depth), BF16),
            pltpu.VMEM((depth, depth), BF16),
            pltpu.VMEM((depth, depth), BF16),
            pltpu.VMEM((size, depth, depth), BF16),
            pltpu.VMEM((heads, depth, depth), BF16),
            pltpu.VMEM((3, heads, rows, depth), BF16),
            pltpu.VMEM((heads, 3, rows, depth), BF16),
            pltpu.VMEM((others, out_rows, rows), F32),
            pltpu.VMEM((others, out_rows, rows), F32),
            pltpu.VMEM((span, depth), F32),
            pltpu.VMEM((span, depth), F32),
            pltpu.VMEM((span, depth), F32),
            pltpu.VMEM((heads, blocks, depth, 2 * depth), F32),
            dma((max(5 * heads, size + 2 * heads + others),)), dma((5,)),
            dma((5,)), dma((steps, 5)),
            dma((3,)), dma((steps + 1, 3)),
            dma((max(groups - 1, 1),)), dma, dma((size - 1,)), dma,
            dma((heads,)), dma,
            dma, dma, dma, dma,
            dma((heads,)),
            dma((2,)),
            dma((others,)),
        ],
        compiler_params=pltpu.CompilerParams(
            collective_id=0, has_side_effects=True, vmem_limit_bytes=60000000
        ),
        name="layer_backward",
    )(*args)
    results = [pltpu.with_memory_space_constraint(item, pltpu.VMEM) for item in results]
    return pl.pallas_call(
        hand_over,
        out_shape=[jax.ShapeDtypeStruct(item.shape, item.dtype) for item in results],
        in_specs=[vmem] * len(results),
        out_specs=[pl.BlockSpec(memory_space=pl.ANY)] * len(results),
        scratch_shapes=[dma((len(results),))],
        name="hand_over",
    )(*results)


def solution(mesh):
    rows = P("seq", "head")
    gates = P("head", "seq")
    return jax.shard_map(
        functools.partial(per_device, mesh.shape["seq"], mesh.shape["head"]),
        mesh=mesh,
        in_specs=(
            rows, rows, rows, rows, rows, gates, P("seq", None, "head"),
            rows, rows, rows, rows, gates, gates, P("seq", "head", None, None),
        ),
        out_specs=(rows, gates, rows, rows, rows, gates, gates),
        check_vma=False,
    )
```

```python
import functools
import jax
import jax.numpy as jnp
from jax import lax
from jax.experimental import pallas as pl
from jax.experimental.pallas import tpu as pltpu
from jax.sharding import PartitionSpec as P

BLOCK = 64
WINDOW = 1024
EPS = 1e-06
MESH = pl.DeviceIdType.MESH
F32 = jnp.float32
BF16 = jnp.bfloat16

NN = (((1,), (0,)), ((), ()))
NT = (((1,), (1,)), ((), ()))
TN = (((0,), (0,)), ((), ()))


def dot(left, right, dims=NN):
    return lax.dot_general(left, right, dims, preferred_element_type=F32)


def split(matrix):
    high = matrix.astype(BF16)
    return high, (matrix - high.astype(F32)).astype(BF16)


def mm(left, right, dims=NN):
    left_high, left_low = split(left)
    right_high, right_low = split(right)
    return dot(left_high, right_high, dims) + (
        dot(left_high, right_low, dims) + dot(left_low, right_high, dims)
    )


def mm_once(left, right, dims=NN):
    return dot(left.astype(BF16), right.astype(BF16), dims)


def mm_full(left, right, dims=NN):
    return lax.dot_general(
        left, right, dims, precision=lax.Precision.HIGHEST, preferred_element_type=F32
    )


def row_sum(matrix):
    return jnp.sum(matrix, axis=1, keepdims=True)


def column_sum(matrix):
    return jnp.sum(matrix, axis=0, keepdims=True)


def stack_heads(matrix, heads):
    depth = matrix.shape[1] // heads
    return jnp.concatenate([matrix[:, h * depth : (h + 1) * depth] for h in range(heads)], axis=0)


def kernel(
    n,
    head_n,
    q_hbm, k_hbm, v_hbm, out_hbm, dout_hbm, lse_hbm, w_hbm,
    gq_hbm, gk_hbm, gv_hbm, gdo_hbm, decay_hbm, beta_hbm, states_hbm,
    dq_out, dx_out, gdq_out, gdk_out, gdv_out, gdecay_out, gbeta_out,
    out_ref, dout_ref, lse_ref, w_ref,
    gq_ref, gk_ref, gv_ref, gdo_ref, decay_ref, beta_ref, states_ref,
    kv_buf, qd_buf, stat_buf, stat_own, w_all, ab_send_buf, ab_buf,
    map_hi, map_lo, map_add, whole_out, whole_in, carry_in, carry_out, adj_out, adj_in,
    grad_out, grad_in, dx_send, dx_recv, dq_acc, dk_acc, dv_acc, map_buf,
    sems, a_recv, z_send, z_recv, p_send, p_recv,
    w_send, w_recv, w_pass, w_taken, ab_send, ab_recv, o_send, o_recv, c_send, c_recv, j_recv,
    t_recv, x_recv,
):
    me = lax.axis_index("seq")
    my_head = lax.axis_index("head")
    rows, columns = q_hbm.shape
    heads = lse_ref.shape[0]
    depth = columns // heads
    blocks = rows // BLOCK
    total = heads * rows
    size = 2 * heads
    groups = n // size
    steps = WINDOW // (size * rows)
    reach = 2 * steps
    rank = lax.rem(me, size)
    group = lax.div(me, size)
    first = group * size
    core = lax.rem(my_head, 2)
    pair = my_head - core
    partner = pair + 1 - core
    half = lax.div(rank, heads)
    place = lax.rem(rank, heads)
    place_rows = pl.ds(pl.multiple_of(place * rows, rows), rows)
    composer = half == core
    scaling = depth ** (-0.5)

    barrier = pltpu.get_barrier_semaphore()

    def greet(device):
        pl.semaphore_signal(barrier, inc=1, device_id=device, device_id_type=MESH)

    for j in range(1, size):
        peer = first + lax.rem(rank + j, size)
        greet({"seq": peer, "head": my_head})
        greet({"seq": peer, "head": partner})
    for m in range(1, groups):
        greet({"seq": lax.rem(me + m * size, n), "head": my_head})
    for j in range(1, head_n):
        greet({"seq": me, "head": lax.rem(my_head + j, head_n)})
    greeted = 2 * (size - 1) + groups - 1 + head_n - 1

    spare = [ab_send.at[h] for h in range(heads)] + [p_send.at[i] for i in range(3)]
    spare += [z_send.at[i] for i in range(5)] + [o_send]

    def load(source, target, index):
        copy = pltpu.make_async_copy(source, target, spare[index])
        copy.start()
        return copy

    gdn_loads = [
        load(source, target, index)
        for index, (source, target) in enumerate([
            (decay_hbm, decay_ref), (beta_hbm, beta_ref), (gk_hbm, gk_ref), (gq_hbm, gq_ref),
            (gv_hbm, gv_ref), (gdo_hbm, gdo_ref),
        ])
    ]
    attention_loads = [
        load(source, target, len(gdn_loads) + index)
        for index, (source, target) in enumerate([
            (lse_hbm, lse_ref), (dout_hbm, dout_ref), (out_hbm, out_ref), (w_hbm, w_ref),
        ])
    ]
    states_load = load(states_hbm, states_ref, len(spare) - 1)

    def move(source, target, sent, received, seq, head):
        return pltpu.make_async_remote_copy(
            src_ref=source,
            dst_ref=target,
            send_sem=sent,
            recv_sem=received,
            device_id={"seq": seq, "head": head},
            device_id_type=MESH,
        )

    own_kv = 1 - core
    own_qd = core

    def spread_refs(h, kind):
        cols = slice(h * depth, (h + 1) * depth)
        if kind == 4:
            return stat_own.at[h], stat_buf.at[half, place]
        source = (k_hbm, v_hbm, q_hbm, dout_hbm)[kind].at[:, cols]
        if kind < 2:
            return source, kv_buf.at[1 - half, kind, place_rows, :]
        return source, qd_buf.at[half, kind - 2, place_rows, :]

    def spread(h, kind):
        source, target = spread_refs(h, kind)
        return move(
            source, target, sems.at[5 * h + kind], a_recv.at[kind],
            first + heads * core + h, pair + half,
        )

    def spread_here(h, kind):
        source, target = spread_refs(h, kind)
        return pltpu.make_async_copy(source, target, a_recv.at[kind])

    def spread_in(kind):
        target = chunk(kind, slot(kind, 0, core))
        return move(target, target, sems.at[kind], a_recv.at[kind], me, partner)

    def start_spread(kinds):
        for kind in kinds:
            for h in range(heads):
                @pl.when(heads * core + h == rank)
                def _():
                    spread_here(h, kind).start()

                @pl.when(heads * core + h != rank)
                def _():
                    spread(h, kind).start()

    def take_spread(kinds):
        for kind in kinds:
            spread_in(kind).wait_recv()

    def chunk(kind, index):
        if kind == 4:
            return stat_buf.at[index]
        if kind < 2:
            return kv_buf.at[index, kind]
        return qd_buf.at[index, kind - 2]

    def slot(kind, m, lane):
        return 2 * m + 1 - lane if kind < 2 else 2 * m + lane

    def hop(kind, m):
        return move(
            chunk(kind, slot(kind, m - 1, core)), chunk(kind, slot(kind, m, core)),
            z_send.at[kind], z_recv.at[m - 1, kind],
            lax.rem(me + (size if kind < 2 else n - size), n), my_head,
        )

    def hop_goes(kind, m):
        if kind < 2:
            return (group >= m - 1) & (group + 1 < groups)
        return (group + m - 1 < groups) & (group >= 1)

    def there(kind, m):
        return group >= m if kind < 2 else group + m < groups

    def share_refs(kind, m, lane):
        index = slot(kind, m, lane)
        return kv_buf.at[index] if kind == 0 else qd_buf.at[index] if kind == 2 else stat_buf.at[index]

    def share(kind, m):
        refs = share_refs(kind, m, core)
        return move(refs, refs, p_send.at[kind // 2], p_recv.at[m, kind // 2], me, partner)

    def share_in(kind, m):
        refs = share_refs(kind, m, 1 - core)
        return move(refs, refs, p_send.at[kind // 2], p_recv.at[m, kind // 2], me, partner)

    def share_goes(kind, m):
        near, far = (0, 1) if kind < 2 else (1, 0)
        needed = there(kind, m)
        if m == 0:
            needed = needed & (core == near)
        if m == steps:
            needed = needed & (core == far)
        return needed

    def share_comes(kind, m):
        near, far = (1, 0) if kind < 2 else (0, 1)
        needed = there(kind, m)
        if m == 0:
            needed = needed & (core == near)
        if m == steps:
            needed = needed & (core == far)
        return needed

    KEYS = (0, 1)
    QUERIES = (2, 3, 4)

    def act_if(condition, copy, act):
        @pl.when(condition)
        def _():
            getattr(copy, act)()

    def pass_on(kind, m):
        act_if(hop_goes(kind, m + 1), hop(kind, m + 1), "start")

    def share_all(kinds, m):
        for kind in kinds:
            if kind % 2 == 0:
                if m:
                    act_if(share_goes(kind, m - 1), share(kind, m - 1), "wait_send")
                act_if(share_goes(kind, m), share(kind, m), "start")

    def arrive(kinds, m, condition=True):
        for kind in kinds:
            act_if(there(kind, m) & condition(kind), hop(kind, m), "wait_recv")
            if m < steps:
                act_if(hop_goes(kind, m) & condition(kind), hop(kind, m), "wait_send")
                act_if(hop_goes(kind, m + 1) & condition(kind), hop(kind, m + 1), "start")

    w_rows = w_ref.shape[0]

    def w_copy(m):
        return move(
            w_all.at[group, rank], w_all.at[group, rank], w_send.at[m - 1], w_recv,
            lax.rem(me + m * size, n), my_head,
        )

    def w_in():
        refs = w_all.at[0 : groups - 1, rank]
        return move(refs, refs, w_send.at[0], w_recv, me, partner)

    def w_spread(j):
        return move(
            w_all.at[:, rank], w_all.at[:, rank], w_pass.at[j - 1], w_taken,
            first + lax.rem(rank + j, size), my_head,
        )

    def w_spread_in():
        refs = w_all.at[:, 0 : size - 1]
        return move(refs, refs, w_pass.at[0], w_taken, me, partner)

    def ab_copy(h):
        return move(
            ab_send_buf.at[h], ab_buf.at[rank], ab_send.at[h], ab_recv,
            first + heads * core + h, my_head,
        )

    def ab_in():
        refs = ab_buf.at[0 : size - 1]
        return move(refs, refs, ab_send.at[0], ab_recv, me, partner)

    def whole_copy():
        return move(whole_out, whole_in, o_send, o_recv, lax.rem(me + n - size, n), my_head)

    def carry_copy():
        return move(
            carry_out, carry_in, c_send, c_recv, lax.rem(me + 2 * n - 2 * size, n), my_head
        )

    def adj_copy(target):
        return move(
            adj_out.at[target], adj_in.at[place], sems.at[target], j_recv.at[place],
            first + target, my_head,
        )

    def adj_arrival(h):
        return move(adj_in.at[h], adj_in.at[h], sems.at[0], j_recv.at[h], me, partner)

    def back_rank(block):
        return core * heads + block

    def part_of(item):
        return slice(0, 1) if item == 0 else slice(1, 3)

    def back_copy(block, item):
        return move(
            grad_out.at[part_of(item), block], grad_in.at[place, part_of(item)],
            sems.at[size + 2 * block + item], t_recv.at[item],
            first + back_rank(block), pair + half,
        )

    def back_here(block, item):
        return pltpu.make_async_copy(
            grad_out.at[part_of(item), block], grad_in.at[place, part_of(item)],
            t_recv.at[item],
        )

    def back_in(item):
        refs = grad_in.at[:, part_of(item)]
        return move(refs, refs, sems.at[size], t_recv.at[item], me, partner)

    def open_links():
        pl.semaphore_wait(barrier, greeted)
        start_spread((0, 2, 1, 3))

    pl.when(half == 1)(open_links)
    for copy in gdn_loads:
        copy.wait()

    row_ids = lax.broadcasted_iota(jnp.int32, (rows, rows), 0)
    col_ids = lax.broadcasted_iota(jnp.int32, (rows, rows), 1)
    shift = BLOCK.bit_length() - 1
    same = lax.shift_right_logical(row_ids, shift) == lax.shift_right_logical(col_ids, shift)
    eye = row_ids == col_ids
    causal = same & (row_ids >= col_ids)
    strict = same & (row_ids > col_ids)

    def to_column(row):
        return row_sum(jnp.where(eye, row, 0.0))

    def to_row(column):
        return column_sum(jnp.where(eye, column, 0.0))

    def per_head(function, *lists):
        return [function(*items) for items in zip(*lists)]

    def cut(ref):
        return [ref[:, h * depth : (h + 1) * depth].astype(F32) for h in range(heads)]

    decay_row = [decay_ref[h : h + 1, :] for h in range(heads)]
    decay_col = per_head(to_column, decay_row)
    beta = [to_column(beta_ref[h : h + 1, :]) for h in range(heads)]
    summed = [row_sum(jnp.where(causal, row, 0.0)) for row in decay_row]
    summed_row = [column_sum(jnp.where(same & (row_ids <= col_ids), col, 0.0)) for col in decay_col]
    raw_q = cut(gq_ref)
    raw_k = cut(gk_ref)
    inv_q = [lax.rsqrt(row_sum(raw * raw) + EPS) for raw in raw_q]
    inv_k = [lax.rsqrt(row_sum(raw * raw) + EPS) for raw in raw_k]
    unit_q = [raw * inv * scaling for raw, inv in zip(raw_q, inv_q)]
    unit_k = [raw * inv for raw, inv in zip(raw_k, inv_k)]
    fading = per_head(
        lambda col, row: jnp.where(causal, jnp.exp(jnp.where(causal, col - row, 0.0)), 0.0),
        summed, summed_row,
    )
    products = [
        mm(jnp.concatenate([k, q], axis=0), k, NT) for k, q in zip(unit_k, unit_q)
    ]
    key_products = [item[:rows] for item in products]
    query_products = [item[rows:] for item in products]
    strict_fading = [jnp.where(strict, item, 0.0) for item in fading]
    faded_keys = per_head(lambda a, b: a * b, strict_fading, key_products)
    lower = per_head(lambda a, b: a * b, beta, faded_keys)

    def pack(matrix):
        packed = matrix[:BLOCK]
        for b in range(1, blocks):
            packed = packed + matrix[b * BLOCK : (b + 1) * BLOCK]
        return packed

    def unpack(packed):
        return jnp.where(same, jnp.concatenate([packed] * blocks, axis=0), 0.0)

    packed = per_head(pack, lower)
    unit = pack(jnp.where(eye, 1.0, 0.0))
    solved = [unit - item for item in packed]
    powered = per_head(mm, packed, lower)

    pl.when(half == 0)(open_links)
    for copy in attention_loads:
        copy.wait()
    ones = jnp.ones((8, depth), F32)
    top = lax.broadcasted_iota(jnp.int32, (8, rows), 0) == 0
    for h in range(heads):
        cols = slice(h * depth, (h + 1) * depth)
        product = dout_ref[:, cols].astype(F32) * out_ref[:, cols].astype(F32)
        stat_own[h] = jnp.where(top, lse_ref[h : h + 1, :], mm_full(ones, product, NT))
    start_spread((4,))
    w_all[group, rank, :, :columns] = w_ref[:, 0, :]
    w_all[group, rank, :, columns:] = w_ref[:, 1, :]
    for m in range(1, groups):
        w_copy(m).start()

    for step in range(BLOCK.bit_length() - 2):
        wide = per_head(unpack, powered)
        if step < BLOCK.bit_length() - 3:
            both = [
                mm(jnp.concatenate([a, b], axis=0), c) for a, b, c in zip(solved, powered, wide)
            ]
            solved = [a + b[:BLOCK] for a, b in zip(solved, both)]
            powered = [b[BLOCK:] for b in both]
        else:
            solved = [a + mm(a, c) for a, c in zip(solved, wide)]
    solved = per_head(unpack, solved)

    whole = [row_sum(jnp.where(same, row, 0.0)) for row in decay_row]
    growth = per_head(jnp.exp, summed)
    tail = [
        jnp.exp(row_sum(jnp.where(same & (row_ids < col_ids), row, 0.0))) for row in decay_row
    ]
    end_growth = per_head(jnp.exp, whole)
    out_grad = cut(gdo_ref)
    attention = per_head(lambda a, b: a * b, fading, query_products)
    widened = [mm(s, (b * g) * k) for s, b, g, k in zip(solved, beta, growth, unit_k)]
    pulled = per_head(lambda a, o: mm(a, o, TN), attention, out_grad)
    tailing = per_head(lambda a, b: a * b, tail, unit_k)
    grown_q = per_head(lambda a, b: a * b, growth, unit_q)

    def part(matrix, h, b):
        return matrix[h][b * BLOCK : (b + 1) * BLOCK]

    depth_eye = jnp.where(
        lax.broadcasted_iota(jnp.int32, (depth, depth), 0)
        == lax.broadcasted_iota(jnp.int32, (depth, depth), 1),
        1.0,
        0.0,
    )
    ends = []
    for h in range(heads):
        across = None
        for b in reversed(range(blocks)):
            wide = part(widened, h, b)
            right = jnp.concatenate([part(tailing, h, b), part(pulled, h, b)], axis=1)
            product = mm(wide, right, TN)
            carry_map = part(end_growth, h, b)[0:1, :] * depth_eye - product[:, :depth]
            local = mm(part(grown_q, h, b), part(out_grad, h, b), TN) - product[:, depth:]
            map_buf[h, b, :, :depth] = carry_map
            map_buf[h, b, :, depth:] = local
            if across is None:
                across, offset = carry_map, local
            else:
                joined = mm(carry_map, jnp.concatenate([across, offset], axis=1))
                across, offset = joined[:, :depth], joined[:, depth:] + local
        ends.append((across, offset))
    for h in range(heads):
        across, offset = ends[h]
        change = jnp.concatenate([across - depth_eye, offset], axis=1).astype(BF16)
        ab_send_buf[h] = change

        @pl.when(heads * core + h == rank)
        def _():
            ab_buf[rank] = change

        act_if(heads * core + h != rank, ab_copy(h), "start")

    def by_parts(make):
        return [
            jnp.concatenate([make(h, b) for b in range(blocks)], axis=0) for h in range(heads)
        ]

    values = cut(gv_ref)
    states_load.wait()
    reads = [
        [
            mm(jnp.concatenate([part(unit_k, h, b), part(unit_q, h, b)], axis=0), states_ref[b, h])
            for b in range(blocks)
        ]
        for h in range(heads)
    ]
    key_reads = [jnp.concatenate([item[:BLOCK] for item in row], axis=0) for row in reads]
    query_reads = [jnp.concatenate([item[BLOCK:] for item in row], axis=0) for row in reads]
    remainder = [v - g * r for v, g, r in zip(values, growth, key_reads)]
    fresh = [mm(s, b * r) for s, b, r in zip(solved, beta, remainder)]
    faded_grad = [f * mm(o, r, NT) for f, o, r in zip(fading, out_grad, fresh)]
    out_back = by_parts(lambda h, b: mm_once(part(out_grad, h, b), states_ref[b, h], NT))
    unit_q_grad = [
        g * o + mm_once(f, k) for g, o, f, k in zip(growth, out_back, faded_grad, unit_k)
    ]
    faded_back = [mm_once(f, q, TN) for f, q in zip(faded_grad, unit_q)]

    for kinds in ((0, 2), (1, 3, 4)):
        take_spread(kinds)
        for kind in kinds:
            pass_on(kind, 0)
    share_all(KEYS + QUERIES, 0)
    for kind in KEYS + QUERIES:
        for h in range(heads):
            act_if(heads * core + h != rank, spread(h, kind), "wait_send")

    key_ids = lax.broadcasted_iota(jnp.int32, (total, total), 0)
    query_ids = lax.broadcasted_iota(jnp.int32, (total, total), 1)

    def stat_row(index, which):
        return jnp.concatenate(
            [stat_buf[index, block, which : which + 1, :] for block in range(heads)], axis=1
        )

    def terms(logits, grad_prob, lse, dots, mask):
        shifted = logits * scaling - lse
        if mask is None:
            chances = jnp.exp(shifted)
        else:
            chances = jnp.where(mask, jnp.exp(jnp.where(mask, shifted, 0.0)), 0.0)
        return (chances * (grad_prob - dots)).astype(BF16), chances.astype(BF16)

    own_lse = stat_row(own_qd, 0)
    own_dots = stat_row(own_qd, 1)
    keys = kv_buf[own_kv, 0]
    queries = qd_buf[own_qd, 0]
    grads = qd_buf[own_qd, 1]
    grad_logit, weights = terms(
        dot(keys, queries, NT), dot(kv_buf[own_kv, 1], grads, NT),
        own_lse, own_dots, query_ids >= key_ids,
    )
    dq_acc[...] = dot(grad_logit, keys, TN)
    dk_acc[...] = dot(grad_logit, queries)
    dv_acc[...] = dot(weights, grads)

    def stat_column(which):
        return jnp.concatenate(
            [
                to_column(stat_buf[own_qd, block, which : which + 1, :])
                for block in range(heads)
            ],
            axis=0,
        )

    lse_column = stat_column(0)
    dots_column = stat_column(1)

    def attend_keys(d):
        @pl.when(2 * group + core >= d)
        def _():
            keys = kv_buf[d + 1 - core, 0]
            grad_logit, _ = terms(
                dot(qd_buf[own_qd, 0], keys, NT),
                dot(qd_buf[own_qd, 1], kv_buf[d + 1 - core, 1], NT),
                lse_column, dots_column, key_ids < query_ids if d == reach else None,
            )
            dq_acc[...] += dot(grad_logit, keys)

    def attend_queries(d):
        @pl.when(2 * group + core + d < 2 * groups)
        def _():
            queries = qd_buf[d + core, 0]
            grads = qd_buf[d + core, 1]
            grad_logit, weights = terms(
                dot(kv_buf[own_kv, 0], queries, NT), dot(kv_buf[own_kv, 1], grads, NT),
                stat_row(d + core, 0), stat_row(d + core, 1),
                query_ids < key_ids if d == reach else None,
            )
            dk_acc[...] += dot(grad_logit, queries)
            dv_acc[...] += dot(weights, grads)

    def take_shared_keys(d):
        for lane in range(2):
            m = (d + 1 - lane) // 2
            act_if(share_comes(0, m) & (core == lane), share_in(0, m), "wait_recv")

    def take_shared_queries(d):
        for lane in range(2):
            m = (d + lane) // 2
            for kind in (2, 4):
                act_if(share_comes(kind, m) & (core == lane), share_in(kind, m), "wait_recv")

    def attend_shared(d):
        take_shared_keys(d)
        attend_keys(d)
        take_shared_queries(d)
        attend_queries(d)

    relays = {kind: hop_goes(kind, 2) for kind in KEYS + QUERIES} if steps > 1 else {}
    if steps > 1:
        arrive((0, 2), 1, lambda kind: relays[kind])

    @pl.when(composer)
    def _():
        joined = None
        ab_in().wait_recv()
        for r in reversed(range(size)):
            change = ab_buf[r, :, :depth]
            local = ab_buf[r, :, depth:].astype(F32)
            if joined is None:
                joined = jnp.concatenate([change.astype(F32) + depth_eye, local], axis=1)
            else:
                high, low = split(joined)
                joined = joined + (dot(change, high) + dot(change, low))
                joined = jnp.concatenate([joined[:, :depth], joined[:, depth:] + local], axis=1)
            map_hi[r], map_lo[r] = split(joined[:, :depth])
            map_add[r] = joined[:, depth:]

        @pl.when(group > 0)
        def _():
            whole_out[:, :depth] = (joined[:, :depth] - depth_eye).astype(BF16)
            whole_out[:, depth:] = joined[:, depth:].astype(BF16)
            whole_copy().start()

    if groups > 1:
        w_in().wait_recv()
    for j in range(1, size):
        w_spread(j).start()

    def carry_step(condition):
        @pl.when(composer & condition)
        def _():
            state_buf = adj_out.at[size - 1]

            @pl.when(group == groups - 1)
            def _():
                state_buf[...] = jnp.zeros_like(carry_in)

            @pl.when(group < groups - 1)
            def _():
                whole_copy().wait_recv()

            @pl.when(group == groups - 2)
            def _():
                state_buf[...] = whole_in[:, depth:]

            @pl.when(group < groups - 2)
            def _():
                carry_copy().wait_recv()
                carried = carry_in[...]
                state_buf[...] = (
                    carried.astype(F32)
                    + (dot(whole_in[:, :depth], carried) + whole_in[:, depth:].astype(F32))
                ).astype(BF16)

            state = state_buf[...]

            def start_of(r):
                return (dot(map_hi[r], state) + dot(map_lo[r], state) + map_add[r]).astype(BF16)

            @pl.when(group > 1)
            def _():
                carry_out[...] = start_of(0)
                carry_copy().start()

            for r in range(size - 1):
                adj_out[r] = start_of(r + 1)
            for r in range(size):
                act_if(rank != r, adj_copy(r), "start")
            adj_in[place] = adj_out[rank]

    last = groups - 1 - group
    carry_step(last == 0)
    if steps > 1:
        arrive((0, 2), 1, lambda kind: jnp.logical_not(relays[kind]))
    else:
        arrive((0, 2), 1, lambda kind: True)
    arrive((1, 3, 4), 1, lambda kind: True)
    share_all(KEYS + QUERIES, 1)
    attend_keys(2)
    attend_queries(2)
    carry_step(last == 1)
    attend_shared(1)
    carry_step(last == 2)

    def blocks_of(matrix):
        return matrix.astype(BF16).reshape(heads, rows, depth)

    def send_back(item):
        for block in range(heads):
            act_if(back_rank(block) == rank, back_here(block, item), "start")
            act_if(back_rank(block) != rank, back_copy(block, item), "start")

    def send_queries():
        grad_out[0] = blocks_of(dq_acc[...] * scaling)
        send_back(0)

    pl.when(group == 0)(send_queries)
    for m in range(2, steps + 1):
        arrive((0, 2, 1, 3, 4), m, lambda kind: True)
        share_all(KEYS + QUERIES, m)
    for d in range(3, reach + 1):
        if d % 2:
            take_shared_keys(d)
        attend_keys(d)

    pl.when(group > 0)(send_queries)
    for d in range(3, reach + 1):
        if d % 2:
            take_shared_queries(d)
        attend_queries(d)
    grad_out[1] = blocks_of(dk_acc[...] * scaling)
    grad_out[2] = blocks_of(dv_acc[...])
    send_back(1)
    carry_step(last >= 3)

    for item in range(2):
        back_in(item).wait_recv()
    for h in range(heads):
        dq_out[:, h * depth : (h + 1) * depth] = grad_in[h, 0]
    both_grads = jnp.concatenate(
        [grad_in[h, item] for item in (1, 2) for h in range(heads)], axis=1
    )
    w_spread_in().wait_recv()
    out_rows = dx_out.shape[0]
    pieces_each = out_rows // (size * w_rows)

    def dx_rows(owner):
        piece = w_all[pl.ds(owner * pieces_each, pieces_each)].reshape(out_rows, 2 * columns)
        return dot(piece, both_grads, NT)

    def dx_copy(j):
        return move(
            dx_send.at[j - 1], dx_recv.at[j - 1], sems.at[size + 2 * heads + j - 1], x_recv.at[j - 1],
            me, lax.rem(my_head + j, head_n),
        )

    for j in range(1, head_n):
        dx_send[j - 1] = dx_rows(lax.rem(my_head + j, head_n))
        dx_copy(j).start()
    result = dx_rows(my_head)
    for h in range(heads):
        act_if(heads * core + h != rank, adj_arrival(h), "wait_recv")
    later = {}
    for h in range(heads):
        adjoint = adj_in[h].astype(F32)
        for b in reversed(range(blocks)):
            later[h, b] = adjoint
            if b > 0:
                adjoint = mm(map_buf[h, b, :, :depth], adjoint) + map_buf[h, b, :, depth:]
    moved = by_parts(lambda h, b: mm(part(tailing, h, b), later[h, b]))
    fresh_grad = per_head(lambda a, b: a + b, pulled, moved)
    solved_grad = [mm(s, f, TN) for s, f in zip(solved, fresh_grad)]
    lower_grad = [-mm(s, f, NT) for s, f in zip(solved_grad, fresh)]
    key_products_grad = [b * f * g for b, f, g in zip(beta, strict_fading, lower_grad)]
    value_grad = per_head(lambda a, b: a * b, beta, solved_grad)
    value_back = by_parts(lambda h, b: mm_once(part(value_grad, h, b), states_ref[b, h], NT))
    fresh_moved = by_parts(lambda h, b: mm(part(fresh, h, b), later[h, b], NT))
    fresh_back = per_head(lambda a, b: a * b, tail, fresh_moved)
    for h in range(heads):
        cols = slice(h * depth, (h + 1) * depth)
        unit_k_grad = (
            fresh_back[h]
            - growth[h] * value_back[h]
            + faded_back[h]
            + mm_once(key_products_grad[h], unit_k[h])
            + mm_once(key_products_grad[h], unit_k[h], TN)
        )
        q_share = inv_q[h] * inv_q[h] * row_sum(unit_q_grad[h] * raw_q[h])
        k_share = inv_k[h] * inv_k[h] * row_sum(unit_k_grad * raw_k[h])
        gdq_out[:, cols] = (scaling * inv_q[h] * (unit_q_grad[h] - raw_q[h] * q_share)).astype(BF16)
        gdk_out[:, cols] = (inv_k[h] * (unit_k_grad - raw_k[h] * k_share)).astype(BF16)
        gdv_out[:, cols] = value_grad[h].astype(BF16)
        beta_grad = row_sum(solved_grad[h] * remainder[h]) + row_sum(lower_grad[h] * faded_keys[h])
        exponent = faded_grad[h] * query_products[h] + key_products_grad[h] * key_products[h]
        tail_grad = row_sum(unit_k[h] * fresh_back[h])
        growth_grad = row_sum(out_grad[h] * query_reads[h]) - row_sum(value_grad[h] * key_reads[h])
        summed_grad = (
            row_sum(exponent) - to_column(column_sum(exponent)) - tail_grad + growth[h] * growth_grad
        )
        end_grad = end_growth[h] * jnp.concatenate(
            [
                jnp.broadcast_to(column_sum(row_sum(later[h, b] * states_ref[b, h])), (BLOCK, 1))
                for b in range(blocks)
            ],
            axis=0,
        )
        gdecay_out[h : h + 1, :] = (
            column_sum(jnp.where(causal, summed_grad, 0.0))
            + column_sum(jnp.where(same, tail_grad, 0.0))
            + to_row(end_grad)
        )
        gbeta_out[h : h + 1, :] = to_row(beta_grad)

    for j in range(1, head_n):
        dx_copy(j).wait_recv()
        result = result + dx_recv[j - 1]
    dx_out[...] = result.astype(BF16)

    for kind in KEYS + QUERIES:
        act_if(hop_goes(kind, steps), hop(kind, steps), "wait_send")
        if kind % 2 == 0:
            act_if(share_goes(kind, steps), share(kind, steps), "wait_send")
    for m in range(1, groups):
        w_copy(m).wait_send()
    for j in range(1, size):
        w_spread(j).wait_send()
    for h in range(heads):
        act_if(heads * core + h != rank, ab_copy(h), "wait_send")
    act_if(composer & (group > 0), whole_copy(), "wait_send")
    act_if(composer & (group > 1), carry_copy(), "wait_send")
    for r in range(size):
        act_if(composer & (rank != r), adj_copy(r), "wait_send")
    for block in range(heads):
        for item in range(2):
            act_if(back_rank(block) != rank, back_copy(block, item), "wait_send")
    for j in range(1, head_n):
        dx_copy(j).wait_send()


def hand_over(*refs):
    half = (len(refs) - 1) // 2
    sems = refs[-1]
    copies = [
        pltpu.make_async_copy(refs[i], refs[half + i], sems.at[i]) for i in range(half)
    ]
    for copy in copies:
        copy.start()
    for copy in copies:
        copy.wait()


def per_device(n, head_n, *args):
    attn_q, attn_lse, w_kv, states = args[0], args[5], args[6], args[13]
    rows, columns = attn_q.shape
    heads = attn_lse.shape[0]
    depth = columns // heads
    size = 2 * heads
    steps = WINDOW // (size * rows)
    blocks = states.shape[0]
    groups = n // size
    assert head_n % 2 == 0 and n % size == 0 and WINDOW == steps * size * rows
    w_rows = w_kv.shape[0]
    out_rows = n * w_rows // head_n
    dma = pltpu.SemaphoreType.DMA
    vmem = pl.BlockSpec(memory_space=pltpu.VMEM)
    others = max(head_n - 1, 1)
    slots = 2 * (steps + 1)
    span = heads * rows
    results = pl.pallas_call(
        functools.partial(kernel, n, head_n),
        out_shape=(
            pltpu.VMEM((rows, columns), BF16),
            pltpu.VMEM((out_rows, rows), BF16),
            pltpu.VMEM((rows, columns), BF16),
            pltpu.VMEM((rows, columns), BF16),
            pltpu.VMEM((rows, columns), BF16),
            pltpu.VMEM((heads, rows), F32),
            pltpu.VMEM((heads, rows), F32),
        ),
        in_specs=[pl.BlockSpec(memory_space=pl.ANY)] * len(args),
        out_specs=(vmem,) * 7,
        scratch_shapes=[pltpu.VMEM(item.shape, item.dtype) for item in args[3:]] + [
            pltpu.VMEM((slots, 2, span, depth), BF16),
            pltpu.VMEM((slots, 2, span, depth), BF16),
            pltpu.VMEM((slots, heads, 8, rows), F32),
            pltpu.VMEM((heads, 8, rows), F32),
            pltpu.VMEM((groups, size, w_rows, 2 * columns), BF16),
            pltpu.VMEM((heads, depth, 2 * depth), BF16),
            pltpu.VMEM((size, depth, 2 * depth), BF16),
            pltpu.VMEM((size, depth, depth), BF16),
            pltpu.VMEM((size, depth, depth), BF16),
            pltpu.VMEM((size, depth, depth), F32),
            pltpu.VMEM((depth, 2 * depth), BF16),
            pltpu.VMEM((depth, 2 * depth), BF16),
            pltpu.VMEM((depth, depth), BF16),
            pltpu.VMEM((depth, depth), BF16),
            pltpu.VMEM((size, depth, depth), BF16),
            pltpu.VMEM((heads, depth, depth), BF16),
            pltpu.VMEM((3, heads, rows, depth), BF16),
            pltpu.VMEM((heads, 3, rows, depth), BF16),
            pltpu.VMEM((others, out_rows, rows), F32),
            pltpu.VMEM((others, out_rows, rows), F32),
            pltpu.VMEM((span, depth), F32),
            pltpu.VMEM((span, depth), F32),
            pltpu.VMEM((span, depth), F32),
            pltpu.VMEM((heads, blocks, depth, 2 * depth), F32),
            dma((max(5 * heads, size + 2 * heads + others),)), dma((5,)),
            dma((5,)), dma((steps, 5)),
            dma((3,)), dma((steps + 1, 3)),
            dma((max(groups - 1, 1),)), dma, dma((size - 1,)), dma,
            dma((heads,)), dma,
            dma, dma, dma, dma,
            dma((heads,)),
            dma((2,)),
            dma((others,)),
        ],
        compiler_params=pltpu.CompilerParams(
            collective_id=0, has_side_effects=True, vmem_limit_bytes=60000000
        ),
        name="layer_backward",
    )(*args)
    results = [pltpu.with_memory_space_constraint(item, pltpu.VMEM) for item in results]
    return pl.pallas_call(
        hand_over,
        out_shape=[jax.ShapeDtypeStruct(item.shape, item.dtype) for item in results],
        in_specs=[vmem] * len(results),
        out_specs=[pl.BlockSpec(memory_space=pl.ANY)] * len(results),
        scratch_shapes=[dma((len(results),))],
        name="hand_over",
    )(*results)


def solution(mesh):
    rows = P("seq", "head")
    gates = P("head", "seq")
    return jax.shard_map(
        functools.partial(per_device, mesh.shape["seq"], mesh.shape["head"]),
        mesh=mesh,
        in_specs=(
            rows, rows, rows, rows, rows, gates, P("seq", None, "head"),
            rows, rows, rows, rows, gates, gates, P("seq", "head", None, None),
        ),
        out_specs=(rows, gates, rows, rows, rows, gates, gates),
        check_vma=False,
    )
```

```python
import functools
import jax
import jax.numpy as jnp
from jax import lax
from jax.experimental import pallas as pl
from jax.experimental.pallas import tpu as pltpu
from jax.sharding import PartitionSpec as P

BLOCK = 64
WINDOW = 1024
EPS = 1e-06
MESH = pl.DeviceIdType.MESH
F32 = jnp.float32
BF16 = jnp.bfloat16

NN = (((1,), (0,)), ((), ()))
NT = (((1,), (1,)), ((), ()))
TN = (((0,), (0,)), ((), ()))


def dot(left, right, dims=NN):
    return lax.dot_general(left, right, dims, preferred_element_type=F32)


def split(matrix):
    high = matrix.astype(BF16)
    return high, (matrix - high.astype(F32)).astype(BF16)


def mm(left, right, dims=NN):
    left_high, left_low = split(left)
    right_high, right_low = split(right)
    return dot(left_high, right_high, dims) + (
        dot(left_high, right_low, dims) + dot(left_low, right_high, dims)
    )


def mm_once(left, right, dims=NN):
    return dot(left.astype(BF16), right.astype(BF16), dims)


def mm_full(left, right, dims=NN):
    return lax.dot_general(
        left, right, dims, precision=lax.Precision.HIGHEST, preferred_element_type=F32
    )


def row_sum(matrix):
    return jnp.sum(matrix, axis=1, keepdims=True)


def column_sum(matrix):
    return jnp.sum(matrix, axis=0, keepdims=True)


def stack_heads(matrix, heads):
    depth = matrix.shape[1] // heads
    return jnp.concatenate([matrix[:, h * depth : (h + 1) * depth] for h in range(heads)], axis=0)


def kernel(
    n,
    head_n,
    q_hbm, k_hbm, v_hbm, out_hbm, dout_hbm, lse_hbm, w_hbm,
    gq_hbm, gk_hbm, gv_hbm, gdo_hbm, decay_hbm, beta_hbm, states_hbm,
    dq_out, dx_out, gdq_out, gdk_out, gdv_out, gdecay_out, gbeta_out,
    out_ref, dout_ref, lse_ref, w_ref,
    gq_ref, gk_ref, gv_ref, gdo_ref, decay_ref, beta_ref, states_ref,
    kv_buf, qd_buf, stat_buf, stat_own, w_all, ab_send_buf, ab_buf,
    map_hi, map_lo, map_add, whole_out, whole_in, carry_in, carry_out, adj_out, adj_in,
    grad_out, grad_in, dx_send, dx_recv, dq_acc, dk_acc, dv_acc, map_buf,
    sems, a_recv, z_send, z_recv, p_send, p_recv,
    w_send, w_recv, w_pass, w_taken, ab_send, ab_recv, o_send, o_recv, c_send, c_recv, j_recv,
    t_recv, x_recv,
):
    me = lax.axis_index("seq")
    my_head = lax.axis_index("head")
    rows, columns = q_hbm.shape
    heads = lse_ref.shape[0]
    depth = columns // heads
    blocks = rows // BLOCK
    total = heads * rows
    size = 2 * heads
    groups = n // size
    steps = WINDOW // (size * rows)
    reach = 2 * steps
    rank = lax.rem(me, size)
    group = lax.div(me, size)
    first = group * size
    core = lax.rem(my_head, 2)
    pair = my_head - core
    partner = pair + 1 - core
    half = lax.div(rank, heads)
    place = lax.rem(rank, heads)
    place_rows = pl.ds(pl.multiple_of(place * rows, rows), rows)
    composer = half == core
    scaling = depth ** (-0.5)

    barrier = pltpu.get_barrier_semaphore()

    def greet(device):
        pl.semaphore_signal(barrier, inc=1, device_id=device, device_id_type=MESH)

    for j in range(1, size):
        peer = first + lax.rem(rank + j, size)
        greet({"seq": peer, "head": my_head})
        greet({"seq": peer, "head": partner})
    for m in range(1, groups):
        greet({"seq": lax.rem(me + m * size, n), "head": my_head})
    for j in range(1, head_n):
        greet({"seq": me, "head": lax.rem(my_head + j, head_n)})
    greeted = 2 * (size - 1) + groups - 1 + head_n - 1

    spare = [ab_send.at[h] for h in range(heads)] + [p_send.at[i] for i in range(3)]
    spare += [z_send.at[i] for i in range(5)] + [o_send.at[0]]

    def load(source, target, index):
        copy = pltpu.make_async_copy(source, target, spare[index])
        copy.start()
        return copy

    gdn_loads = [
        load(source, target, index)
        for index, (source, target) in enumerate([
            (decay_hbm, decay_ref), (beta_hbm, beta_ref), (gk_hbm, gk_ref), (gq_hbm, gq_ref),
            (gv_hbm, gv_ref), (gdo_hbm, gdo_ref),
        ])
    ]
    attention_loads = [
        load(source, target, len(gdn_loads) + index)
        for index, (source, target) in enumerate([
            (lse_hbm, lse_ref), (dout_hbm, dout_ref), (out_hbm, out_ref), (w_hbm, w_ref),
        ])
    ]
    states_load = load(states_hbm, states_ref, len(spare) - 1)

    def move(source, target, sent, received, seq, head):
        return pltpu.make_async_remote_copy(
            src_ref=source,
            dst_ref=target,
            send_sem=sent,
            recv_sem=received,
            device_id={"seq": seq, "head": head},
            device_id_type=MESH,
        )

    own_kv = 1 - core
    own_qd = core

    def spread_refs(h, kind):
        cols = slice(h * depth, (h + 1) * depth)
        if kind == 4:
            return stat_own.at[h], stat_buf.at[half, place]
        source = (k_hbm, v_hbm, q_hbm, dout_hbm)[kind].at[:, cols]
        if kind < 2:
            return source, kv_buf.at[1 - half, kind, place_rows, :]
        return source, qd_buf.at[half, kind - 2, place_rows, :]

    def spread(h, kind):
        source, target = spread_refs(h, kind)
        return move(
            source, target, sems.at[5 * h + kind], a_recv.at[kind],
            first + heads * core + h, pair + half,
        )

    def spread_here(h, kind):
        source, target = spread_refs(h, kind)
        return pltpu.make_async_copy(source, target, a_recv.at[kind])

    def spread_in(kind):
        target = chunk(kind, slot(kind, 0, core))
        return move(target, target, sems.at[kind], a_recv.at[kind], me, partner)

    def start_spread(kinds):
        for kind in kinds:
            for h in range(heads):
                @pl.when(heads * core + h == rank)
                def _():
                    spread_here(h, kind).start()

                @pl.when(heads * core + h != rank)
                def _():
                    spread(h, kind).start()

    def take_spread(kinds):
        for kind in kinds:
            spread_in(kind).wait_recv()

    def chunk(kind, index):
        if kind == 4:
            return stat_buf.at[index]
        if kind < 2:
            return kv_buf.at[index, kind]
        return qd_buf.at[index, kind - 2]

    def slot(kind, m, lane):
        return 2 * m + 1 - lane if kind < 2 else 2 * m + lane

    def hop(kind, m):
        return move(
            chunk(kind, slot(kind, m - 1, core)), chunk(kind, slot(kind, m, core)),
            z_send.at[kind], z_recv.at[m - 1, kind],
            lax.rem(me + (size if kind < 2 else n - size), n), my_head,
        )

    def hop_goes(kind, m):
        if kind < 2:
            return (group >= m - 1) & (group + 1 < groups)
        return (group + m - 1 < groups) & (group >= 1)

    def there(kind, m):
        return group >= m if kind < 2 else group + m < groups

    def share_refs(kind, m, lane):
        index = slot(kind, m, lane)
        return kv_buf.at[index] if kind == 0 else qd_buf.at[index] if kind == 2 else stat_buf.at[index]

    def share(kind, m):
        refs = share_refs(kind, m, core)
        return move(refs, refs, p_send.at[kind // 2], p_recv.at[m, kind // 2], me, partner)

    def share_in(kind, m):
        refs = share_refs(kind, m, 1 - core)
        return move(refs, refs, p_send.at[kind // 2], p_recv.at[m, kind // 2], me, partner)

    def share_goes(kind, m):
        near, far = (0, 1) if kind < 2 else (1, 0)
        needed = there(kind, m)
        if m == 0:
            needed = needed & (core == near)
        if m == steps:
            needed = needed & (core == far)
        return needed

    def share_comes(kind, m):
        near, far = (1, 0) if kind < 2 else (0, 1)
        needed = there(kind, m)
        if m == 0:
            needed = needed & (core == near)
        if m == steps:
            needed = needed & (core == far)
        return needed

    KEYS = (0, 1)
    QUERIES = (2, 3, 4)

    def act_if(condition, copy, act):
        @pl.when(condition)
        def _():
            getattr(copy, act)()

    def pass_on(kind, m):
        act_if(hop_goes(kind, m + 1), hop(kind, m + 1), "start")

    def share_all(kinds, m):
        for kind in kinds:
            if kind % 2 == 0:
                if m:
                    act_if(share_goes(kind, m - 1), share(kind, m - 1), "wait_send")
                act_if(share_goes(kind, m), share(kind, m), "start")

    def arrive(kinds, m, condition=True):
        for kind in kinds:
            act_if(there(kind, m) & condition(kind), hop(kind, m), "wait_recv")
            if m < steps:
                act_if(hop_goes(kind, m) & condition(kind), hop(kind, m), "wait_send")
                act_if(hop_goes(kind, m + 1) & condition(kind), hop(kind, m + 1), "start")

    w_rows = w_ref.shape[0]

    def w_copy(m):
        return move(
            w_all.at[group, rank], w_all.at[group, rank], w_send.at[m - 1], w_recv,
            lax.rem(me + m * size, n), my_head,
        )

    def w_in():
        refs = w_all.at[0 : groups - 1, rank]
        return move(refs, refs, w_send.at[0], w_recv, me, partner)

    def w_spread(j):
        return move(
            w_all.at[:, rank], w_all.at[:, rank], w_pass.at[j - 1], w_taken,
            first + lax.rem(rank + j, size), my_head,
        )

    def w_spread_in():
        refs = w_all.at[:, 0 : size - 1]
        return move(refs, refs, w_pass.at[0], w_taken, me, partner)

    def ab_copy(h):
        return move(
            ab_send_buf.at[h], ab_buf.at[rank], ab_send.at[h], ab_recv,
            first + heads * core + h, my_head,
        )

    def ab_in():
        refs = ab_buf.at[0 : size - 1]
        return move(refs, refs, ab_send.at[0], ab_recv, me, partner)

    def whole_copy(side):
        return move(
            whole_out.at[side], whole_in.at[side], o_send.at[side], o_recv.at[side],
            lax.rem(me + n - size, n), my_head,
        )

    def carry_copy():
        return move(
            carry_out, carry_in, c_send, c_recv, lax.rem(me + 2 * n - 2 * size, n), my_head
        )

    def adj_copy(target):
        return move(
            adj_out.at[target], adj_in.at[place], sems.at[target], j_recv.at[place],
            first + target, my_head,
        )

    def adj_arrival(h):
        return move(adj_in.at[h], adj_in.at[h], sems.at[0], j_recv.at[h], me, partner)

    def back_rank(block):
        return core * heads + block

    def part_of(item):
        return slice(0, 1) if item == 0 else slice(1, 3)

    def back_copy(block, item):
        return move(
            grad_out.at[part_of(item), block], grad_in.at[place, part_of(item)],
            sems.at[size + 2 * block + item], t_recv.at[item],
            first + back_rank(block), pair + half,
        )

    def back_here(block, item):
        return pltpu.make_async_copy(
            grad_out.at[part_of(item), block], grad_in.at[place, part_of(item)],
            t_recv.at[item],
        )

    def back_in(item):
        refs = grad_in.at[:, part_of(item)]
        return move(refs, refs, sems.at[size], t_recv.at[item], me, partner)

    def open_links():
        pl.semaphore_wait(barrier, greeted)
        start_spread((0, 2, 1, 3))

    pl.when(half == 1)(open_links)
    for copy in gdn_loads:
        copy.wait()

    row_ids = lax.broadcasted_iota(jnp.int32, (rows, rows), 0)
    col_ids = lax.broadcasted_iota(jnp.int32, (rows, rows), 1)
    shift = BLOCK.bit_length() - 1
    same = lax.shift_right_logical(row_ids, shift) == lax.shift_right_logical(col_ids, shift)
    eye = row_ids == col_ids
    causal = same & (row_ids >= col_ids)
    strict = same & (row_ids > col_ids)

    def to_column(row):
        return row_sum(jnp.where(eye, row, 0.0))

    def to_row(column):
        return column_sum(jnp.where(eye, column, 0.0))

    def per_head(function, *lists):
        return [function(*items) for items in zip(*lists)]

    def cut(ref):
        return [ref[:, h * depth : (h + 1) * depth].astype(F32) for h in range(heads)]

    decay_row = [decay_ref[h : h + 1, :] for h in range(heads)]
    decay_col = per_head(to_column, decay_row)
    beta = [to_column(beta_ref[h : h + 1, :]) for h in range(heads)]
    summed = [row_sum(jnp.where(causal, row, 0.0)) for row in decay_row]
    summed_row = [column_sum(jnp.where(same & (row_ids <= col_ids), col, 0.0)) for col in decay_col]
    raw_q = cut(gq_ref)
    raw_k = cut(gk_ref)
    inv_q = [lax.rsqrt(row_sum(raw * raw) + EPS) for raw in raw_q]
    inv_k = [lax.rsqrt(row_sum(raw * raw) + EPS) for raw in raw_k]
    unit_q = [raw * inv * scaling for raw, inv in zip(raw_q, inv_q)]
    unit_k = [raw * inv for raw, inv in zip(raw_k, inv_k)]
    fading = per_head(
        lambda col, row: jnp.where(causal, jnp.exp(jnp.where(causal, col - row, 0.0)), 0.0),
        summed, summed_row,
    )
    products = [
        mm(jnp.concatenate([k, q], axis=0), k, NT) for k, q in zip(unit_k, unit_q)
    ]
    key_products = [item[:rows] for item in products]
    query_products = [item[rows:] for item in products]
    strict_fading = [jnp.where(strict, item, 0.0) for item in fading]
    faded_keys = per_head(lambda a, b: a * b, strict_fading, key_products)
    lower = per_head(lambda a, b: a * b, beta, faded_keys)

    def pack(matrix):
        packed = matrix[:BLOCK]
        for b in range(1, blocks):
            packed = packed + matrix[b * BLOCK : (b + 1) * BLOCK]
        return packed

    def unpack(packed):
        return jnp.where(same, jnp.concatenate([packed] * blocks, axis=0), 0.0)

    packed = per_head(pack, lower)
    unit = pack(jnp.where(eye, 1.0, 0.0))
    solved = [unit - item for item in packed]
    powered = per_head(mm, packed, lower)

    pl.when(half == 0)(open_links)
    for copy in attention_loads:
        copy.wait()
    ones = jnp.ones((8, depth), F32)
    top = lax.broadcasted_iota(jnp.int32, (8, rows), 0) == 0
    for h in range(heads):
        cols = slice(h * depth, (h + 1) * depth)
        product = dout_ref[:, cols].astype(F32) * out_ref[:, cols].astype(F32)
        stat_own[h] = jnp.where(top, lse_ref[h : h + 1, :], mm_full(ones, product, NT))
    start_spread((4,))
    w_all[group, rank, :, :columns] = w_ref[:, 0, :]
    w_all[group, rank, :, columns:] = w_ref[:, 1, :]
    for m in range(1, groups):
        w_copy(m).start()

    for step in range(BLOCK.bit_length() - 2):
        wide = per_head(unpack, powered)
        if step < BLOCK.bit_length() - 3:
            both = [
                mm(jnp.concatenate([a, b], axis=0), c) for a, b, c in zip(solved, powered, wide)
            ]
            solved = [a + b[:BLOCK] for a, b in zip(solved, both)]
            powered = [b[BLOCK:] for b in both]
        else:
            solved = [a + mm(a, c) for a, c in zip(solved, wide)]
    solved = per_head(unpack, solved)

    whole = [row_sum(jnp.where(same, row, 0.0)) for row in decay_row]
    growth = per_head(jnp.exp, summed)
    tail = [
        jnp.exp(row_sum(jnp.where(same & (row_ids < col_ids), row, 0.0))) for row in decay_row
    ]
    end_growth = per_head(jnp.exp, whole)
    out_grad = cut(gdo_ref)
    attention = per_head(lambda a, b: a * b, fading, query_products)
    widened = [mm(s, (b * g) * k) for s, b, g, k in zip(solved, beta, growth, unit_k)]
    pulled = per_head(lambda a, o: mm(a, o, TN), attention, out_grad)
    tailing = per_head(lambda a, b: a * b, tail, unit_k)
    grown_q = per_head(lambda a, b: a * b, growth, unit_q)

    def part(matrix, h, b):
        return matrix[h][b * BLOCK : (b + 1) * BLOCK]

    depth_eye = jnp.where(
        lax.broadcasted_iota(jnp.int32, (depth, depth), 0)
        == lax.broadcasted_iota(jnp.int32, (depth, depth), 1),
        1.0,
        0.0,
    )
    ends = []
    for h in range(heads):
        across = None
        for b in reversed(range(blocks)):
            wide = part(widened, h, b)
            right = jnp.concatenate([part(tailing, h, b), part(pulled, h, b)], axis=1)
            product = mm(wide, right, TN)
            carry_map = part(end_growth, h, b)[0:1, :] * depth_eye - product[:, :depth]
            local = mm(part(grown_q, h, b), part(out_grad, h, b), TN) - product[:, depth:]
            map_buf[h, b, :, :depth] = carry_map
            map_buf[h, b, :, depth:] = local
            if across is None:
                across, offset = carry_map, local
            else:
                joined = mm(carry_map, jnp.concatenate([across, offset], axis=1))
                across, offset = joined[:, :depth], joined[:, depth:] + local
        ends.append((across, offset))
    for h in range(heads):
        across, offset = ends[h]
        change = jnp.concatenate([across - depth_eye, offset], axis=1).astype(BF16)
        ab_send_buf[h] = change

        @pl.when(heads * core + h == rank)
        def _():
            ab_buf[rank] = change

        act_if(heads * core + h != rank, ab_copy(h), "start")

    def by_parts(make):
        return [
            jnp.concatenate([make(h, b) for b in range(blocks)], axis=0) for h in range(heads)
        ]

    values = cut(gv_ref)
    states_load.wait()
    reads = [
        [
            mm(jnp.concatenate([part(unit_k, h, b), part(unit_q, h, b)], axis=0), states_ref[b, h])
            for b in range(blocks)
        ]
        for h in range(heads)
    ]
    key_reads = [jnp.concatenate([item[:BLOCK] for item in row], axis=0) for row in reads]
    query_reads = [jnp.concatenate([item[BLOCK:] for item in row], axis=0) for row in reads]
    remainder = [v - g * r for v, g, r in zip(values, growth, key_reads)]
    fresh = [mm(s, b * r) for s, b, r in zip(solved, beta, remainder)]
    faded_grad = [f * mm(o, r, NT) for f, o, r in zip(fading, out_grad, fresh)]
    out_back = by_parts(lambda h, b: mm_once(part(out_grad, h, b), states_ref[b, h], NT))
    unit_q_grad = [
        g * o + mm_once(f, k) for g, o, f, k in zip(growth, out_back, faded_grad, unit_k)
    ]
    faded_back = [mm_once(f, q, TN) for f, q in zip(faded_grad, unit_q)]

    for kinds in ((0, 2), (1, 3, 4)):
        take_spread(kinds)
        for kind in kinds:
            pass_on(kind, 0)
    share_all(KEYS + QUERIES, 0)
    for kind in KEYS + QUERIES:
        for h in range(heads):
            act_if(heads * core + h != rank, spread(h, kind), "wait_send")

    key_ids = lax.broadcasted_iota(jnp.int32, (total, total), 0)
    query_ids = lax.broadcasted_iota(jnp.int32, (total, total), 1)

    def stat_row(index, which):
        return jnp.concatenate(
            [stat_buf[index, block, which : which + 1, :] for block in range(heads)], axis=1
        )

    def terms(logits, grad_prob, lse, dots, mask):
        shifted = logits * scaling - lse
        if mask is None:
            chances = jnp.exp(shifted)
        else:
            chances = jnp.where(mask, jnp.exp(jnp.where(mask, shifted, 0.0)), 0.0)
        return (chances * (grad_prob - dots)).astype(BF16), chances.astype(BF16)

    own_lse = stat_row(own_qd, 0)
    own_dots = stat_row(own_qd, 1)
    keys = kv_buf[own_kv, 0]
    queries = qd_buf[own_qd, 0]
    grads = qd_buf[own_qd, 1]
    grad_logit, weights = terms(
        dot(keys, queries, NT), dot(kv_buf[own_kv, 1], grads, NT),
        own_lse, own_dots, query_ids >= key_ids,
    )
    dq_acc[...] = dot(grad_logit, keys, TN)
    dk_acc[...] = dot(grad_logit, queries)
    dv_acc[...] = dot(weights, grads)

    def stat_column(which):
        return jnp.concatenate(
            [
                to_column(stat_buf[own_qd, block, which : which + 1, :])
                for block in range(heads)
            ],
            axis=0,
        )

    lse_column = stat_column(0)
    dots_column = stat_column(1)

    def attend_keys(d, lanes=(0, 1)):
        lane_here = (2 * group + core >= d) & ((core == lanes[0]) | (core == lanes[-1]))

        @pl.when(lane_here)
        def _():
            keys = kv_buf[d + 1 - core, 0]
            grad_logit, _ = terms(
                dot(qd_buf[own_qd, 0], keys, NT),
                dot(qd_buf[own_qd, 1], kv_buf[d + 1 - core, 1], NT),
                lse_column, dots_column, key_ids < query_ids if d == reach else None,
            )
            dq_acc[...] += dot(grad_logit, keys)

    def attend_queries(d, lanes=(0, 1)):
        lane_here = (2 * group + core + d < 2 * groups) & (
            (core == lanes[0]) | (core == lanes[-1])
        )

        @pl.when(lane_here)
        def _():
            queries = qd_buf[d + core, 0]
            grads = qd_buf[d + core, 1]
            grad_logit, weights = terms(
                dot(kv_buf[own_kv, 0], queries, NT), dot(kv_buf[own_kv, 1], grads, NT),
                stat_row(d + core, 0), stat_row(d + core, 1),
                query_ids < key_ids if d == reach else None,
            )
            dk_acc[...] += dot(grad_logit, queries)
            dv_acc[...] += dot(weights, grads)

    def take_shared_keys(d, lanes=(0, 1)):
        for lane in lanes:
            m = (d + 1 - lane) // 2
            act_if(share_comes(0, m) & (core == lane), share_in(0, m), "wait_recv")

    def take_shared_queries(d, lanes=(0, 1)):
        for lane in lanes:
            m = (d + lane) // 2
            for kind in (2, 4):
                act_if(share_comes(kind, m) & (core == lane), share_in(kind, m), "wait_recv")

    def attend_shared(d):
        take_shared_keys(d)
        attend_keys(d)
        take_shared_queries(d)
        attend_queries(d)

    relays = {kind: hop_goes(kind, 2) for kind in KEYS + QUERIES} if steps > 1 else {}
    if steps > 1:
        arrive((0, 2), 1, lambda kind: relays[kind])

    @pl.when(composer)
    def _():
        joined = None
        ab_in().wait_recv()
        for r in reversed(range(size)):
            change = ab_buf[r, :, :depth]
            local = ab_buf[r, :, depth:].astype(F32)
            if joined is None:
                joined = jnp.concatenate([change.astype(F32) + depth_eye, local], axis=1)
            else:
                high, low = split(joined)
                joined = joined + (dot(change, high) + dot(change, low))
                joined = jnp.concatenate([joined[:, :depth], joined[:, depth:] + local], axis=1)
            map_hi[r], map_lo[r] = split(joined[:, :depth])
            map_add[r] = joined[:, depth:]

        @pl.when(group > 0)
        def _():
            whole_out[1] = joined[:, depth:].astype(BF16)
            whole_copy(1).start()

        @pl.when((group > 0) & (group < groups - 1))
        def _():
            whole_out[0] = (joined[:, :depth] - depth_eye).astype(BF16)
            whole_copy(0).start()

    if groups > 1:
        w_in().wait_recv()
    for j in range(1, size):
        w_spread(j).start()

    def carry_step(condition):
        @pl.when(composer & condition)
        def _():
            state_buf = adj_out.at[size - 1]

            @pl.when(group == groups - 1)
            def _():
                state_buf[...] = jnp.zeros_like(carry_in)

            @pl.when(group < groups - 1)
            def _():
                whole_copy(1).wait_recv()

            @pl.when(group == groups - 2)
            def _():
                state_buf[...] = whole_in[1]

            @pl.when(group < groups - 2)
            def _():
                whole_copy(0).wait_recv()
                carry_copy().wait_recv()
                carried = carry_in[...]
                state_buf[...] = (
                    carried.astype(F32)
                    + (dot(whole_in[0], carried) + whole_in[1].astype(F32))
                ).astype(BF16)

            state = state_buf[...]

            def start_of(r):
                return (dot(map_hi[r], state) + dot(map_lo[r], state) + map_add[r]).astype(BF16)

            @pl.when(group > 1)
            def _():
                carry_out[...] = start_of(0)
                carry_copy().start()

            for r in range(size):
                if r < size - 1:
                    adj_out[r] = start_of(r + 1)
                act_if(rank != r, adj_copy(r), "start")
            adj_in[place] = adj_out[rank]

    last = groups - 1 - group
    carry_step(last == 0)
    if steps > 1:
        arrive((0, 2), 1, lambda kind: jnp.logical_not(relays[kind]))
    else:
        arrive((0, 2), 1, lambda kind: True)
    arrive((1, 3, 4), 1, lambda kind: True)
    share_all(KEYS + QUERIES, 1)
    attend_keys(2)
    attend_queries(2)
    carry_step(last == 1)
    attend_shared(1)
    carry_step(last == 2)

    def blocks_of(matrix):
        return matrix.astype(BF16).reshape(heads, rows, depth)

    def send_back(item):
        for block in range(heads):
            act_if(back_rank(block) == rank, back_here(block, item), "start")
            act_if(back_rank(block) != rank, back_copy(block, item), "start")

    def send_queries():
        grad_out[0] = blocks_of(dq_acc[...] * scaling)
        send_back(0)

    pl.when(group == 0)(send_queries)
    for m in range(2, steps + 1):
        take_shared_queries(2 * m - 1, (0,))
        attend_queries(2 * m - 1, (0,))
        take_shared_keys(2 * m - 1, (1,))
        attend_keys(2 * m - 1, (1,))
        arrive((0, 2, 1, 3, 4), m, lambda kind: True)
        share_all(KEYS + QUERIES, m)
        attend_keys(2 * m)
        take_shared_keys(2 * m - 1, (0,))
        attend_keys(2 * m - 1, (0,))

    pl.when(group > 0)(send_queries)
    for m in range(2, steps + 1):
        attend_queries(2 * m)
        take_shared_queries(2 * m - 1, (1,))
        attend_queries(2 * m - 1, (1,))
    grad_out[1] = blocks_of(dk_acc[...] * scaling)
    grad_out[2] = blocks_of(dv_acc[...])
    send_back(1)
    carry_step(last >= 3)

    for item in range(2):
        back_in(item).wait_recv()
    for h in range(heads):
        dq_out[:, h * depth : (h + 1) * depth] = grad_in[h, 0]
    both_grads = jnp.concatenate(
        [grad_in[h, item] for item in (1, 2) for h in range(heads)], axis=1
    )
    w_spread_in().wait_recv()
    out_rows = dx_out.shape[0]
    pieces_each = out_rows // (size * w_rows)

    def dx_rows(owner):
        piece = w_all[pl.ds(owner * pieces_each, pieces_each)].reshape(out_rows, 2 * columns)
        return dot(piece, both_grads, NT)

    def dx_copy(j):
        return move(
            dx_send.at[j - 1], dx_recv.at[j - 1], sems.at[size + 2 * heads + j - 1], x_recv.at[j - 1],
            me, lax.rem(my_head + j, head_n),
        )

    for j in range(1, head_n):
        dx_send[j - 1] = dx_rows(lax.rem(my_head + j, head_n))
        dx_copy(j).start()
    result = dx_rows(my_head)
    for h in range(heads):
        act_if(heads * core + h != rank, adj_arrival(h), "wait_recv")
    later = {}
    for h in range(heads):
        adjoint = adj_in[h].astype(F32)
        for b in reversed(range(blocks)):
            later[h, b] = adjoint
            if b > 0:
                adjoint = mm(map_buf[h, b, :, :depth], adjoint) + map_buf[h, b, :, depth:]
    moved = by_parts(lambda h, b: mm(part(tailing, h, b), later[h, b]))
    fresh_grad = per_head(lambda a, b: a + b, pulled, moved)
    solved_grad = [mm(s, f, TN) for s, f in zip(solved, fresh_grad)]
    lower_grad = [-mm(s, f, NT) for s, f in zip(solved_grad, fresh)]
    key_products_grad = [b * f * g for b, f, g in zip(beta, strict_fading, lower_grad)]
    value_grad = per_head(lambda a, b: a * b, beta, solved_grad)
    value_back = by_parts(lambda h, b: mm_once(part(value_grad, h, b), states_ref[b, h], NT))
    fresh_moved = by_parts(lambda h, b: mm(part(fresh, h, b), later[h, b], NT))
    fresh_back = per_head(lambda a, b: a * b, tail, fresh_moved)
    for h in range(heads):
        cols = slice(h * depth, (h + 1) * depth)
        unit_k_grad = (
            fresh_back[h]
            - growth[h] * value_back[h]
            + faded_back[h]
            + mm_once(key_products_grad[h], unit_k[h])
            + mm_once(key_products_grad[h], unit_k[h], TN)
        )
        q_share = inv_q[h] * inv_q[h] * row_sum(unit_q_grad[h] * raw_q[h])
        k_share = inv_k[h] * inv_k[h] * row_sum(unit_k_grad * raw_k[h])
        gdq_out[:, cols] = (scaling * inv_q[h] * (unit_q_grad[h] - raw_q[h] * q_share)).astype(BF16)
        gdk_out[:, cols] = (inv_k[h] * (unit_k_grad - raw_k[h] * k_share)).astype(BF16)
        gdv_out[:, cols] = value_grad[h].astype(BF16)
        beta_grad = row_sum(solved_grad[h] * remainder[h]) + row_sum(lower_grad[h] * faded_keys[h])
        exponent = faded_grad[h] * query_products[h] + key_products_grad[h] * key_products[h]
        tail_grad = row_sum(unit_k[h] * fresh_back[h])
        growth_grad = row_sum(out_grad[h] * query_reads[h]) - row_sum(value_grad[h] * key_reads[h])
        summed_grad = (
            row_sum(exponent) - to_column(column_sum(exponent)) - tail_grad + growth[h] * growth_grad
        )
        end_grad = end_growth[h] * jnp.concatenate(
            [
                jnp.broadcast_to(column_sum(row_sum(later[h, b] * states_ref[b, h])), (BLOCK, 1))
                for b in range(blocks)
            ],
            axis=0,
        )
        gdecay_out[h : h + 1, :] = (
            column_sum(jnp.where(causal, summed_grad, 0.0))
            + column_sum(jnp.where(same, tail_grad, 0.0))
            + to_row(end_grad)
        )
        gbeta_out[h : h + 1, :] = to_row(beta_grad)

    for j in range(1, head_n):
        dx_copy(j).wait_recv()
        result = result + dx_recv[j - 1]
    dx_out[...] = result.astype(BF16)

    for kind in KEYS + QUERIES:
        act_if(hop_goes(kind, steps), hop(kind, steps), "wait_send")
        if kind % 2 == 0:
            act_if(share_goes(kind, steps), share(kind, steps), "wait_send")
    for m in range(1, groups):
        w_copy(m).wait_send()
    for j in range(1, size):
        w_spread(j).wait_send()
    for h in range(heads):
        act_if(heads * core + h != rank, ab_copy(h), "wait_send")
    act_if(composer & (group > 0), whole_copy(1), "wait_send")
    act_if(composer & (group > 0) & (group < groups - 1), whole_copy(0), "wait_send")
    act_if(composer & (group > 1), carry_copy(), "wait_send")
    for r in range(size):
        act_if(composer & (rank != r), adj_copy(r), "wait_send")
    for block in range(heads):
        for item in range(2):
            act_if(back_rank(block) != rank, back_copy(block, item), "wait_send")
    for j in range(1, head_n):
        dx_copy(j).wait_send()


def hand_over(*refs):
    half = (len(refs) - 1) // 2
    sems = refs[-1]
    copies = [
        pltpu.make_async_copy(refs[i], refs[half + i], sems.at[i]) for i in range(half)
    ]
    for copy in copies:
        copy.start()
    for copy in copies:
        copy.wait()


def per_device(n, head_n, *args):
    attn_q, attn_lse, w_kv, states = args[0], args[5], args[6], args[13]
    rows, columns = attn_q.shape
    heads = attn_lse.shape[0]
    depth = columns // heads
    size = 2 * heads
    steps = WINDOW // (size * rows)
    blocks = states.shape[0]
    groups = n // size
    assert head_n % 2 == 0 and n % size == 0 and WINDOW == steps * size * rows
    w_rows = w_kv.shape[0]
    out_rows = n * w_rows // head_n
    dma = pltpu.SemaphoreType.DMA
    vmem = pl.BlockSpec(memory_space=pltpu.VMEM)
    others = max(head_n - 1, 1)
    slots = 2 * (steps + 1)
    span = heads * rows
    results = pl.pallas_call(
        functools.partial(kernel, n, head_n),
        out_shape=(
            pltpu.VMEM((rows, columns), BF16),
            pltpu.VMEM((out_rows, rows), BF16),
            pltpu.VMEM((rows, columns), BF16),
            pltpu.VMEM((rows, columns), BF16),
            pltpu.VMEM((rows, columns), BF16),
            pltpu.VMEM((heads, rows), F32),
            pltpu.VMEM((heads, rows), F32),
        ),
        in_specs=[pl.BlockSpec(memory_space=pl.ANY)] * len(args),
        out_specs=(vmem,) * 7,
        scratch_shapes=[pltpu.VMEM(item.shape, item.dtype) for item in args[3:]] + [
            pltpu.VMEM((slots, 2, span, depth), BF16),
            pltpu.VMEM((slots, 2, span, depth), BF16),
            pltpu.VMEM((slots, heads, 8, rows), F32),
            pltpu.VMEM((heads, 8, rows), F32),
            pltpu.VMEM((groups, size, w_rows, 2 * columns), BF16),
            pltpu.VMEM((heads, depth, 2 * depth), BF16),
            pltpu.VMEM((size, depth, 2 * depth), BF16),
            pltpu.VMEM((size, depth, depth), BF16),
            pltpu.VMEM((size, depth, depth), BF16),
            pltpu.VMEM((size, depth, depth), F32),
            pltpu.VMEM((2, depth, depth), BF16),
            pltpu.VMEM((2, depth, depth), BF16),
            pltpu.VMEM((depth, depth), BF16),
            pltpu.VMEM((depth, depth), BF16),
            pltpu.VMEM((size, depth, depth), BF16),
            pltpu.VMEM((heads, depth, depth), BF16),
            pltpu.VMEM((3, heads, rows, depth), BF16),
            pltpu.VMEM((heads, 3, rows, depth), BF16),
            pltpu.VMEM((others, out_rows, rows), F32),
            pltpu.VMEM((others, out_rows, rows), F32),
            pltpu.VMEM((span, depth), F32),
            pltpu.VMEM((span, depth), F32),
            pltpu.VMEM((span, depth), F32),
            pltpu.VMEM((heads, blocks, depth, 2 * depth), F32),
            dma((max(5 * heads, size + 2 * heads + others),)), dma((5,)),
            dma((5,)), dma((steps, 5)),
            dma((3,)), dma((steps + 1, 3)),
            dma((max(groups - 1, 1),)), dma, dma((size - 1,)), dma,
            dma((heads,)), dma,
            dma((2,)), dma((2,)), dma, dma,
            dma((heads,)),
            dma((2,)),
            dma((others,)),
        ],
        compiler_params=pltpu.CompilerParams(
            collective_id=0, has_side_effects=True, vmem_limit_bytes=60000000
        ),
        name="layer_backward",
    )(*args)
    results = [pltpu.with_memory_space_constraint(item, pltpu.VMEM) for item in results]
    return pl.pallas_call(
        hand_over,
        out_shape=[jax.ShapeDtypeStruct(item.shape, item.dtype) for item in results],
        in_specs=[vmem] * len(results),
        out_specs=[pl.BlockSpec(memory_space=pl.ANY)] * len(results),
        scratch_shapes=[dma((len(results),))],
        name="hand_over",
    )(*results)


def solution(mesh):
    rows = P("seq", "head")
    gates = P("head", "seq")
    return jax.shard_map(
        functools.partial(per_device, mesh.shape["seq"], mesh.shape["head"]),
        mesh=mesh,
        in_specs=(
            rows, rows, rows, rows, rows, gates, P("seq", None, "head"),
            rows, rows, rows, rows, gates, gates, P("seq", "head", None, None),
        ),
        out_specs=(rows, gates, rows, rows, rows, gates, gates),
        check_vma=False,
    )
```

```python
import functools
import jax
import jax.numpy as jnp
from jax import lax
from jax.experimental import pallas as pl
from jax.experimental.pallas import tpu as pltpu
from jax.sharding import PartitionSpec as P

BLOCK = 64
WINDOW = 1024
EPS = 1e-06
MESH = pl.DeviceIdType.MESH
F32 = jnp.float32
BF16 = jnp.bfloat16

NN = (((1,), (0,)), ((), ()))
NT = (((1,), (1,)), ((), ()))
TN = (((0,), (0,)), ((), ()))


def dot(left, right, dims=NN):
    return lax.dot_general(left, right, dims, preferred_element_type=F32)


def split(matrix):
    high = matrix.astype(BF16)
    return high, (matrix - high.astype(F32)).astype(BF16)


def mm(left, right, dims=NN):
    left_high, left_low = split(left)
    right_high, right_low = split(right)
    return dot(left_high, right_high, dims) + (
        dot(left_high, right_low, dims) + dot(left_low, right_high, dims)
    )


def mm_once(left, right, dims=NN):
    return dot(left.astype(BF16), right.astype(BF16), dims)


def mm_full(left, right, dims=NN):
    return lax.dot_general(
        left, right, dims, precision=lax.Precision.HIGHEST, preferred_element_type=F32
    )


def row_sum(matrix):
    return jnp.sum(matrix, axis=1, keepdims=True)


def column_sum(matrix):
    return jnp.sum(matrix, axis=0, keepdims=True)


def stack_heads(matrix, heads):
    depth = matrix.shape[1] // heads
    return jnp.concatenate([matrix[:, h * depth : (h + 1) * depth] for h in range(heads)], axis=0)


def kernel(
    n,
    head_n,
    q_hbm, k_hbm, v_hbm, out_hbm, dout_hbm, lse_hbm, w_hbm,
    gq_hbm, gk_hbm, gv_hbm, gdo_hbm, decay_hbm, beta_hbm, states_hbm,
    dq_out, dx_out, gdq_out, gdk_out, gdv_out, gdecay_out, gbeta_out,
    out_ref, dout_ref, lse_ref, w_ref,
    gq_ref, gk_ref, gv_ref, gdo_ref, decay_ref, beta_ref, states_ref,
    kv_buf, qd_buf, stat_buf, stat_own, w_all, ab_send_buf, ab_buf,
    map_hi, map_lo, map_add, whole_out, whole_in, carry_in, carry_out, adj_out, adj_in,
    grad_out, grad_in, dx_send, dx_recv, dq_acc, dk_acc, dv_acc, map_buf,
    sems, a_recv, z_send, z_recv, p_send, p_recv,
    w_send, w_recv, w_pass, w_taken, ab_send, ab_recv, o_send, o_recv, c_send, c_recv, j_recv,
    t_recv, x_recv,
):
    me = lax.axis_index("seq")
    my_head = lax.axis_index("head")
    rows, columns = q_hbm.shape
    heads = lse_ref.shape[0]
    depth = columns // heads
    blocks = rows // BLOCK
    total = heads * rows
    size = 2 * heads
    groups = n // size
    steps = WINDOW // (size * rows)
    reach = 2 * steps
    rank = lax.rem(me, size)
    group = lax.div(me, size)
    first = group * size
    core = lax.rem(my_head, 2)
    pair = my_head - core
    partner = pair + 1 - core
    half = lax.div(rank, heads)
    place = lax.rem(rank, heads)
    place_rows = pl.ds(pl.multiple_of(place * rows, rows), rows)
    composer = half == core
    scaling = depth ** (-0.5)

    barrier = pltpu.get_barrier_semaphore()

    def greet(device):
        pl.semaphore_signal(barrier, inc=1, device_id=device, device_id_type=MESH)

    for j in range(1, size):
        peer = first + lax.rem(rank + j, size)
        greet({"seq": peer, "head": my_head})
        greet({"seq": peer, "head": partner})
    for m in range(1, groups):
        greet({"seq": lax.rem(me + m * size, n), "head": my_head})
    for j in range(1, head_n):
        greet({"seq": me, "head": lax.rem(my_head + j, head_n)})
    greeted = 2 * (size - 1) + groups - 1 + head_n - 1

    spare = [ab_send.at[h] for h in range(heads)] + [p_send.at[i] for i in range(3)]
    spare += [z_send.at[i] for i in range(5)] + [o_send.at[0]]

    def load(source, target, index):
        copy = pltpu.make_async_copy(source, target, spare[index])
        copy.start()
        return copy

    gdn_loads = [
        load(source, target, index)
        for index, (source, target) in enumerate([
            (decay_hbm, decay_ref), (beta_hbm, beta_ref), (gk_hbm, gk_ref), (gq_hbm, gq_ref),
            (gv_hbm, gv_ref), (gdo_hbm, gdo_ref),
        ])
    ]
    attention_loads = [
        load(source, target, len(gdn_loads) + index)
        for index, (source, target) in enumerate([
            (lse_hbm, lse_ref), (dout_hbm, dout_ref), (out_hbm, out_ref), (w_hbm, w_ref),
        ])
    ]
    states_load = load(states_hbm, states_ref, len(spare) - 1)

    def move(source, target, sent, received, seq, head):
        return pltpu.make_async_remote_copy(
            src_ref=source,
            dst_ref=target,
            send_sem=sent,
            recv_sem=received,
            device_id={"seq": seq, "head": head},
            device_id_type=MESH,
        )

    own_kv = 1 - core
    own_qd = core

    def spread_refs(h, kind):
        cols = slice(h * depth, (h + 1) * depth)
        if kind == 4:
            return stat_own.at[h], stat_buf.at[half, place]
        source = (k_hbm, v_hbm, q_hbm, dout_hbm)[kind].at[:, cols]
        if kind < 2:
            return source, kv_buf.at[1 - half, kind, place_rows, :]
        return source, qd_buf.at[half, kind - 2, place_rows, :]

    def spread(h, kind):
        source, target = spread_refs(h, kind)
        return move(
            source, target, sems.at[5 * h + kind], a_recv.at[kind],
            first + heads * core + h, pair + half,
        )

    def spread_here(h, kind):
        source, target = spread_refs(h, kind)
        return pltpu.make_async_copy(source, target, a_recv.at[kind])

    def spread_in(kind):
        target = chunk(kind, slot(kind, 0, core))
        return move(target, target, sems.at[kind], a_recv.at[kind], me, partner)

    def start_spread(kinds):
        for kind in kinds:
            for h in range(heads):
                @pl.when(heads * core + h == rank)
                def _():
                    spread_here(h, kind).start()

                @pl.when(heads * core + h != rank)
                def _():
                    spread(h, kind).start()

    def take_spread(kinds):
        for kind in kinds:
            spread_in(kind).wait_recv()

    def chunk(kind, index):
        if kind == 4:
            return stat_buf.at[index]
        if kind < 2:
            return kv_buf.at[index, kind]
        return qd_buf.at[index, kind - 2]

    def slot(kind, m, lane):
        return 2 * m + 1 - lane if kind < 2 else 2 * m + lane

    def hop(kind, m):
        return move(
            chunk(kind, slot(kind, m - 1, core)), chunk(kind, slot(kind, m, core)),
            z_send.at[kind], z_recv.at[m - 1, kind],
            lax.rem(me + (size if kind < 2 else n - size), n), my_head,
        )

    def hop_goes(kind, m):
        if kind < 2:
            return (group >= m - 1) & (group + 1 < groups)
        return (group + m - 1 < groups) & (group >= 1)

    def there(kind, m):
        return group >= m if kind < 2 else group + m < groups

    def share_refs(kind, m, lane):
        index = slot(kind, m, lane)
        return kv_buf.at[index] if kind == 0 else qd_buf.at[index] if kind == 2 else stat_buf.at[index]

    def share(kind, m):
        refs = share_refs(kind, m, core)
        return move(refs, refs, p_send.at[kind // 2], p_recv.at[m, kind // 2], me, partner)

    def share_in(kind, m):
        refs = share_refs(kind, m, 1 - core)
        return move(refs, refs, p_send.at[kind // 2], p_recv.at[m, kind // 2], me, partner)

    def share_goes(kind, m):
        near, far = (0, 1) if kind < 2 else (1, 0)
        needed = there(kind, m)
        if m == 0:
            needed = needed & (core == near)
        if m == steps:
            needed = needed & (core == far)
        return needed

    def share_comes(kind, m):
        near, far = (1, 0) if kind < 2 else (0, 1)
        needed = there(kind, m)
        if m == 0:
            needed = needed & (core == near)
        if m == steps:
            needed = needed & (core == far)
        return needed

    KEYS = (0, 1)
    QUERIES = (2, 3, 4)

    def act_if(condition, copy, act):
        @pl.when(condition)
        def _():
            getattr(copy, act)()

    def pass_on(kind, m):
        act_if(hop_goes(kind, m + 1), hop(kind, m + 1), "start")

    def share_all(kinds, m):
        for kind in kinds:
            if kind % 2 == 0:
                if m:
                    act_if(share_goes(kind, m - 1), share(kind, m - 1), "wait_send")
                act_if(share_goes(kind, m), share(kind, m), "start")

    def arrive(kinds, m, condition=True):
        for kind in kinds:
            act_if(there(kind, m) & condition(kind), hop(kind, m), "wait_recv")
            if m < steps:
                act_if(hop_goes(kind, m) & condition(kind), hop(kind, m), "wait_send")
                act_if(hop_goes(kind, m + 1) & condition(kind), hop(kind, m + 1), "start")

    w_rows = w_ref.shape[0]

    def w_copy(m):
        return move(
            w_all.at[group, rank], w_all.at[group, rank], w_send.at[m - 1], w_recv,
            lax.rem(me + m * size, n), my_head,
        )

    def w_in():
        refs = w_all.at[0 : groups - 1, rank]
        return move(refs, refs, w_send.at[0], w_recv, me, partner)

    def w_spread(j):
        return move(
            w_all.at[:, rank], w_all.at[:, rank], w_pass.at[j - 1], w_taken,
            first + lax.rem(rank + j, size), my_head,
        )

    def w_spread_in():
        refs = w_all.at[:, 0 : size - 1]
        return move(refs, refs, w_pass.at[0], w_taken, me, partner)

    def ab_copy(h):
        return move(
            ab_send_buf.at[h], ab_buf.at[rank], ab_send.at[h], ab_recv,
            first + heads * core + h, my_head,
        )

    def ab_in():
        refs = ab_buf.at[0 : size - 1]
        return move(refs, refs, ab_send.at[0], ab_recv, me, partner)

    def whole_copy(side):
        return move(
            whole_out.at[side], whole_in.at[side], o_send.at[side], o_recv.at[side],
            lax.rem(me + n - size, n), my_head,
        )

    def carry_copy():
        return move(
            carry_out, carry_in, c_send, c_recv, lax.rem(me + 2 * n - 2 * size, n), my_head
        )

    def adj_copy(target):
        return move(
            adj_out.at[target], adj_in.at[place], sems.at[target], j_recv.at[place],
            first + target, my_head,
        )

    def adj_arrival(h):
        return move(adj_in.at[h], adj_in.at[h], sems.at[0], j_recv.at[h], me, partner)

    def back_rank(block):
        return core * heads + block

    def part_of(item):
        return slice(0, 1) if item == 0 else slice(1, 3)

    def back_copy(block, item):
        return move(
            grad_out.at[part_of(item), block], grad_in.at[place, part_of(item)],
            sems.at[size + 2 * block + item], t_recv.at[item],
            first + back_rank(block), pair + half,
        )

    def back_here(block, item):
        return pltpu.make_async_copy(
            grad_out.at[part_of(item), block], grad_in.at[place, part_of(item)],
            t_recv.at[item],
        )

    def back_in(item):
        refs = grad_in.at[:, part_of(item)]
        return move(refs, refs, sems.at[size], t_recv.at[item], me, partner)

    def open_links():
        pl.semaphore_wait(barrier, greeted)
        start_spread((0, 2, 1, 3))

    pl.when(half == 1)(open_links)
    for copy in gdn_loads:
        copy.wait()

    row_ids = lax.broadcasted_iota(jnp.int32, (rows, rows), 0)
    col_ids = lax.broadcasted_iota(jnp.int32, (rows, rows), 1)
    shift = BLOCK.bit_length() - 1
    same = lax.shift_right_logical(row_ids, shift) == lax.shift_right_logical(col_ids, shift)
    eye = row_ids == col_ids
    causal = same & (row_ids >= col_ids)
    strict = same & (row_ids > col_ids)

    def to_column(row):
        return row_sum(jnp.where(eye, row, 0.0))

    def to_row(column):
        return column_sum(jnp.where(eye, column, 0.0))

    def per_head(function, *lists):
        return [function(*items) for items in zip(*lists)]

    def cut(ref):
        return [ref[:, h * depth : (h + 1) * depth].astype(F32) for h in range(heads)]

    decay_row = [decay_ref[h : h + 1, :] for h in range(heads)]
    decay_col = per_head(to_column, decay_row)
    beta = [to_column(beta_ref[h : h + 1, :]) for h in range(heads)]
    summed = [row_sum(jnp.where(causal, row, 0.0)) for row in decay_row]
    summed_row = [column_sum(jnp.where(same & (row_ids <= col_ids), col, 0.0)) for col in decay_col]
    raw_q = cut(gq_ref)
    raw_k = cut(gk_ref)
    inv_q = [lax.rsqrt(row_sum(raw * raw) + EPS) for raw in raw_q]
    inv_k = [lax.rsqrt(row_sum(raw * raw) + EPS) for raw in raw_k]
    unit_q = [raw * inv * scaling for raw, inv in zip(raw_q, inv_q)]
    unit_k = [raw * inv for raw, inv in zip(raw_k, inv_k)]
    fading = per_head(
        lambda col, row: jnp.where(causal, jnp.exp(jnp.where(causal, col - row, 0.0)), 0.0),
        summed, summed_row,
    )
    products = [
        mm(jnp.concatenate([k, q], axis=0), k, NT) for k, q in zip(unit_k, unit_q)
    ]
    key_products = [item[:rows] for item in products]
    query_products = [item[rows:] for item in products]
    strict_fading = [jnp.where(strict, item, 0.0) for item in fading]
    faded_keys = per_head(lambda a, b: a * b, strict_fading, key_products)
    lower = per_head(lambda a, b: a * b, beta, faded_keys)

    def pack(matrix):
        packed = matrix[:BLOCK]
        for b in range(1, blocks):
            packed = packed + matrix[b * BLOCK : (b + 1) * BLOCK]
        return packed

    def unpack(packed):
        return jnp.where(same, jnp.concatenate([packed] * blocks, axis=0), 0.0)

    packed = per_head(pack, lower)
    unit = pack(jnp.where(eye, 1.0, 0.0))
    solved = [unit - item for item in packed]
    powered = per_head(mm, packed, lower)

    pl.when(half == 0)(open_links)
    for copy in attention_loads:
        copy.wait()
    ones = jnp.ones((8, depth), F32)
    top = lax.broadcasted_iota(jnp.int32, (8, rows), 0) == 0
    for h in range(heads):
        cols = slice(h * depth, (h + 1) * depth)
        product = dout_ref[:, cols].astype(F32) * out_ref[:, cols].astype(F32)
        stat_own[h] = jnp.where(top, lse_ref[h : h + 1, :], mm_full(ones, product, NT))
    start_spread((4,))
    w_all[group, rank, :, :columns] = w_ref[:, 0, :]
    w_all[group, rank, :, columns:] = w_ref[:, 1, :]
    for m in range(1, groups):
        w_copy(m).start()

    for step in range(BLOCK.bit_length() - 2):
        wide = per_head(unpack, powered)
        if step < BLOCK.bit_length() - 3:
            both = [
                mm(jnp.concatenate([a, b], axis=0), c) for a, b, c in zip(solved, powered, wide)
            ]
            solved = [a + b[:BLOCK] for a, b in zip(solved, both)]
            powered = [b[BLOCK:] for b in both]
        else:
            solved = [a + mm(a, c) for a, c in zip(solved, wide)]
    solved = per_head(unpack, solved)

    whole = [row_sum(jnp.where(same, row, 0.0)) for row in decay_row]
    growth = per_head(jnp.exp, summed)
    tail = [
        jnp.exp(row_sum(jnp.where(same & (row_ids < col_ids), row, 0.0))) for row in decay_row
    ]
    end_growth = per_head(jnp.exp, whole)
    out_grad = cut(gdo_ref)
    attention = per_head(lambda a, b: a * b, fading, query_products)
    widened = [mm(s, (b * g) * k) for s, b, g, k in zip(solved, beta, growth, unit_k)]
    pulled = per_head(lambda a, o: mm(a, o, TN), attention, out_grad)
    tailing = per_head(lambda a, b: a * b, tail, unit_k)
    grown_q = per_head(lambda a, b: a * b, growth, unit_q)

    def part(matrix, h, b):
        return matrix[h][b * BLOCK : (b + 1) * BLOCK]

    depth_eye = jnp.where(
        lax.broadcasted_iota(jnp.int32, (depth, depth), 0)
        == lax.broadcasted_iota(jnp.int32, (depth, depth), 1),
        1.0,
        0.0,
    )
    ends = []
    for h in range(heads):
        across = None
        for b in reversed(range(blocks)):
            wide = part(widened, h, b)
            right = jnp.concatenate([part(tailing, h, b), part(pulled, h, b)], axis=1)
            product = mm(wide, right, TN)
            carry_map = part(end_growth, h, b)[0:1, :] * depth_eye - product[:, :depth]
            local = mm(part(grown_q, h, b), part(out_grad, h, b), TN) - product[:, depth:]
            map_buf[h, b, :, :depth] = carry_map
            map_buf[h, b, :, depth:] = local
            if across is None:
                across, offset = carry_map, local
            else:
                joined = mm(carry_map, jnp.concatenate([across, offset], axis=1))
                across, offset = joined[:, :depth], joined[:, depth:] + local
        ends.append((across, offset))
    for h in range(heads):
        across, offset = ends[h]
        change = jnp.concatenate([across - depth_eye, offset], axis=1).astype(BF16)
        ab_send_buf[h] = change

        @pl.when(heads * core + h == rank)
        def _():
            ab_buf[rank] = change

        act_if(heads * core + h != rank, ab_copy(h), "start")

    def by_parts(make):
        return [
            jnp.concatenate([make(h, b) for b in range(blocks)], axis=0) for h in range(heads)
        ]

    values = cut(gv_ref)
    states_load.wait()
    reads = [
        [
            mm(jnp.concatenate([part(unit_k, h, b), part(unit_q, h, b)], axis=0), states_ref[b, h])
            for b in range(blocks)
        ]
        for h in range(heads)
    ]
    key_reads = [jnp.concatenate([item[:BLOCK] for item in row], axis=0) for row in reads]
    query_reads = [jnp.concatenate([item[BLOCK:] for item in row], axis=0) for row in reads]
    remainder = [v - g * r for v, g, r in zip(values, growth, key_reads)]
    fresh = [mm(s, b * r) for s, b, r in zip(solved, beta, remainder)]
    faded_grad = [f * mm(o, r, NT) for f, o, r in zip(fading, out_grad, fresh)]
    out_back = by_parts(lambda h, b: mm_once(part(out_grad, h, b), states_ref[b, h], NT))
    unit_q_grad = [
        g * o + mm_once(f, k) for g, o, f, k in zip(growth, out_back, faded_grad, unit_k)
    ]
    faded_back = [mm_once(f, q, TN) for f, q in zip(faded_grad, unit_q)]

    for kinds in ((0, 2), (1, 3, 4)):
        take_spread(kinds)
        for kind in kinds:
            pass_on(kind, 0)
    share_all(KEYS + QUERIES, 0)
    for kind in KEYS + QUERIES:
        for h in range(heads):
            act_if(heads * core + h != rank, spread(h, kind), "wait_send")

    key_ids = lax.broadcasted_iota(jnp.int32, (total, total), 0)
    query_ids = lax.broadcasted_iota(jnp.int32, (total, total), 1)

    def stat_row(index, which):
        return jnp.concatenate(
            [stat_buf[index, block, which : which + 1, :] for block in range(heads)], axis=1
        )

    def terms(logits, grad_prob, lse, dots, mask):
        shifted = logits * scaling - lse
        if mask is None:
            chances = jnp.exp(shifted)
        else:
            chances = jnp.where(mask, jnp.exp(jnp.where(mask, shifted, 0.0)), 0.0)
        return (chances * (grad_prob - dots)).astype(BF16), chances.astype(BF16)

    own_lse = stat_row(own_qd, 0)
    own_dots = stat_row(own_qd, 1)
    keys = kv_buf[own_kv, 0]
    queries = qd_buf[own_qd, 0]
    grads = qd_buf[own_qd, 1]
    grad_logit, weights = terms(
        dot(keys, queries, NT), dot(kv_buf[own_kv, 1], grads, NT),
        own_lse, own_dots, query_ids >= key_ids,
    )
    dq_acc[...] = dot(grad_logit, keys, TN)
    dk_acc[...] = dot(grad_logit, queries)
    dv_acc[...] = dot(weights, grads)

    def stat_column(which):
        return jnp.concatenate(
            [
                to_column(stat_buf[own_qd, block, which : which + 1, :])
                for block in range(heads)
            ],
            axis=0,
        )

    lse_column = stat_column(0)
    dots_column = stat_column(1)

    def attend_keys(d, lanes=(0, 1)):
        lane_here = (2 * group + core >= d) & ((core == lanes[0]) | (core == lanes[-1]))

        @pl.when(lane_here)
        def _():
            keys = kv_buf[d + 1 - core, 0]
            grad_logit, _ = terms(
                dot(qd_buf[own_qd, 0], keys, NT),
                dot(qd_buf[own_qd, 1], kv_buf[d + 1 - core, 1], NT),
                lse_column, dots_column, key_ids < query_ids if d == reach else None,
            )
            dq_acc[...] += dot(grad_logit, keys)

    def attend_queries(d, lanes=(0, 1)):
        lane_here = (2 * group + core + d < 2 * groups) & (
            (core == lanes[0]) | (core == lanes[-1])
        )

        @pl.when(lane_here)
        def _():
            queries = qd_buf[d + core, 0]
            grads = qd_buf[d + core, 1]
            grad_logit, weights = terms(
                dot(kv_buf[own_kv, 0], queries, NT), dot(kv_buf[own_kv, 1], grads, NT),
                stat_row(d + core, 0), stat_row(d + core, 1),
                query_ids < key_ids if d == reach else None,
            )
            dk_acc[...] += dot(grad_logit, queries)
            dv_acc[...] += dot(weights, grads)

    def take_shared_keys(d, lanes=(0, 1)):
        for lane in lanes:
            m = (d + 1 - lane) // 2
            act_if(share_comes(0, m) & (core == lane), share_in(0, m), "wait_recv")

    def take_shared_queries(d, lanes=(0, 1)):
        for lane in lanes:
            m = (d + lane) // 2
            for kind in (2, 4):
                act_if(share_comes(kind, m) & (core == lane), share_in(kind, m), "wait_recv")

    def attend_shared(d):
        take_shared_keys(d)
        attend_keys(d)
        take_shared_queries(d)
        attend_queries(d)

    relays = {kind: hop_goes(kind, 2) for kind in KEYS + QUERIES} if steps > 1 else {}
    if steps > 1:
        arrive((0, 2), 1, lambda kind: relays[kind])

    @pl.when(composer)
    def _():
        joined = None
        ab_in().wait_recv()
        for r in reversed(range(size)):
            change = ab_buf[r, :, :depth]
            local = ab_buf[r, :, depth:].astype(F32)
            if joined is None:
                joined = jnp.concatenate([change.astype(F32) + depth_eye, local], axis=1)
            else:
                high, low = split(joined)
                joined = joined + (dot(change, high) + dot(change, low))
                joined = jnp.concatenate([joined[:, :depth], joined[:, depth:] + local], axis=1)
            map_hi[r], map_lo[r] = split(joined[:, :depth])
            map_add[r] = joined[:, depth:]

        @pl.when(group > 0)
        def _():
            whole_out[1] = joined[:, depth:].astype(BF16)
            whole_copy(1).start()

        @pl.when((group > 0) & (group < groups - 1))
        def _():
            whole_out[0] = (joined[:, :depth] - depth_eye).astype(BF16)
            whole_copy(0).start()

    if groups > 1:
        w_in().wait_recv()
    for j in range(1, size):
        w_spread(j).start()

    def carry_step(condition):
        @pl.when(composer & condition)
        def _():
            state_buf = adj_out.at[size - 1]

            @pl.when(group == groups - 1)
            def _():
                state_buf[...] = jnp.zeros_like(carry_in)

            @pl.when(group < groups - 1)
            def _():
                whole_copy(1).wait_recv()

            @pl.when(group == groups - 2)
            def _():
                state_buf[...] = whole_in[1]

            @pl.when(group < groups - 2)
            def _():
                whole_copy(0).wait_recv()
                carry_copy().wait_recv()
                carried = carry_in[...]
                state_buf[...] = (
                    carried.astype(F32)
                    + (dot(whole_in[0], carried) + whole_in[1].astype(F32))
                ).astype(BF16)

            state = state_buf[...]

            def start_of(r):
                return (dot(map_hi[r], state) + dot(map_lo[r], state) + map_add[r]).astype(BF16)

            @pl.when(group > 1)
            def _():
                carry_out[...] = start_of(0)
                carry_copy().start()

            adj_out[0] = start_of(1)
            act_if(rank != 0, adj_copy(0), "start")
            for r in range(1, size - 1):
                adj_out[r] = start_of(r + 1)
            for r in range(1, size):
                act_if(rank != r, adj_copy(r), "start")
            adj_in[place] = adj_out[rank]

    last = groups - 1 - group
    carry_step(last == 0)
    if steps > 1:
        arrive((0, 2), 1, lambda kind: jnp.logical_not(relays[kind]))
    else:
        arrive((0, 2), 1, lambda kind: True)
    arrive((1, 3, 4), 1, lambda kind: True)
    share_all(KEYS + QUERIES, 1)
    attend_keys(2)
    attend_queries(2)
    carry_step(last == 1)
    attend_shared(1)
    carry_step(last == 2)

    def blocks_of(matrix):
        return matrix.astype(BF16).reshape(heads, rows, depth)

    def send_back(item):
        for block in range(heads):
            act_if(back_rank(block) == rank, back_here(block, item), "start")
            act_if(back_rank(block) != rank, back_copy(block, item), "start")

    def send_queries():
        grad_out[0] = blocks_of(dq_acc[...] * scaling)
        send_back(0)

    pl.when(group == 0)(send_queries)
    for m in range(2, steps + 1):
        take_shared_queries(2 * m - 1, (0,))
        attend_queries(2 * m - 1, (0,))
        take_shared_keys(2 * m - 1, (1,))
        attend_keys(2 * m - 1, (1,))
        arrive((0, 2, 1, 3, 4), m, lambda kind: True)
        share_all(KEYS + QUERIES, m)
        attend_keys(2 * m)
        take_shared_keys(2 * m - 1, (0,))
        attend_keys(2 * m - 1, (0,))

    pl.when(group > 0)(send_queries)
    for m in range(2, steps + 1):
        attend_queries(2 * m)
        take_shared_queries(2 * m - 1, (1,))
        attend_queries(2 * m - 1, (1,))
    grad_out[1] = blocks_of(dk_acc[...] * scaling)
    grad_out[2] = blocks_of(dv_acc[...])
    send_back(1)
    carry_step(last >= 3)

    for item in range(2):
        back_in(item).wait_recv()
    for h in range(heads):
        dq_out[:, h * depth : (h + 1) * depth] = grad_in[h, 0]
    both_grads = jnp.concatenate(
        [grad_in[h, item] for item in (1, 2) for h in range(heads)], axis=1
    )
    w_spread_in().wait_recv()
    out_rows = dx_out.shape[0]
    pieces_each = out_rows // (size * w_rows)

    def dx_rows(owner):
        piece = w_all[pl.ds(owner * pieces_each, pieces_each)].reshape(out_rows, 2 * columns)
        return dot(piece, both_grads, NT)

    def dx_copy(j):
        return move(
            dx_send.at[j - 1], dx_recv.at[j - 1], sems.at[size + 2 * heads + j - 1], x_recv.at[j - 1],
            me, lax.rem(my_head + j, head_n),
        )

    for j in range(1, head_n):
        dx_send[j - 1] = dx_rows(lax.rem(my_head + j, head_n))
        dx_copy(j).start()
    result = dx_rows(my_head)
    for h in range(heads):
        act_if(heads * core + h != rank, adj_arrival(h), "wait_recv")
    later = {}
    for h in range(heads):
        adjoint = adj_in[h].astype(F32)
        for b in reversed(range(blocks)):
            later[h, b] = adjoint
            if b > 0:
                adjoint = mm(map_buf[h, b, :, :depth], adjoint) + map_buf[h, b, :, depth:]
    moved = by_parts(lambda h, b: mm(part(tailing, h, b), later[h, b]))
    fresh_grad = per_head(lambda a, b: a + b, pulled, moved)
    solved_grad = [mm(s, f, TN) for s, f in zip(solved, fresh_grad)]
    lower_grad = [-mm(s, f, NT) for s, f in zip(solved_grad, fresh)]
    key_products_grad = [b * f * g for b, f, g in zip(beta, strict_fading, lower_grad)]
    value_grad = per_head(lambda a, b: a * b, beta, solved_grad)
    value_back = by_parts(lambda h, b: mm_once(part(value_grad, h, b), states_ref[b, h], NT))
    fresh_moved = by_parts(lambda h, b: mm(part(fresh, h, b), later[h, b], NT))
    fresh_back = per_head(lambda a, b: a * b, tail, fresh_moved)
    for h in range(heads):
        cols = slice(h * depth, (h + 1) * depth)
        unit_k_grad = (
            fresh_back[h]
            - growth[h] * value_back[h]
            + faded_back[h]
            + mm_once(key_products_grad[h], unit_k[h])
            + mm_once(key_products_grad[h], unit_k[h], TN)
        )
        q_share = inv_q[h] * inv_q[h] * row_sum(unit_q_grad[h] * raw_q[h])
        k_share = inv_k[h] * inv_k[h] * row_sum(unit_k_grad * raw_k[h])
        gdq_out[:, cols] = (scaling * inv_q[h] * (unit_q_grad[h] - raw_q[h] * q_share)).astype(BF16)
        gdk_out[:, cols] = (inv_k[h] * (unit_k_grad - raw_k[h] * k_share)).astype(BF16)
        gdv_out[:, cols] = value_grad[h].astype(BF16)
        beta_grad = row_sum(solved_grad[h] * remainder[h]) + row_sum(lower_grad[h] * faded_keys[h])
        exponent = faded_grad[h] * query_products[h] + key_products_grad[h] * key_products[h]
        tail_grad = row_sum(unit_k[h] * fresh_back[h])
        growth_grad = row_sum(out_grad[h] * query_reads[h]) - row_sum(value_grad[h] * key_reads[h])
        summed_grad = (
            row_sum(exponent) - to_column(column_sum(exponent)) - tail_grad + growth[h] * growth_grad
        )
        end_grad = end_growth[h] * jnp.concatenate(
            [
                jnp.broadcast_to(column_sum(row_sum(later[h, b] * states_ref[b, h])), (BLOCK, 1))
                for b in range(blocks)
            ],
            axis=0,
        )
        gdecay_out[h : h + 1, :] = (
            column_sum(jnp.where(causal, summed_grad, 0.0))
            + column_sum(jnp.where(same, tail_grad, 0.0))
            + to_row(end_grad)
        )
        gbeta_out[h : h + 1, :] = to_row(beta_grad)

    for j in range(1, head_n):
        dx_copy(j).wait_recv()
        result = result + dx_recv[j - 1]
    dx_out[...] = result.astype(BF16)

    for kind in KEYS + QUERIES:
        act_if(hop_goes(kind, steps), hop(kind, steps), "wait_send")
        if kind % 2 == 0:
            act_if(share_goes(kind, steps), share(kind, steps), "wait_send")
    for m in range(1, groups):
        w_copy(m).wait_send()
    for j in range(1, size):
        w_spread(j).wait_send()
    for h in range(heads):
        act_if(heads * core + h != rank, ab_copy(h), "wait_send")
    act_if(composer & (group > 0), whole_copy(1), "wait_send")
    act_if(composer & (group > 0) & (group < groups - 1), whole_copy(0), "wait_send")
    act_if(composer & (group > 1), carry_copy(), "wait_send")
    for r in range(size):
        act_if(composer & (rank != r), adj_copy(r), "wait_send")
    for block in range(heads):
        for item in range(2):
            act_if(back_rank(block) != rank, back_copy(block, item), "wait_send")
    for j in range(1, head_n):
        dx_copy(j).wait_send()


def hand_over(*refs):
    half = (len(refs) - 1) // 2
    sems = refs[-1]
    copies = [
        pltpu.make_async_copy(refs[i], refs[half + i], sems.at[i]) for i in range(half)
    ]
    for copy in copies:
        copy.start()
    for copy in copies:
        copy.wait()


def per_device(n, head_n, *args):
    attn_q, attn_lse, w_kv, states = args[0], args[5], args[6], args[13]
    rows, columns = attn_q.shape
    heads = attn_lse.shape[0]
    depth = columns // heads
    size = 2 * heads
    steps = WINDOW // (size * rows)
    blocks = states.shape[0]
    groups = n // size
    assert head_n % 2 == 0 and n % size == 0 and WINDOW == steps * size * rows
    w_rows = w_kv.shape[0]
    out_rows = n * w_rows // head_n
    dma = pltpu.SemaphoreType.DMA
    vmem = pl.BlockSpec(memory_space=pltpu.VMEM)
    others = max(head_n - 1, 1)
    slots = 2 * (steps + 1)
    span = heads * rows
    results = pl.pallas_call(
        functools.partial(kernel, n, head_n),
        out_shape=(
            pltpu.VMEM((rows, columns), BF16),
            pltpu.VMEM((out_rows, rows), BF16),
            pltpu.VMEM((rows, columns), BF16),
            pltpu.VMEM((rows, columns), BF16),
            pltpu.VMEM((rows, columns), BF16),
            pltpu.VMEM((heads, rows), F32),
            pltpu.VMEM((heads, rows), F32),
        ),
        in_specs=[pl.BlockSpec(memory_space=pl.ANY)] * len(args),
        out_specs=(vmem,) * 7,
        scratch_shapes=[pltpu.VMEM(item.shape, item.dtype) for item in args[3:]] + [
            pltpu.VMEM((slots, 2, span, depth), BF16),
            pltpu.VMEM((slots, 2, span, depth), BF16),
            pltpu.VMEM((slots, heads, 8, rows), F32),
            pltpu.VMEM((heads, 8, rows), F32),
            pltpu.VMEM((groups, size, w_rows, 2 * columns), BF16),
            pltpu.VMEM((heads, depth, 2 * depth), BF16),
            pltpu.VMEM((size, depth, 2 * depth), BF16),
            pltpu.VMEM((size, depth, depth), BF16),
            pltpu.VMEM((size, depth, depth), BF16),
            pltpu.VMEM((size, depth, depth), F32),
            pltpu.VMEM((2, depth, depth), BF16),
            pltpu.VMEM((2, depth, depth), BF16),
            pltpu.VMEM((depth, depth), BF16),
            pltpu.VMEM((depth, depth), BF16),
            pltpu.VMEM((size, depth, depth), BF16),
            pltpu.VMEM((heads, depth, depth), BF16),
            pltpu.VMEM((3, heads, rows, depth), BF16),
            pltpu.VMEM((heads, 3, rows, depth), BF16),
            pltpu.VMEM((others, out_rows, rows), F32),
            pltpu.VMEM((others, out_rows, rows), F32),
            pltpu.VMEM((span, depth), F32),
            pltpu.VMEM((span, depth), F32),
            pltpu.VMEM((span, depth), F32),
            pltpu.VMEM((heads, blocks, depth, 2 * depth), F32),
            dma((max(5 * heads, size + 2 * heads + others),)), dma((5,)),
            dma((5,)), dma((steps, 5)),
            dma((3,)), dma((steps + 1, 3)),
            dma((max(groups - 1, 1),)), dma, dma((size - 1,)), dma,
            dma((heads,)), dma,
            dma((2,)), dma((2,)), dma, dma,
            dma((heads,)),
            dma((2,)),
            dma((others,)),
        ],
        compiler_params=pltpu.CompilerParams(
            collective_id=0, has_side_effects=True, vmem_limit_bytes=60000000
        ),
        name="layer_backward",
    )(*args)
    results = [pltpu.with_memory_space_constraint(item, pltpu.VMEM) for item in results]
    return pl.pallas_call(
        hand_over,
        out_shape=[jax.ShapeDtypeStruct(item.shape, item.dtype) for item in results],
        in_specs=[vmem] * len(results),
        out_specs=[pl.BlockSpec(memory_space=pl.ANY)] * len(results),
        scratch_shapes=[dma((len(results),))],
        name="hand_over",
    )(*results)


def solution(mesh):
    rows = P("seq", "head")
    gates = P("head", "seq")
    return jax.shard_map(
        functools.partial(per_device, mesh.shape["seq"], mesh.shape["head"]),
        mesh=mesh,
        in_specs=(
            rows, rows, rows, rows, rows, gates, P("seq", None, "head"),
            rows, rows, rows, rows, gates, gates, P("seq", "head", None, None),
        ),
        out_specs=(rows, gates, rows, rows, rows, gates, gates),
        check_vma=False,
    )
```
